256 devices in a mesh: seq: 8 (over y, x_lo), rep: 16 (over z, core), exp: 2 (over x_hi).
Axes of the slice: x: 4 (x_hi: 2, x_lo: 2; x = x_hi * 2 + x_lo), y: 4, z: 8, core: 2. Of those that a mesh axis runs over, the one named last changes fastest.
Arguments:
- residual_in: bfloat16 [32, 1024, 2048], P(('rep', 'exp'), 'seq'), may hold values from -40 to 40
- queries: bfloat16 [32, 1024, 2048], P(('rep', 'exp'), 'seq'), may hold values from -6 to 6
- key_feats: bfloat16 [32, 1024, 2048], P(('rep', 'exp'), 'seq'), may hold values from -0.5390625 to 0.5390625
- value_feats: bfloat16 [32, 1024, 2048], P(('rep', 'exp'), 'seq'), may hold values from -6 to 6
- log_decay: float32 [32, 16, 1024], P(('rep', 'exp'), None, 'seq'), may hold values from -1.3 to 0
- out_cotangent: bfloat16 [32, 8, 32, 2048], P(('rep', 'exp'), 'seq'), may hold values from -6 to 6
- mask_pos: int32 [32, 8, 32], P(('rep', 'exp'), 'seq'), may hold values from 0 to 127, as said below
- route_rows: int32 [32, 8, 2, 128], P(('rep', 'exp'), 'seq'), may hold values from 0 to 127, as said below
- route_weight: float32 [32, 8, 2, 128], P(('rep', 'exp'), 'seq'), may hold values from 0.2 to 1
- up_proj: bfloat16 [2, 2048, 768], P('exp', ('seq', 'rep')), may hold values from -0.125 to 0.125
- down_proj: bfloat16 [2, 2048, 768], P('exp', ('seq', 'rep')), may hold values from -0.21875 to 0.21875
Outputs:
- query_grad: bfloat16 [32, 1024, 2048], P(('rep', 'exp'), 'seq')
- key_grad: bfloat16 [32, 1024, 2048], P(('rep', 'exp'), 'seq')
- value_grad: bfloat16 [32, 1024, 2048], P(('rep', 'exp'), 'seq')
- up_grad: float32 [2, 2048, 768], P('exp', ('seq', 'rep'))
- down_grad: float32 [2, 2048, 768], P('exp', ('seq', 'rep'))
The draws below stay inside these ranges and needn't reach their ends.
Inputs may be any that keep to these rules, and one draw needn't show every extreme that they name: `mask_pos`: the 32 entries of one device are distinct local positions of its 128. `route_rows`: for each device and expert the 128 entries are distinct local positions of that device, so each list is a permutation of the device's 128 positions (one tile of 128 rows).
All inputs are finite; a program needn't handle non-finite values.
Results may differ from the reference program's by a relative error of at most 0.018.
Values may be sent and summed in bfloat16 or wider, within the bound.
No kernel may reach another device: no remote copies, remote signals or barrier semaphores. Data moves between devices by JAX's collectives and lax.ppermute only.
A program may use at most 192 MiB of HBM per device.

```python
import math
import jax
import jax.numpy as jnp
from jax import lax

HALF_HEAD_COUNT = 16
HD = 128
FF = 768
TOK_DEV = 128
D = 2048
EXPERTS = 2
SEQUENCE_COUNT = 32
LENGTH = 1024
ROUTED = 128
MASKED = 32
N_SEQ = 8
N_REP = 16


def draw_residual_in(key, part):
    every_random_key = jax.random.split(key, 3)
    entries = jax.random.normal(every_random_key[0], (SEQUENCE_COUNT, LENGTH, D), jnp.float32)
    column = jnp.exp(jax.random.uniform(every_random_key[1], (1, 1, D), jnp.float32, 0.0, math.log(10.0)))
    row_part = jnp.exp(jax.random.uniform(every_random_key[2], (SEQUENCE_COUNT, LENGTH, 1), jnp.float32, -1.2, 1.2))
    return jnp.clip(entries * column * row_part / 3.0, -40.0, 40.0).astype(jnp.bfloat16)


def draw_log_decay(key, part):
    every_random_key = jax.random.split(key, 5)
    fast_share = 0.5
    fast_head = jax.random.uniform(every_random_key[0], (SEQUENCE_COUNT, HALF_HEAD_COUNT, 1), jnp.float32) < fast_share
    fast_rate = jnp.exp(jax.random.uniform(every_random_key[1], (SEQUENCE_COUNT, HALF_HEAD_COUNT, 1), jnp.float32, math.log(1.0 / 50.0), math.log(1.0 / 25.0)))
    rates = jnp.where(fast_head, fast_rate, 0.5 / LENGTH)
    rough = jnp.exp(jax.random.uniform(every_random_key[2], (SEQUENCE_COUNT, HALF_HEAD_COUNT, LENGTH), jnp.float32, math.log(0.5), math.log(2.0)))
    places = jax.random.randint(every_random_key[3], (SEQUENCE_COUNT, HALF_HEAD_COUNT, 2), 0, LENGTH)
    token_volley = jnp.log(jax.random.uniform(every_random_key[4], (SEQUENCE_COUNT, HALF_HEAD_COUNT, 2), jnp.float32, 0.55, 0.8))
    token_locations = jnp.arange(LENGTH, dtype=jnp.int32)
    expert_tallies = (token_locations[None, None, None, :] == places[:, :, :, None]).astype(jnp.float32)
    masked_loss_values = jnp.sum(expert_tallies * token_volley[:, :, :, None], axis=2)
    return (-rates * rough + masked_loss_values).astype(jnp.float32)


def draw_mask_pos(key, part):
    every_random_key = jax.random.split(jax.random.fold_in(key, 11), SEQUENCE_COUNT * N_SEQ)
    chosen = jax.vmap(lambda single: jax.random.permutation(single, TOK_DEV)[:MASKED])(every_random_key)
    return chosen.reshape(SEQUENCE_COUNT, N_SEQ, MASKED).astype(jnp.int32)


def draw_route_rows(key, part):
    every_random_key = jax.random.split(jax.random.fold_in(key, 23), SEQUENCE_COUNT * N_SEQ * EXPERTS)
    chosen = jax.vmap(lambda single: jax.random.permutation(single, TOK_DEV)[:ROUTED])(every_random_key)
    return chosen.reshape(SEQUENCE_COUNT, N_SEQ, EXPERTS, ROUTED).astype(jnp.int32)


def with_spikes(array, key, source, target, blocks, factor):
    owner, partner = [(jnp.arange(array.shape[axis_at]) // (array.shape[axis_at] // blocks)).reshape([-1 if axis == axis_at else 1 for axis in range(array.ndim)]) for axis_at in (source, target)]
    chosen = jax.random.permutation(key, blocks)[partner]
    strong = (owner == chosen) | (owner == (partner + blocks // 2) % blocks)
    return jnp.where(strong, factor * array, array)


def block_levels(rng, extent, cuts, least, high):
    def one(position, shards_of):
        draws = jax.random.uniform(jax.random.fold_in(jax.random.fold_in(rng, 6), position), (shards_of,), jnp.float32, least / len(cuts), high / len(cuts))
        return jnp.repeat(jnp.exp(draws), extent[position] // shards_of).reshape((-1,) + (1,) * (len(extent) - position - 1))

    factor_of = one(*cuts[0])
    for cut in cuts[1:]:
        factor_of = factor_of * one(*cut)
    return factor_of


def gaussian(own_key, extent, deviation, bound, cuts=(), kind=jnp.bfloat16):
    loudness = block_levels(own_key, extent, cuts, -0.22, 0.18) if cuts else 1.0
    drawn = jax.random.normal(own_key, extent, jnp.float32) * deviation * loudness
    return jnp.minimum(jnp.maximum(drawn, -bound), bound).astype(kind)


def heavy_noise(rng, dims, deviation, limit, cuts, heavy, kind=jnp.bfloat16):
    drawn = deviation * jax.random.normal(rng, dims, jnp.float32)
    if cuts:
        drawn = drawn * block_levels(rng, dims, cuts, -0.22, 0.18)
    return jnp.clip(with_spikes(drawn, jax.random.fold_in(rng, 3), *heavy), -limit, limit).astype(kind)


def setup_inputs(seed: int = 0) -> dict:
    splits = jax.random.split(jax.random.key(seed), 12)
    return {
        "residual_in": draw_residual_in(jax.random.fold_in(splits[11], 71), 0),
        "queries": gaussian(splits[1], (SEQUENCE_COUNT, LENGTH, D), 1.0, 6.0, ((0, 32), (1, 8))),
        "key_feats": gaussian(splits[2], (SEQUENCE_COUNT, LENGTH, D), 0.09, 0.5390625, ((0, 32), (1, 8))),
        "value_feats": gaussian(splits[3], (SEQUENCE_COUNT, LENGTH, D), 1.0, 6.0, ((0, 32), (1, 8))),
        "log_decay": draw_log_decay(jax.random.fold_in(splits[11], 71), 0),
        "out_cotangent": heavy_noise(splits[5], (SEQUENCE_COUNT, N_SEQ, MASKED, D), 1.0, 6.0, ((0, 32), (1, 8)), (1, 3, 8, 2.0)),
        "mask_pos": draw_mask_pos(jax.random.fold_in(splits[11], 71), 0),
        "route_rows": draw_route_rows(jax.random.fold_in(splits[11], 71), 0),
        "route_weight": jnp.clip(0.2 + 0.8 * jax.random.uniform(splits[8], (SEQUENCE_COUNT, N_SEQ, EXPERTS, ROUTED), jnp.float32) ** block_levels(splits[8], (SEQUENCE_COUNT, N_SEQ, EXPERTS, ROUTED), ((0, 32), (1, 8)), -0.2, 0.2), 0.2, 1.0),
        "up_proj": gaussian(splits[9], (EXPERTS, D, FF), D ** -0.5, 0.125, ((0, 2), (1, 128))),
        "down_proj": gaussian(splits[10], (EXPERTS, D, FF), FF ** -0.5, 0.21875, ((0, 2), (1, 128))),
    }


EPS = 1e-05

def to_blocks(matrix):
    return matrix.reshape(N_SEQ, TOK_DEV, HALF_HEAD_COUNT, HD).transpose(0, 2, 1, 3)

def from_blocks(tensor):
    return tensor.transpose(0, 2, 1, 3).reshape(N_SEQ * TOK_DEV, HALF_HEAD_COUNT * HD)

def block_terms(query_h, key_h, value_h, cum_log):
    cum_end = cum_log[:, -1]
    spread = jnp.exp(-jnp.abs(cum_log[:, :, None] - cum_log[:, None, :]))
    scores = jnp.einsum('hre,hse->hrs', query_h.astype(jnp.float32), key_h.astype(jnp.float32), precision=lax.Precision.HIGHEST)
    weights = (scores * spread).astype(jnp.bfloat16)
    inner_part = jnp.einsum('hrs,hse->hre', weights.astype(jnp.float32), value_h.astype(jnp.float32), precision=lax.Precision.HIGHEST)
    keys_fwd = (key_h.astype(jnp.float32) * jnp.exp(cum_end[:, None] - cum_log)[:, :, None]).astype(jnp.bfloat16)
    keys_bwd = (key_h.astype(jnp.float32) * jnp.exp(cum_log)[:, :, None]).astype(jnp.bfloat16)
    state_fwd = jnp.einsum('hse,hsf->hef', keys_fwd.astype(jnp.float32), value_h.astype(jnp.float32), precision=lax.Precision.HIGHEST)
    state_bwd = jnp.einsum('hse,hsf->hef', keys_bwd.astype(jnp.float32), value_h.astype(jnp.float32), precision=lax.Precision.HIGHEST)
    return (inner_part, jnp.exp(cum_end), state_fwd, state_bwd)

def finish(query_h, inner_part, cum_log, carried_fwd, carried_bwd):
    query_f = query_h.astype(jnp.float32)
    cum_end = cum_log[:, -1:]
    fwd_round = lax.optimization_barrier(carried_fwd.astype(jnp.bfloat16)).astype(jnp.float32)
    backward_sweep = lax.optimization_barrier(carried_bwd.astype(jnp.bfloat16)).astype(jnp.float32)
    early_part = jnp.einsum('hre,hef->hrf', query_f, fwd_round, precision=lax.Precision.HIGHEST)
    late_part = jnp.einsum('hre,hef->hrf', query_f, backward_sweep, precision=lax.Precision.HIGHEST)
    return inner_part + jnp.exp(cum_log)[:, :, None] * early_part + jnp.exp(cum_end - cum_log)[:, :, None] * late_part

def bi_attn(query_b, key_b, value_b, cum_log):
    inner_part, decays, state_fwd, state_bwd = jax.vmap(block_terms)(query_b, key_b, value_b, cum_log)
    running = jnp.zeros_like(state_fwd[0])
    before = []
    for number in range(N_SEQ):
        before.append(running)
        running = decays[number][:, None, None] * running + state_fwd[number]
    after = [running] * N_SEQ
    running = jnp.zeros_like(state_bwd[0])
    for number in reversed(range(N_SEQ)):
        after[number] = running
        running = decays[number][:, None, None] * running + state_bwd[number]
    return jax.vmap(finish)(query_b, inner_part, cum_log, jnp.stack(before), jnp.stack(after))

def reference(residual_in, queries, key_feats, value_feats, log_decay, out_cotangent, mask_pos, route_rows, route_weight, up_proj, down_proj):

    def one_sequence(totals, inputs):
        residual_seq, query_seq, key_seq, value_seq, decay_seq, cot_seq, mask_seq, rows_seq, gate_seq = inputs
        cum_log = jnp.cumsum(decay_seq.reshape(HALF_HEAD_COUNT, N_SEQ, TOK_DEV), axis=2).transpose(1, 0, 2)
        query_b = to_blocks(query_seq)
        key_b = to_blocks(key_seq)
        value_b = to_blocks(value_seq)
        attn = bi_attn(query_b, key_b, value_b, cum_log)
        head_scale = lax.rsqrt(lax.optimization_barrier(jnp.mean(attn * attn, axis=-1, keepdims=True)) + EPS)
        normed = attn * head_scale
        residual = (residual_seq.astype(jnp.float32) + from_blocks(normed)).astype(jnp.bfloat16)
        residual_f = residual.astype(jnp.float32)
        row_scale = lax.rsqrt(lax.optimization_barrier(jnp.mean(residual_f * residual_f, axis=-1, keepdims=True)) + EPS)
        normalized = residual_f * row_scale
        routed = normalized.astype(jnp.bfloat16)
        offsets = jnp.arange(N_SEQ, dtype=jnp.int32)[:, None] * TOK_DEV
        marked = (offsets + mask_seq.astype(jnp.int32)).reshape(-1)
        out_grad = jnp.zeros((N_SEQ * TOK_DEV, HALF_HEAD_COUNT * HD), jnp.float32).at[marked].add(cot_seq.reshape(-1, HALF_HEAD_COUNT * HD).astype(jnp.float32))
        z_grad = jnp.zeros_like(out_grad)
        up_total, down_total = totals
        for expert in range(EXPERTS):
            picked = (offsets + rows_seq[:, expert, :].astype(jnp.int32)).reshape(-1)
            rows_in = routed[picked]
            send_grad = (gate_seq[:, expert, :].reshape(-1, 1) * out_grad[picked]).astype(jnp.bfloat16)
            pre = jnp.dot(rows_in, up_proj[expert], preferred_element_type=jnp.float32)
            sigmoid_pre = jax.nn.sigmoid(pre)
            act = (pre * sigmoid_pre).astype(jnp.bfloat16)
            act_grad = jnp.dot(send_grad, down_proj[expert], preferred_element_type=jnp.float32)
            pre_grad = (act_grad * sigmoid_pre * (1.0 + pre * (1.0 - sigmoid_pre))).astype(jnp.bfloat16)
            z_part = jnp.dot(pre_grad, up_proj[expert].T, preferred_element_type=jnp.float32).astype(jnp.bfloat16)
            z_grad = z_grad.at[picked].add(z_part.astype(jnp.float32))
            up_total = up_total.at[expert].add(jnp.dot(rows_in.T, pre_grad, preferred_element_type=jnp.float32))
            down_total = down_total.at[expert].add(jnp.dot(send_grad.T, act, preferred_element_type=jnp.float32))
        residual_grad = out_grad + row_scale * (z_grad - normalized * lax.optimization_barrier(jnp.mean(z_grad * normalized, axis=-1, keepdims=True)))
        grad_blocks = to_blocks(residual_grad)
        attn_grad = (head_scale * (grad_blocks - normed * lax.optimization_barrier(jnp.mean(grad_blocks * normed, axis=-1, keepdims=True)))).astype(jnp.bfloat16)
        query_grad = from_blocks(bi_attn(attn_grad, value_b, key_b, cum_log)).astype(jnp.bfloat16)
        key_grad = from_blocks(bi_attn(value_b, attn_grad, query_b, cum_log)).astype(jnp.bfloat16)
        value_grad = from_blocks(bi_attn(key_b, query_b, attn_grad, cum_log)).astype(jnp.bfloat16)
        return ((up_total, down_total), (query_grad, key_grad, value_grad))
    start_totals = (jnp.zeros((EXPERTS, HALF_HEAD_COUNT * HD, FF), jnp.float32), jnp.zeros((EXPERTS, HALF_HEAD_COUNT * HD, FF), jnp.float32))
    totals, grads = lax.scan(one_sequence, start_totals, (residual_in, queries, key_feats, value_feats, log_decay, out_cotangent, mask_pos, route_rows, route_weight))
    groups = N_SEQ * N_REP
    return (grads[0], grads[1], grads[2], totals[0] / groups, totals[1] / groups)
```

```python
import jax
import jax.numpy as jnp
from jax import lax
from jax.experimental import pallas as pl
from jax.experimental.pallas import tpu as pltpu
from jax.sharding import Mesh, PartitionSpec as P

HEADS = 16
HD = 128
EPS = 1e-05
SEQ = ("y", "xl")
GRP = ("xl", "c", "e")
F32 = jnp.float32
BF16 = jnp.bfloat16
HIGH = lax.Precision.HIGHEST


def call(body, outs, *args, flops=10**8, scalar=False):
    shapes = [jax.ShapeDtypeStruct(s, d) for s, d in outs]
    moved = sum(a.size * a.dtype.itemsize for a in (*args, *shapes))
    spaces = [pltpu.SMEM if scalar and k == 0 else pltpu.VMEM for k in range(len(args))]
    result = pl.pallas_call(
        body,
        out_shape=shapes,
        in_specs=[pl.BlockSpec(memory_space=m) for m in spaces],
        compiler_params=pltpu.CompilerParams(vmem_limit_bytes=44 << 20),
        cost_estimate=pl.CostEstimate(flops=flops, bytes_accessed=moved, transcendentals=0),
    )(*args)
    return result


def iota(shape, dim):
    return lax.broadcasted_iota(jnp.int32, shape, dim)


def tn(a, b, **kw):
    return lax.dot_general(a, b, (((0,), (0,)), ((), ())), preferred_element_type=F32, **kw)


def nt(a, b, **kw):
    return lax.dot_general(a, b, (((1,), (1,)), ((), ())), preferred_element_type=F32, **kw)


def nn(a, b, **kw):
    return lax.dot_general(a, b, (((1,), (0,)), ((), ())), preferred_element_type=F32, **kw)


def head(h):
    return slice(h * HD, (h + 1) * HD)


def exchange(x, axes):
    return lax.all_to_all(x, axes, split_axis=0, concat_axis=0, tiled=True)


def broadcast(x, axes, n):
    return exchange(jnp.broadcast_to(x[None], (n, *x.shape)), axes)


def weights_body(up, down, out):
    low = iota((up.shape[0], HD), 1) < 64
    for c in range(12):
        u = up[:, head(c // 2)].astype(F32)
        d = down[:, head(c // 2)].astype(F32)
        if c % 2:
            u = pltpu.roll(u, 64, 1)
        else:
            d = pltpu.roll(d, 64, 1)
        out[c // 3, :, head(c % 3)] = jnp.where(low, u, d).astype(BF16)


def weight_grads_body(scale, g, up, down):
    low = iota((up.shape[0], HD), 1) < 64
    for b in range(6):
        first, second = 2 * b, 2 * b + 1
        x = g[first // 3, :, head(first % 3)] * scale
        y = g[second // 3, :, head(second % 3)] * scale
        up[:, head(b)] = jnp.where(low, x, pltpu.roll(y, 64, 1))
        down[:, head(b)] = jnp.where(low, pltpu.roll(x, 64, 1), y)


def states_body(ld, key, value, places, out, cum_out, cum_t_out):
    rows, cols = iota((HD, HD), 0), iota((HD, HD), 1)
    ldv = ld[...]
    cum = nn(ldv, (rows <= cols).astype(F32), precision=HIGH)
    cum_t = nt((cols <= rows).astype(F32), ldv, precision=HIGH)
    cum_out[...] = cum
    cum_t_out[...] = cum_t
    falling = jnp.exp(cum_t[HD - 1 : HD, :] - cum_t)
    rising = jnp.exp(cum_t)
    for h in range(HEADS):
        k = key[:, head(h)].astype(F32)
        kf = (k * falling[:, h : h + 1]).astype(BF16)
        kb = (k * rising[:, h : h + 1]).astype(BF16)
        v = value[:, head(h)]
        g, at = h // 2, (h % 2) * HD
        out[g, at : at + HD, :] = tn(kf, v).astype(BF16)
        out[g, 256 + at : 256 + at + HD, :] = tn(kb, v).astype(BF16)
    chosen = nn(cum, (rows == places[...]).astype(F32), precision=HIGH)
    hi = chosen.astype(BF16).astype(F32)
    mid = (chosen - hi).astype(BF16).astype(F32)
    low = (chosen - hi - mid).astype(BF16).astype(F32)
    lane = iota((HEADS, HD), 1)
    first = (lane < 32) | (lane == 96)
    second = ((lane >= 32) & (lane < 64)) | (lane == 97)
    third = ((lane >= 64) & (lane < 96)) | (lane == 98)
    packed = jnp.where(first, hi, jnp.where(second, mid, jnp.where(third, low, 0.0))).astype(BF16)
    for g in range(8):
        out[g, 512:528, :] = packed


def masked_body(
    query, key, value, residual, cot, mask, routes, gates, cum, cum_t, qm_out, rm_out, inner_out, sg_out, cm_out
):
    pick_t = (iota((HD, 32), 0) == mask[...]).astype(BF16)
    qm = tn(pick_t, query[...]).astype(BF16)
    qm_out[...] = qm
    rm_out[...] = tn(pick_t, residual[...])
    lane = iota((HD, HD), 1)
    sub = iota((HD, HD), 0)
    pick_f = pick_t.astype(F32)
    cm = tn(pick_f, cum_t[...], precision=HIGH)
    cm_out[...] = cm
    cumv = cum[...]
    for h in range(HEADS):
        s = nt(qm[:, head(h)], key[:, head(h)])
        p = (s * jnp.exp(-jnp.abs(cm[:, h : h + 1] - cumv[h : h + 1, :]))).astype(BF16)
        inner_out[:, head(h)] = nn(p, value[:, head(h)])
    table = jnp.zeros((HD, HD), F32)
    for e in range(2):
        hit = jnp.where(sub == routes[e : e + 1, :], gates[e : e + 1, :], 0.0)
        table = jnp.where(lane == e, jnp.sum(hit, axis=1, keepdims=True), table)
    gm = tn(pick_f, table, precision=HIGH)
    cotf = cot[...].astype(F32)
    for e in range(2):
        sg = (gm[:, e : e + 1] * cotf).astype(BF16)
        for k in range(4):
            sg_out[2 * k + e] = sg


def carry_body(mine, parts, out):
    row, lane = iota((HEADS, HD), 0), iota((HEADS, HD), 1)
    ends = (lane >= 96) & (lane < 99)
    n = parts.shape[0]
    for j in range(2):
        at = slice(j * HD, (j + 1) * HD)
        back = slice(256 + j * HD, 256 + (j + 1) * HD)
        wanted = ends & (row == 2 * mine[0] + j)
        decay = [
            jnp.exp(jnp.sum(jnp.where(wanted, parts[a, 512:528, :].astype(F32), 0.0), keepdims=True))
            for a in range(n)
        ]
        run = jnp.zeros((HD, HD), F32)
        for a in range(n):
            out[a, at, :] = run.astype(BF16)
            run = decay[a] * run + parts[a, at, :].astype(F32)
        run = jnp.zeros((HD, HD), F32)
        for a in reversed(range(n)):
            out[a, back, :] = run.astype(BF16)
            run = decay[a] * run + parts[a, back, :].astype(F32)


def states_of(carried, h):
    at = (h % 2) * HD
    return carried[h // 2, at : at + HD, :], carried[h // 2, 256 + at : 256 + at + HD, :]


def rows_body(qm, rm, inner, cm, cum_t, carried, routed_out, normed_out, normalized_out, stats_out):
    cmv = cm[...]
    rising = jnp.exp(cmv)
    falling = jnp.exp(cum_t[HD - 1 : HD, :] - cmv)
    lane = iota((32, HD), 1)
    stats = jnp.zeros((32, HD), F32)
    total = jnp.zeros((32, HD), F32)
    residuals = []
    for h in range(HEADS):
        fwd, bwd = states_of(carried, h)
        q = qm[:, head(h)]
        attn = inner[:, head(h)] + rising[:, h : h + 1] * nn(q, fwd) + falling[:, h : h + 1] * nn(q, bwd)
        scale = lax.rsqrt(jnp.mean(attn * attn, axis=-1, keepdims=True) + EPS)
        normed = attn * scale
        normed_out[:, head(h)] = normed
        stats = jnp.where(lane == h, scale, stats)
        r = (rm[:, head(h)] + normed).astype(BF16).astype(F32)
        total = total + r * r
        residuals.append(r)
    row_scale = lax.rsqrt(jnp.sum(total, axis=-1, keepdims=True) * (1.0 / (HEADS * HD)) + EPS)
    stats_out[...] = jnp.where(lane == HEADS, row_scale, stats)
    for h in range(HEADS):
        normalized = residuals[h] * row_scale
        normalized_out[:, head(h)] = normalized
        routed = normalized.astype(BF16)
        for k in range(8):
            routed_out[k, :, head(h)] = routed


def expert_body(rows, grads, weights, z_out, dw_out, w_ref):
    ny, nz, nx, unit = weights.shape[:4]
    for y in range(ny):
        for z in range(nz):
            for x in range(nx):
                w_ref[pl.ds(((y * nx + x) * nz + z) * unit, unit), :] = weights[y, z, x]
    r = rows[...].reshape(256, HEADS * HD)
    g = grads[...].reshape(256, HEADS * HD)
    w = w_ref[...]
    pre_all = nn(r, w)
    grad_all = nn(g, w)
    low = iota((256, HD), 1) < 64
    pgs, acts = [], []
    for b in range(3):
        pre = pre_all[:, head(b)]
        act_grad = pltpu.roll(grad_all[:, head(b)], 64, 1)
        sig = jax.nn.sigmoid(pre)
        act = pltpu.roll(pre * sig, 64, 1)
        pre_grad = act_grad * sig * (1.0 + pre * (1.0 - sig))
        pgs.append(jnp.where(low, pre_grad, 0.0).astype(BF16))
        acts.append(jnp.where(low, 0.0, act).astype(BF16))
    pg = jnp.concatenate(pgs, axis=1)
    ac = jnp.concatenate(acts, axis=1)
    z_out[...] = nt(pg, w).astype(BF16).reshape(z_out.shape)
    both = jnp.concatenate((pg, ac), axis=0)
    for y in range(4):
        cols = slice(y * 512, (y + 1) * 512)
        sides = jnp.concatenate((r[:, cols], g[:, cols]), axis=0)
        dw_out[y] = tn(sides, both).astype(BF16)


def sum_y_body(parts, out):
    ny = parts.shape[0]
    nz, nx, unit = out.shape[:3]
    for x in range(nx):
        for z in range(nz):
            at = slice((x * nz + z) * unit, (x * nz + z + 1) * unit)
            total = parts[0, at, :].astype(F32)
            for y in range(1, ny):
                total = total + parts[y, at, :].astype(F32)
            out[z, x] = total.astype(BF16)


def sum_z_body(parts, out):
    total = parts[0].astype(F32)
    for z in range(1, parts.shape[0]):
        total = total + parts[z].astype(F32)
    out[...] = total


def grads_body(z_parts, cot, normed, normalized, stats, out):
    z = z_parts[0].astype(F32)
    for k in range(1, 8):
        z = z + z_parts[k].astype(F32)
    norm = normalized[...]
    st = stats[...]
    mean = jnp.sum(z * norm, axis=-1, keepdims=True) * (1.0 / (HEADS * HD))
    rg = cot[...].astype(F32) + st[:, HEADS : HEADS + 1] * (z - norm * mean)
    for h in range(HEADS):
        n = normed[:, head(h)]
        g = rg[:, head(h)]
        m = jnp.mean(g * n, axis=-1, keepdims=True)
        a = (st[:, h : h + 1] * (g - n * m)).astype(BF16)
        for k in range(8):
            out[k, :, head(h)] = a


def query_grad_body(da8, key, value, mask, cm, cum, cum_t, carried, out):
    da = da8[0]
    pick_t = (iota((HD, 32), 0) == mask[...]).astype(BF16)
    cmv = cm[...]
    cumv = cum[...]
    rising = jnp.exp(cmv)
    falling = jnp.exp(cum_t[HD - 1 : HD, :] - cmv)
    for h in range(HEADS):
        fwd, bwd = states_of(carried, h)
        a = da[:, head(h)]
        s = nt(a, value[:, head(h)])
        p = (s * jnp.exp(-jnp.abs(cmv[:, h : h + 1] - cumv[h : h + 1, :]))).astype(BF16)
        q = nn(p, key[:, head(h)]) + rising[:, h : h + 1] * nt(a, fwd) + falling[:, h : h + 1] * nt(a, bwd)
        out[:, head(h)] = nn(pick_t, q.astype(BF16)).astype(BF16)


def scores_body(mine, parts, qm_all, key, cum_t, decay_out, scores_out):
    n = parts.shape[0]
    lane, col = iota((HD, n * 32), 0), iota((HD, n * 32), 1)
    block = col // 32
    me = mine[0]
    at = jnp.zeros((HEADS, n * 32), F32)
    for a in range(n):
        own = (lane < 96) & (lane % 32 == col % 32) & (block == a)
        ends = (lane >= 96) & (lane < 99)
        after = ends & (block > a) & (a >= me)
        before = ends & (block <= a) & (a < me)
        take = jnp.where(own | after, 1.0, jnp.where(before, -1.0, 0.0)).astype(BF16)
        at = at + nn(parts[a, 512:528, :], take)
    ct = cum_t[...]
    for h in range(HEADS):
        decay = jnp.exp(-jnp.abs(ct[:, h : h + 1] - at[h : h + 1, :]))
        decay_out[h] = decay
        qm = qm_all[:, :, head(h)].reshape(n * 32, HD)
        scores_out[h] = (nt(key[:, head(h)], qm) * decay).astype(BF16)


def key_value_grads_body(da_all, qm_all, value, decay, scores, key_out, value_out):
    rows = da_all.shape[0] * 32
    for h in range(HEADS):
        da = da_all[:, :, head(h)].reshape(rows, HD)
        qm = qm_all[:, :, head(h)].reshape(rows, HD)
        value_out[:, head(h)] = nn(scores[h], da).astype(BF16)
        p = (nt(value[:, head(h)], da) * decay[h]).astype(BF16)
        key_out[:, head(h)] = nn(p, qm).astype(BF16)


def local(residual, query, key, value, ld, cot, mask, routes, gates, up, down):
    residual, query, key, value, ld = residual[0], query[0], key[0], value[0], ld[0]
    cot, mask, routes, gates, up, down = cot[0, 0], mask[0], routes[0, 0], gates[0, 0], up[0], down[0]
    width = HEADS * HD
    ny, nx, nz, nc = (lax.axis_size(a) for a in ("y", "xl", "z", "c"))
    shard = up.shape[0]
    mine = (lax.axis_index("y") * nx + lax.axis_index("xl")).astype(jnp.int32).reshape(1)
    places = jnp.concatenate((mask, mask, mask, jnp.full_like(mask, HD - 1)), axis=1)

    [w0] = call(weights_body, [((4, shard, 384), BF16)], up, down)
    states, cum, cum_t = call(
        states_body,
        [((8, 528, HD), BF16), ((HEADS, HD), F32), ((HD, HEADS), F32)],
        ld, key, value, places,
    )
    parts = exchange(states, SEQ)
    w1 = exchange(w0, ("xl", "c"))
    qm, rm, inner, sg, cm = call(
        masked_body,
        [((32, width), BF16), ((32, width), F32), ((32, width), F32), ((8, 32, width), BF16), ((32, HEADS), F32)],
        query, key, value, residual, cot, mask, routes, gates, cum, cum_t,
    )
    [carries] = call(carry_body, [((8, 512, HD), BF16)], mine, parts, scalar=True)
    carried = exchange(carries, SEQ)
    w2 = broadcast(w1.reshape(4 * shard, 384), "z", nz)
    w3 = broadcast(w2.reshape(nz * 4 * shard, 384), "y", ny)
    grads = exchange(sg, GRP)
    routed8, normed, normalized, stats = call(
        rows_body,
        [((8, 32, width), BF16), ((32, width), F32), ((32, width), F32), ((32, HD), F32)],
        qm, rm, inner, cm, cum_t, carried,
    )
    rows = exchange(routed8, GRP)
    weights = w3.reshape(ny, nz, nx, nc * shard, 384)
    z_send, dw = expert_call(rows, grads, weights, ny)
    z_parts = exchange(z_send, GRP)
    [da8] = call(grads_body, [((8, 32, width), BF16)], z_parts, cot, normed, normalized, stats)
    da_all = exchange(da8, SEQ)
    qm_all = broadcast(qm, SEQ, 8)
    [query_grad] = call(query_grad_body, [((HD, width), BF16)], da8, key, value, mask, cm, cum, cum_t, carried)
    decay, scores = call(
        scores_body,
        [((HEADS, HD, 256), F32), ((HEADS, HD, 256), BF16)],
        mine, parts, qm_all, key, cum_t,
        scalar=True,
    )
    key_grad, value_grad = call(
        key_value_grads_body,
        [((HD, width), BF16), ((HD, width), BF16)],
        da_all, qm_all, value, decay, scores,
    )
    d1 = exchange(dw, "y")
    [d2] = call(sum_y_body, [((nz, nx, nc * shard, 384), BF16)], d1)
    d3 = exchange(d2, "z")
    [d4] = call(sum_z_body, [((nx, nc * shard, 384), F32)], d3)
    d5 = exchange(d4.reshape(4, shard, 384), ("xl", "c"))
    scale = 1.0 / (ny * nx * nz * nc)

    def finish(g, a, b):
        weight_grads_body(scale, g, a, b)

    up_grad, down_grad = call(finish, [((shard, 768), F32), ((shard, 768), F32)], d5)
    return query_grad[None], key_grad[None], value_grad[None], up_grad[None], down_grad[None]


def expert_call(rows, grads, weights, ny):
    width = rows.shape[2]
    outs = [
        jax.ShapeDtypeStruct(rows.shape, BF16),
        jax.ShapeDtypeStruct((ny, width // ny, 384), BF16),
    ]
    moved = sum(a.size * a.dtype.itemsize for a in (rows, grads, weights, *outs))
    return pl.pallas_call(
        expert_body,
        out_shape=outs,
        scratch_shapes=[pltpu.VMEM((width, 384), BF16)],
        compiler_params=pltpu.CompilerParams(vmem_limit_bytes=44 << 20),
        cost_estimate=pl.CostEstimate(flops=2 * 10**9, bytes_accessed=moved, transcendentals=0),
    )(rows, grads, weights)


def solution(mesh):
    shape = mesh.shape
    grid = mesh.devices.reshape(shape["seq"] // 2, 2, shape["rep"] // 2, 2, shape["exp"])
    fine = Mesh(grid, ("y", "xl", "z", "c", "e"))
    sequences, data = ("z", "c", "e"), ("y", "xl", "z", "c")
    in_specs = (
        P(sequences, SEQ, None),
        P(sequences, SEQ, None),
        P(sequences, SEQ, None),
        P(sequences, SEQ, None),
        P(sequences, None, SEQ),
        P(sequences, SEQ, None, None),
        P(sequences, SEQ, None),
        P(sequences, SEQ, None, None),
        P(sequences, SEQ, None, None),
        P("e", data, None),
        P("e", data, None),
    )
    out_specs = (
        P(sequences, SEQ, None),
        P(sequences, SEQ, None),
        P(sequences, SEQ, None),
        P("e", data, None),
        P("e", data, None),
    )
    return jax.shard_map(local, mesh=fine, in_specs=in_specs, out_specs=out_specs, check_vma=False)
```

```python
import jax
import jax.numpy as jnp
from jax import lax
from jax.experimental import pallas as pl
from jax.experimental.pallas import tpu as pltpu
from jax.sharding import Mesh, PartitionSpec as P

HEADS = 16
HD = 128
EPS = 1e-05
SEQ = ("y", "xl")
GRP = ("xl", "c", "e")
Y, XL, Z, C, E = range(5)
F32 = jnp.float32
BF16 = jnp.bfloat16
HIGH = lax.Precision.HIGHEST


def call(body, outs, *args, flops=10**8, scalar=False, scratch=()):
    shapes = [jax.ShapeDtypeStruct(s, d) for s, d in outs]
    moved = sum(a.size * a.dtype.itemsize for a in (*args, *shapes))
    spaces = [pltpu.SMEM if scalar and k == 0 else pltpu.VMEM for k in range(len(args))]
    result = pl.pallas_call(
        body,
        out_shape=shapes,
        in_specs=[pl.BlockSpec(memory_space=m) for m in spaces],
        scratch_shapes=list(scratch),
        compiler_params=pltpu.CompilerParams(vmem_limit_bytes=20 << 20),
        cost_estimate=pl.CostEstimate(flops=flops, bytes_accessed=moved, transcendentals=0),
    )(*args)
    return result


def iota(shape, dim):
    return lax.broadcasted_iota(jnp.int32, shape, dim)


def tn(a, b, **kw):
    return lax.dot_general(a, b, (((0,), (0,)), ((), ())), preferred_element_type=F32, **kw)


def nt(a, b, **kw):
    return lax.dot_general(a, b, (((1,), (1,)), ((), ())), preferred_element_type=F32, **kw)


def nn(a, b, **kw):
    return lax.dot_general(a, b, (((1,), (0,)), ((), ())), preferred_element_type=F32, **kw)


def head(h):
    return slice(h * HD, (h + 1) * HD)


def exchange(x, axes):
    return lax.all_to_all(x, axes, split_axis=0, concat_axis=0, tiled=True)


def prepare_body(ids, up, down, cot, mask, routes, gates, w0, w1, w2, w3, own_out, other_out, slices):
    low = iota((up.shape[0], HD), 1) < 64
    for c in range(12):
        u = up[:, head(c // 2)].astype(F32)
        d = down[:, head(c // 2)].astype(F32)
        if c % 2:
            u = pltpu.roll(u, 64, 1)
        else:
            d = pltpu.roll(d, 64, 1)
        slices[c // 3, :, head(c % 3)] = jnp.where(low, u, d).astype(BF16)
    for k, w in enumerate((w0, w1, w2, w3)):
        w[...] = slices[(ids[XL] * 2 + ids[C]) ^ k]
    lane = iota((HD, HD), 1)
    sub = iota((HD, HD), 0)
    table = jnp.zeros((HD, HD), F32)
    for e in range(2):
        hit = jnp.where(sub == routes[e : e + 1, :], gates[e : e + 1, :], 0.0)
        table = jnp.where(lane == e, jnp.sum(hit, axis=1, keepdims=True), table)
    pick_f = (iota((HD, 32), 0) == mask[...]).astype(F32)
    gm = tn(pick_f, table, precision=HIGH)
    cotf = cot[...].astype(F32)
    first, second = (gm[:, 0:1] * cotf).astype(BF16), (gm[:, 1:2] * cotf).astype(BF16)
    swap = ids[E] == 1
    own_out[...] = jnp.where(swap, second, first)
    other_out[...] = jnp.where(swap, first, second)


def weight_grads_body(scale, g, up, down):
    low = iota((up.shape[0], HD), 1) < 64
    for b in range(6):
        first, second = 2 * b, 2 * b + 1
        x = g[first // 3, :, head(first % 3)] * scale
        y = g[second // 3, :, head(second % 3)] * scale
        up[:, head(b)] = jnp.where(low, x, pltpu.roll(y, 64, 1))
        down[:, head(b)] = jnp.where(low, pltpu.roll(x, 64, 1), y)


def states_body(ld, key, value, places, out, cum_out, cum_t_out):
    rows, cols = iota((HD, HD), 0), iota((HD, HD), 1)
    ldv = ld[...]
    cum = nn(ldv, (rows <= cols).astype(F32), precision=HIGH)
    cum_t = nt((cols <= rows).astype(F32), ldv, precision=HIGH)
    cum_out[...] = cum
    cum_t_out[...] = cum_t
    falling = jnp.exp(cum_t[HD - 1 : HD, :] - cum_t)
    rising = jnp.exp(cum_t)
    for h in range(HEADS):
        k = key[:, head(h)].astype(F32)
        kf = (k * falling[:, h : h + 1]).astype(BF16)
        kb = (k * rising[:, h : h + 1]).astype(BF16)
        v = value[:, head(h)]
        g, at = h // 2, (h % 2) * HD
        out[g, at : at + HD, :] = tn(kf, v).astype(BF16)
        out[g, 256 + at : 256 + at + HD, :] = tn(kb, v).astype(BF16)
    chosen = nn(cum, (rows == places[...]).astype(F32), precision=HIGH)
    hi = chosen.astype(BF16).astype(F32)
    mid = (chosen - hi).astype(BF16).astype(F32)
    low = (chosen - hi - mid).astype(BF16).astype(F32)
    lane = iota((HEADS, HD), 1)
    first = (lane < 32) | (lane == 96)
    second = ((lane >= 32) & (lane < 64)) | (lane == 97)
    third = ((lane >= 64) & (lane < 96)) | (lane == 98)
    packed = jnp.where(first, hi, jnp.where(second, mid, jnp.where(third, low, 0.0))).astype(BF16)
    for g in range(8):
        out[g, 512:528, :] = packed


def masked_body(query, key, value, residual, mask, cum, cum_t, qm_out, rm_out, inner_out, cm_out):
    pick_t = (iota((HD, 32), 0) == mask[...]).astype(BF16)
    qm = tn(pick_t, query[...]).astype(BF16)
    qm_out[...] = qm
    rm_out[...] = tn(pick_t, residual[...])
    cm = tn(pick_t.astype(F32), cum_t[...], precision=HIGH)
    cm_out[...] = cm
    cumv = cum[...]
    for h in range(HEADS):
        s = nt(qm[:, head(h)], key[:, head(h)])
        p = (s * jnp.exp(-jnp.abs(cm[:, h : h + 1] - cumv[h : h + 1, :]))).astype(BF16)
        inner_out[:, head(h)] = nn(p, value[:, head(h)])


def carry_body(ids, parts, out):
    row, lane = iota((HEADS, HD), 0), iota((HEADS, HD), 1)
    ends = (lane >= 96) & (lane < 99)
    n = parts.shape[0]
    for j in range(2):
        at = slice(j * HD, (j + 1) * HD)
        back = slice(256 + j * HD, 256 + (j + 1) * HD)
        wanted = ends & (row == 2 * (2 * ids[Y] + ids[XL]) + j)
        decay = [
            jnp.exp(jnp.sum(jnp.where(wanted, parts[a, 512:528, :].astype(F32), 0.0), keepdims=True))
            for a in range(n)
        ]
        run = jnp.zeros((HD, HD), F32)
        for a in range(n):
            out[a, at, :] = run.astype(BF16)
            run = decay[a] * run + parts[a, at, :].astype(F32)
        run = jnp.zeros((HD, HD), F32)
        for a in reversed(range(n)):
            out[a, back, :] = run.astype(BF16)
            run = decay[a] * run + parts[a, back, :].astype(F32)


def states_of(carried, h):
    at = (h % 2) * HD
    return carried[h // 2, at : at + HD, :], carried[h // 2, 256 + at : 256 + at + HD, :]


def rows_body(qm, rm, inner, cm, cum_t, carried, routed_out, normed_out, normalized_out, stats_out):
    cmv = cm[...]
    rising = jnp.exp(cmv)
    falling = jnp.exp(cum_t[HD - 1 : HD, :] - cmv)
    lane = iota((32, HD), 1)
    stats = jnp.zeros((32, HD), F32)
    total = jnp.zeros((32, HD), F32)
    residuals = []
    for h in range(HEADS):
        fwd, bwd = states_of(carried, h)
        q = qm[:, head(h)]
        attn = inner[:, head(h)] + rising[:, h : h + 1] * nn(q, fwd) + falling[:, h : h + 1] * nn(q, bwd)
        scale = lax.rsqrt(jnp.mean(attn * attn, axis=-1, keepdims=True) + EPS)
        normed = attn * scale
        normed_out[:, head(h)] = normed
        stats = jnp.where(lane == h, scale, stats)
        r = (rm[:, head(h)] + normed).astype(BF16).astype(F32)
        total = total + r * r
        residuals.append(r)
    row_scale = lax.rsqrt(jnp.sum(total, axis=-1, keepdims=True) * (1.0 / (HEADS * HD)) + EPS)
    stats_out[...] = jnp.where(lane == HEADS, row_scale, stats)
    for h in range(HEADS):
        normalized = residuals[h] * row_scale
        normalized_out[:, head(h)] = normalized
        routed = normalized.astype(BF16)
        for k in range(8):
            routed_out[k, :, head(h)] = routed


def expert_body(ids, rows, grads, w0, w1, w2, w3, z_out, d0, d1, d2, d3, w_ref, g_ref):
    nz, unit = w0.shape[0], w0.shape[2]
    for k, piece in enumerate((w0, w1, w2, w3)):
        y = (ids[Y] + 4 - k) % 4
        for zs in range(nz):
            for cs in range(4):
                x = ids[XL] ^ (cs // 2)
                at = (((y * 2 + x) * nz + (ids[Z] ^ zs)) * 2 + (ids[C] ^ (cs % 2))) * unit
                w_ref[pl.ds(pl.multiple_of(at, unit), unit), :] = piece[zs, cs]
    for k in range(8):
        slot = ((k % 2) ^ ids[E]) + 2 * ((k // 4) ^ ids[XL]) + 4 * ((k // 2 % 2) ^ ids[C])
        g_ref[k] = grads[slot]
    width = HEADS * HD
    r = rows[...].reshape(256, width)
    g = g_ref[...].reshape(256, width)
    w = w_ref[...]
    pre_all = nn(r, w)
    grad_all = nn(g, w)
    low = iota((256, HD), 1) < 64
    pgs, acts = [], []
    for b in range(3):
        pre = pre_all[:, head(b)]
        act_grad = pltpu.roll(grad_all[:, head(b)], 64, 1)
        sig = jax.nn.sigmoid(pre)
        act = pltpu.roll(pre * sig, 64, 1)
        pre_grad = act_grad * sig * (1.0 + pre * (1.0 - sig))
        pgs.append(jnp.where(low, pre_grad, 0.0).astype(BF16))
        acts.append(jnp.where(low, 0.0, act).astype(BF16))
    pg = jnp.concatenate(pgs, axis=1)
    ac = jnp.concatenate(acts, axis=1)
    z_out[...] = nt(pg, w).astype(BF16).reshape(z_out.shape)
    both = jnp.concatenate((pg, ac), axis=0)
    for k, out in enumerate((d0, d1, d2, d3)):
        y = (ids[Y] + k) % 4
        cols = pl.ds(pl.multiple_of(y * 512, 512), 512)
        sides = jnp.concatenate((rows[:, :, cols].reshape(256, 512), g_ref[:, :, cols].reshape(256, 512)), axis=0)
        out[...] = tn(sides, both).astype(BF16)


def sum_y_body(p0, p1, p2, p3, out):
    nz, nx, unit = out.shape[:3]
    for x in range(nx):
        for z in range(nz):
            at = slice((x * nz + z) * unit, (x * nz + z + 1) * unit)
            total = p0[at, :].astype(F32) + p1[at, :].astype(F32) + p2[at, :].astype(F32) + p3[at, :].astype(F32)
            out[z, x] = total.astype(BF16)


def sum_z_body(parts, out):
    total = parts[0].astype(F32)
    for z in range(1, parts.shape[0]):
        total = total + parts[z].astype(F32)
    out[...] = total


def grads_body(z_parts, cot, normed, normalized, stats, out):
    z = z_parts[0].astype(F32)
    for k in range(1, 8):
        z = z + z_parts[k].astype(F32)
    norm = normalized[...]
    st = stats[...]
    mean = jnp.sum(z * norm, axis=-1, keepdims=True) * (1.0 / (HEADS * HD))
    rg = cot[...].astype(F32) + st[:, HEADS : HEADS + 1] * (z - norm * mean)
    for h in range(HEADS):
        n = normed[:, head(h)]
        g = rg[:, head(h)]
        m = jnp.mean(g * n, axis=-1, keepdims=True)
        out[:, head(h)] = (st[:, h : h + 1] * (g - n * m)).astype(BF16)


def query_grad_body(da_own, key, value, mask, cm, cum, cum_t, carried, out):
    da = da_own[...]
    pick_t = (iota((HD, 32), 0) == mask[...]).astype(BF16)
    cmv = cm[...]
    cumv = cum[...]
    rising = jnp.exp(cmv)
    falling = jnp.exp(cum_t[HD - 1 : HD, :] - cmv)
    for h in range(HEADS):
        fwd, bwd = states_of(carried, h)
        a = da[:, head(h)]
        s = nt(a, value[:, head(h)])
        p = (s * jnp.exp(-jnp.abs(cmv[:, h : h + 1] - cumv[h : h + 1, :]))).astype(BF16)
        q = nn(p, key[:, head(h)]) + rising[:, h : h + 1] * nt(a, fwd) + falling[:, h : h + 1] * nt(a, bwd)
        out[:, head(h)] = nn(pick_t, q.astype(BF16)).astype(BF16)


def rows_of(pieces, h):
    return jnp.concatenate([p[:, :, head(h)].reshape(64, HD) for p in pieces], axis=0)


def scores_body(ids, parts, q0, q1, q2, q3, key, cum_t, decay_out, scores_out):
    n = parts.shape[0]
    lane, col = iota((HD, n * 32), 0), iota((HD, n * 32), 1)
    me = 2 * ids[Y] + ids[XL]
    block = jnp.zeros((HD, n * 32), jnp.int32)
    for k in range(n):
        there = 2 * ((ids[Y] + 4 - k // 2) % 4) + (ids[XL] ^ (k % 2))
        block = jnp.where(col // 32 == k, there, block)
    at = jnp.zeros((HEADS, n * 32), F32)
    for a in range(n):
        own = (lane < 96) & (lane % 32 == col % 32) & (block == a)
        ends = (lane >= 96) & (lane < 99)
        after = ends & (block > a) & (a >= me)
        before = ends & (block <= a) & (a < me)
        take = jnp.where(own | after, 1.0, jnp.where(before, -1.0, 0.0)).astype(BF16)
        at = at + nn(parts[a, 512:528, :], take)
    ct = cum_t[...]
    for h in range(HEADS):
        decay = jnp.exp(-jnp.abs(ct[:, h : h + 1] - at[h : h + 1, :]))
        decay_out[h] = decay
        scores_out[h] = (nt(key[:, head(h)], rows_of((q0, q1, q2, q3), h)) * decay).astype(BF16)


def key_value_grads_body(a0, a1, a2, a3, q0, q1, q2, q3, value, decay, scores, key_out, value_out):
    for h in range(HEADS):
        da = rows_of((a0, a1, a2, a3), h)
        value_out[:, head(h)] = nn(scores[h], da).astype(BF16)
        p = (nt(value[:, head(h)], da) * decay[h]).astype(BF16)
        key_out[:, head(h)] = nn(p, rows_of((q0, q1, q2, q3), h)).astype(BF16)


def trade(x, axis, bit=1):
    n = lax.axis_size(axis)
    return lax.ppermute(x, axis, [(i, i ^ bit) for i in range(n)])


def turn(x, k):
    n = lax.axis_size("y")
    return lax.ppermute(x, "y", [(i, (i + k) % n) for i in range(n)])


def along_y(x):
    return [x] + [turn(x, k) for k in range(1, 4)]


def along_sequence(x):
    return along_y(jnp.stack((x, trade(x, "xl"))))


def local(residual, query, key, value, ld, cot, mask, routes, gates, up, down):
    residual, query, key, value, ld = residual[0], query[0], key[0], value[0], ld[0]
    cot, mask, routes, gates, up, down = cot[0, 0], mask[0], routes[0, 0], gates[0, 0], up[0], down[0]
    width = HEADS * HD
    ny, nx, nz, nc = (lax.axis_size(a) for a in ("y", "xl", "z", "c"))
    shard = up.shape[0]
    ids = jnp.stack([lax.axis_index(a) for a in ("y", "xl", "z", "c", "e")]).astype(jnp.int32)
    places = jnp.concatenate((mask, mask, mask, jnp.full_like(mask, HD - 1)), axis=1)

    prepared = call(
        prepare_body,
        [((shard, 384), BF16)] * 4 + [((32, width), BF16)] * 2,
        ids, up, down, cot, mask, routes, gates,
        scalar=True,
        scratch=[pltpu.VMEM((4, shard, 384), BF16)],
    )
    w = [prepared[0]] + [
        lax.ppermute(prepared[k], ("xl", "c"), [(i, i ^ k) for i in range(4)]) for k in range(1, 4)
    ]
    grads = jnp.stack((prepared[4], trade(prepared[5], "e")))
    states, cum, cum_t = call(
        states_body,
        [((8, 528, HD), BF16), ((HEADS, HD), F32), ((HD, HEADS), F32)],
        ld, key, value, places,
    )
    parts = exchange(states, SEQ)
    qm, rm, inner, cm = call(
        masked_body,
        [((32, width), BF16), ((32, width), F32), ((32, width), F32), ((32, HEADS), F32)],
        query, key, value, residual, mask, cum, cum_t,
    )
    [carries] = call(carry_body, [((8, 512, HD), BF16)], ids, parts, scalar=True)
    carried = exchange(carries, SEQ)
    grads = jnp.concatenate((grads, trade(grads, "xl")))
    grads = jnp.concatenate((grads, trade(grads, "c")))
    w = jnp.stack(w)[None]
    bit = 1
    while bit < nz:
        w = jnp.concatenate((w, trade(w, "z", bit)))
        bit *= 2
    routed8, normed, normalized, stats = call(
        rows_body,
        [((8, 32, width), BF16), ((32, width), F32), ((32, width), F32), ((32, HD), F32)],
        qm, rm, inner, cm, cum_t, carried,
    )
    weights = along_y(w)
    rows = exchange(routed8, GRP)
    z_send, *dw = call(
        expert_body,
        [((8, 32, width), BF16)] + [((width // ny, 384), BF16)] * 4,
        ids, rows, grads, *weights,
        scalar=True,
        scratch=[pltpu.VMEM((width, 384), BF16), pltpu.VMEM((8, 32, width), BF16)],
        flops=2 * 10**9,
    )
    z_parts = exchange(z_send, GRP)
    queries = along_sequence(qm)
    d1 = [dw[0]] + [turn(dw[k], k) for k in range(1, 4)]
    decay, scores = call(
        scores_body,
        [((HEADS, HD, 256), F32), ((HEADS, HD, 256), BF16)],
        ids, parts, *queries, key, cum_t,
        scalar=True,
    )
    [da] = call(grads_body, [((32, width), BF16)], z_parts, cot, normed, normalized, stats)
    das = along_sequence(da)
    [d2] = call(sum_y_body, [((nz, nx, nc * shard, 384), BF16)], *d1)
    d3 = exchange(d2, "z")
    [query_grad] = call(query_grad_body, [((HD, width), BF16)], da, key, value, mask, cm, cum, cum_t, carried)
    [d4] = call(sum_z_body, [((nx, nc * shard, 384), F32)], d3)
    d5 = exchange(d4.reshape(4, shard, 384), ("xl", "c"))
    key_grad, value_grad = call(
        key_value_grads_body,
        [((HD, width), BF16), ((HD, width), BF16)],
        *das, *queries, value, decay, scores,
    )
    scale = 1.0 / (ny * nx * nz * nc)

    def finish(g, a, b):
        weight_grads_body(scale, g, a, b)

    up_grad, down_grad = call(finish, [((shard, 768), F32), ((shard, 768), F32)], d5)
    return query_grad[None], key_grad[None], value_grad[None], up_grad[None], down_grad[None]


def solution(mesh):
    shape = mesh.shape
    grid = mesh.devices.reshape(shape["seq"] // 2, 2, shape["rep"] // 2, 2, shape["exp"])
    fine = Mesh(grid, ("y", "xl", "z", "c", "e"))
    sequences, data = ("z", "c", "e"), ("y", "xl", "z", "c")
    in_specs = (
        P(sequences, SEQ, None),
        P(sequences, SEQ, None),
        P(sequences, SEQ, None),
        P(sequences, SEQ, None),
        P(sequences, None, SEQ),
        P(sequences, SEQ, None, None),
        P(sequences, SEQ, None),
        P(sequences, SEQ, None, None),
        P(sequences, SEQ, None, None),
        P("e", data, None),
        P("e", data, None),
    )
    out_specs = (
        P(sequences, SEQ, None),
        P(sequences, SEQ, None),
        P(sequences, SEQ, None),
        P("e", data, None),
        P("e", data, None),
    )
    return jax.shard_map(local, mesh=fine, in_specs=in_specs, out_specs=out_specs, check_vma=False)
```

```python
import jax
import jax.numpy as jnp
from jax import lax
from jax.experimental import pallas as pl
from jax.experimental.pallas import tpu as pltpu
from jax.sharding import Mesh, PartitionSpec as P

HEADS = 16
HD = 128
EPS = 1e-05
SEQ = ("y", "xl")
GRP = ("xl", "c", "e")
Y, XL, Z, C, E = range(5)
F32 = jnp.float32
BF16 = jnp.bfloat16
HIGH = lax.Precision.HIGHEST


def call(body, outs, *args, flops=10**8, scalar=False, scratch=()):
    shapes = [jax.ShapeDtypeStruct(s, d) for s, d in outs]
    moved = sum(a.size * a.dtype.itemsize for a in (*args, *shapes))
    in_specs = [pl.BlockSpec()] * len(args)
    if scalar:
        in_specs[0] = pl.BlockSpec(memory_space=pltpu.SMEM)
    result = pl.pallas_call(
        body,
        out_shape=shapes,
        in_specs=in_specs,
        scratch_shapes=list(scratch),
        compiler_params=pltpu.CompilerParams(vmem_limit_bytes=56 << 20),
        cost_estimate=pl.CostEstimate(flops=flops, bytes_accessed=moved, transcendentals=0),
    )(*args)
    return result


def iota(shape, dim):
    return lax.broadcasted_iota(jnp.int32, shape, dim)


def tn(a, b, **kw):
    return lax.dot_general(a, b, (((0,), (0,)), ((), ())), preferred_element_type=F32, **kw)


def nt(a, b, **kw):
    return lax.dot_general(a, b, (((1,), (1,)), ((), ())), preferred_element_type=F32, **kw)


def nn(a, b, **kw):
    return lax.dot_general(a, b, (((1,), (0,)), ((), ())), preferred_element_type=F32, **kw)


def head(h):
    return slice(h * HD, (h + 1) * HD)


def exchange(x, axes):
    return lax.all_to_all(x, axes, split_axis=0, concat_axis=0, tiled=True)


def prepare_body(ids, up, down, cot, mask, routes, gates, w0, w1, w2, w3, own_out, other_out, slices):
    low = iota((up.shape[0], HD), 1) < 64
    for c in range(12):
        u = up[:, head(c // 2)].astype(F32)
        d = down[:, head(c // 2)].astype(F32)
        if c % 2:
            u = pltpu.roll(u, 64, 1)
        else:
            d = pltpu.roll(d, 64, 1)
        slices[c // 3, :, head(c % 3)] = jnp.where(low, u, d).astype(BF16)
    for k, w in enumerate((w0, w1, w2, w3)):
        w[...] = slices[(ids[XL] * 2 + ids[C]) ^ k]
    lane = iota((HD, HD), 1)
    sub = iota((HD, HD), 0)
    table = jnp.zeros((HD, HD), F32)
    for e in range(2):
        hit = jnp.where(sub == routes[e : e + 1, :], gates[e : e + 1, :], 0.0)
        table = jnp.where(lane == e, jnp.sum(hit, axis=1, keepdims=True), table)
    pick_f = (iota((HD, 32), 0) == mask[...]).astype(F32)
    gm = tn(pick_f, table, precision=HIGH)
    cotf = cot[...].astype(F32)
    first, second = (gm[:, 0:1] * cotf).astype(BF16), (gm[:, 1:2] * cotf).astype(BF16)
    swap = ids[E] == 1
    own_out[...] = jnp.where(swap, second, first)
    other_out[...] = jnp.where(swap, first, second)


def weight_grads_body(scale, g, up, down):
    low = iota((up.shape[0], HD), 1) < 64
    for b in range(6):
        first, second = 2 * b, 2 * b + 1
        x = g[first // 3, :, head(first % 3)] * scale
        y = g[second // 3, :, head(second % 3)] * scale
        up[:, head(b)] = jnp.where(low, x, pltpu.roll(y, 64, 1))
        down[:, head(b)] = jnp.where(low, pltpu.roll(x, 64, 1), y)


def states_body(ld, key, value, mask, out, cum_out, cum_t_out):
    rows, cols = iota((HD, HD), 0), iota((HD, HD), 1)
    ldv = ld[...]
    cum = nn(ldv, (rows <= cols).astype(F32), precision=HIGH)
    cum_t = nt((cols <= rows).astype(F32), ldv, precision=HIGH)
    cum_out[...] = cum
    cum_t_out[...] = cum_t
    falling = jnp.exp(cum_t[HD - 1 : HD, :] - cum_t)
    rising = jnp.exp(cum_t)
    for h in range(HEADS):
        k = key[:, head(h)].astype(F32)
        kf = (k * falling[:, h : h + 1]).astype(BF16)
        kb = (k * rising[:, h : h + 1]).astype(BF16)
        v = value[:, head(h)]
        g, at = h // 2, (h % 2) * HD
        out[g, at : at + HD, :] = tn(kf, v).astype(BF16)
        out[g, 256 + at : 256 + at + HD, :] = tn(kb, v).astype(BF16)
    repeat = (iota((32, HD), 0) == iota((32, HD), 1) % 32).astype(BF16)
    places = nn(mask[...].astype(F32).astype(BF16), repeat).astype(jnp.int32)
    places = jnp.where(iota((1, HD), 1) < 96, places, HD - 1)
    chosen = nn(cum, (rows == places).astype(F32), precision=HIGH)
    hi = chosen.astype(BF16).astype(F32)
    mid = (chosen - hi).astype(BF16).astype(F32)
    low = (chosen - hi - mid).astype(BF16).astype(F32)
    lane = iota((HEADS, HD), 1)
    first = (lane < 32) | (lane == 96)
    second = ((lane >= 32) & (lane < 64)) | (lane == 97)
    third = ((lane >= 64) & (lane < 96)) | (lane == 98)
    packed = jnp.where(first, hi, jnp.where(second, mid, jnp.where(third, low, 0.0))).astype(BF16)
    for g in range(8):
        out[g, 512:528, :] = packed


def masked_body(query, key, value, residual, mask, cum, cum_t, qm_out, rm_out, inner_out, cm_out):
    pick_t = (iota((HD, 32), 0) == mask[...]).astype(BF16)
    qm = tn(pick_t, query[...]).astype(BF16)
    qm_out[...] = qm
    rm_out[...] = tn(pick_t, residual[...])
    cm = tn(pick_t.astype(F32), cum_t[...], precision=HIGH)
    cm_out[...] = cm
    cumv = cum[...]
    for h in range(HEADS):
        s = nt(qm[:, head(h)], key[:, head(h)])
        p = (s * jnp.exp(-jnp.abs(cm[:, h : h + 1] - cumv[h : h + 1, :]))).astype(BF16)
        inner_out[:, head(h)] = nn(p, value[:, head(h)])


def carry_body(ids, parts, out):
    row, lane = iota((HEADS, HD), 0), iota((HEADS, HD), 1)
    ends = (lane >= 96) & (lane < 99)
    n = parts.shape[0]
    for j in range(2):
        at = slice(j * HD, (j + 1) * HD)
        back = slice(256 + j * HD, 256 + (j + 1) * HD)
        wanted = ends & (row == 2 * (2 * ids[Y] + ids[XL]) + j)
        decay = [
            jnp.exp(jnp.sum(jnp.where(wanted, parts[a, 512:528, :].astype(F32), 0.0), keepdims=True))
            for a in range(n)
        ]
        run = jnp.zeros((HD, HD), F32)
        for a in range(n):
            out[a, at, :] = run.astype(BF16)
            run = decay[a] * run + parts[a, at, :].astype(F32)
        run = jnp.zeros((HD, HD), F32)
        for a in reversed(range(n)):
            out[a, back, :] = run.astype(BF16)
            run = decay[a] * run + parts[a, back, :].astype(F32)


def states_of(carried, h):
    at = (h % 2) * HD
    return carried[h // 2, at : at + HD, :], carried[h // 2, 256 + at : 256 + at + HD, :]


def rows_body(qm, rm, inner, cm, cum_t, carried, routed_out, normed_out, normalized_out, stats_out):
    cmv = cm[...]
    rising = jnp.exp(cmv)
    falling = jnp.exp(cum_t[HD - 1 : HD, :] - cmv)
    lane = iota((32, HD), 1)
    stats = jnp.zeros((32, HD), F32)
    total = jnp.zeros((32, HD), F32)
    residuals = []
    for h in range(HEADS):
        fwd, bwd = states_of(carried, h)
        q = qm[:, head(h)]
        attn = inner[:, head(h)] + rising[:, h : h + 1] * nn(q, fwd) + falling[:, h : h + 1] * nn(q, bwd)
        scale = lax.rsqrt(jnp.mean(attn * attn, axis=-1, keepdims=True) + EPS)
        normed = attn * scale
        normed_out[:, head(h)] = normed
        stats = jnp.where(lane == h, scale, stats)
        r = (rm[:, head(h)] + normed).astype(BF16).astype(F32)
        total = total + r * r
        residuals.append(r)
    row_scale = lax.rsqrt(jnp.sum(total, axis=-1, keepdims=True) * (1.0 / (HEADS * HD)) + EPS)
    stats_out[...] = jnp.where(lane == HEADS, row_scale, stats)
    for h in range(HEADS):
        normalized = residuals[h] * row_scale
        normalized_out[:, head(h)] = normalized
        routed = normalized.astype(BF16)
        for k in range(8):
            routed_out[k, :, head(h)] = routed


def expert_body(ids, rows, g1, g2, g3, g4, w0, w1, w2, w3, z_out, d0, d1, d2, d3, w_ref, g_ref):
    nz, unit = w0.shape[0], w0.shape[2]
    for k, piece in enumerate((w0, w1, w2, w3)):
        y = (ids[Y] + 4 - k) % 4
        for zs in range(nz):
            for cs in range(4):
                x = ids[XL] ^ (cs // 2)
                at = (((y * 2 + x) * nz + (ids[Z] ^ zs)) * 2 + (ids[C] ^ (cs % 2))) * unit
                w_ref[pl.ds(pl.multiple_of(at, unit), unit), :] = piece[zs, cs]
    slot = 0
    for piece in (g1, g2, g3, g4):
        for j in range(piece.shape[0]):
            there = 4 * (ids[XL] ^ (slot // 2 % 2)) + 2 * (ids[C] ^ (slot // 4)) + (ids[E] ^ (slot % 2))
            g_ref[there] = piece[j]
            slot += 1
    width = HEADS * HD
    r = rows[...].reshape(256, width)
    g = g_ref[...].reshape(256, width)
    w = w_ref[...]
    pre_all = nn(r, w)
    grad_all = nn(g, w)
    low = iota((256, HD), 1) < 64
    pgs, acts = [], []
    for b in range(3):
        pre = pre_all[:, head(b)]
        act_grad = pltpu.roll(grad_all[:, head(b)], 64, 1)
        sig = jax.nn.sigmoid(pre)
        act = pltpu.roll(pre * sig, 64, 1)
        pre_grad = act_grad * sig * (1.0 + pre * (1.0 - sig))
        pgs.append(jnp.where(low, pre_grad, 0.0).astype(BF16))
        acts.append(jnp.where(low, 0.0, act).astype(BF16))
    pg = jnp.concatenate(pgs, axis=1)
    ac = jnp.concatenate(acts, axis=1)
    z_out[...] = nt(pg, w).astype(BF16).reshape(z_out.shape)
    both = jnp.concatenate((pg, ac), axis=0)
    for k, out in enumerate((d0, d1, d2, d3)):
        y = (ids[Y] + k) % 4
        cols = pl.ds(pl.multiple_of(y * 512, 512), 512)
        sides = jnp.concatenate((rows[:, :, cols].reshape(256, 512), g_ref[:, :, cols].reshape(256, 512)), axis=0)
        out[...] = tn(sides, both).astype(BF16)


def sum_y_body(p0, p1, p2, p3, out):
    nz, nx, unit = out.shape[:3]
    for x in range(nx):
        for z in range(nz):
            at = slice((x * nz + z) * unit, (x * nz + z + 1) * unit)
            total = p0[at, :].astype(F32) + p1[at, :].astype(F32) + p2[at, :].astype(F32) + p3[at, :].astype(F32)
            out[z, x] = total.astype(BF16)


def sum_z_body(parts, out):
    total = parts[0].astype(F32)
    for z in range(1, parts.shape[0]):
        total = total + parts[z].astype(F32)
    out[...] = total


def grads_body(z_parts, cot, normed, normalized, stats, out):
    z = z_parts[0].astype(F32)
    for k in range(1, 8):
        z = z + z_parts[k].astype(F32)
    norm = normalized[...]
    st = stats[...]
    mean = jnp.sum(z * norm, axis=-1, keepdims=True) * (1.0 / (HEADS * HD))
    rg = cot[...].astype(F32) + st[:, HEADS : HEADS + 1] * (z - norm * mean)
    for h in range(HEADS):
        n = normed[:, head(h)]
        g = rg[:, head(h)]
        m = jnp.mean(g * n, axis=-1, keepdims=True)
        out[:, head(h)] = (st[:, h : h + 1] * (g - n * m)).astype(BF16)


def query_grad_body(da_own, key, value, mask, cm, cum, cum_t, carried, out):
    da = da_own[...]
    pick_t = (iota((HD, 32), 0) == mask[...]).astype(BF16)
    cmv = cm[...]
    cumv = cum[...]
    rising = jnp.exp(cmv)
    falling = jnp.exp(cum_t[HD - 1 : HD, :] - cmv)
    for h in range(HEADS):
        fwd, bwd = states_of(carried, h)
        a = da[:, head(h)]
        s = nt(a, value[:, head(h)])
        p = (s * jnp.exp(-jnp.abs(cmv[:, h : h + 1] - cumv[h : h + 1, :]))).astype(BF16)
        q = nn(p, key[:, head(h)]) + rising[:, h : h + 1] * nt(a, fwd) + falling[:, h : h + 1] * nt(a, bwd)
        out[:, head(h)] = nn(pick_t, q.astype(BF16)).astype(BF16)


def rows_of(pieces, h):
    return jnp.concatenate([p[:, :, head(h)].reshape(64, HD) for p in pieces], axis=0)


def scores_body(ids, parts, q0, q1, q2, q3, key, cum_t, decay_out, scores_out):
    n = parts.shape[0]
    lane, col = iota((HD, n * 32), 0), iota((HD, n * 32), 1)
    me = 2 * ids[Y] + ids[XL]
    block = jnp.zeros((HD, n * 32), jnp.int32)
    for k in range(n):
        there = 2 * ((ids[Y] + 4 - k // 2) % 4) + (ids[XL] ^ (k % 2))
        block = jnp.where(col // 32 == k, there, block)
    at = jnp.zeros((HEADS, n * 32), F32)
    for a in range(n):
        own = (lane < 96) & (lane % 32 == col % 32) & (block == a)
        ends = (lane >= 96) & (lane < 99)
        after = ends & (block > a) & (a >= me)
        before = ends & (block <= a) & (a < me)
        take = jnp.where(own | after, 1.0, jnp.where(before, -1.0, 0.0)).astype(BF16)
        at = at + nn(parts[a, 512:528, :], take)
    ct = cum_t[...]
    for h in range(HEADS):
        decay = jnp.exp(-jnp.abs(ct[:, h : h + 1] - at[h : h + 1, :]))
        decay_out[h] = decay
        scores_out[h] = (nt(key[:, head(h)], rows_of((q0, q1, q2, q3), h)) * decay).astype(BF16)


def key_value_grads_body(a0, a1, a2, a3, q0, q1, q2, q3, value, decay, scores, key_out, value_out):
    for h in range(HEADS):
        da = rows_of((a0, a1, a2, a3), h)
        value_out[:, head(h)] = nn(scores[h], da).astype(BF16)
        p = (nt(value[:, head(h)], da) * decay[h]).astype(BF16)
        key_out[:, head(h)] = nn(p, rows_of((q0, q1, q2, q3), h)).astype(BF16)


def trade(x, axis, bit=1):
    n = lax.axis_size(axis)
    return lax.ppermute(x, axis, [(i, i ^ bit) for i in range(n)])


def turn(x, k):
    n = lax.axis_size("y")
    return lax.ppermute(x, "y", [(i, (i + k) % n) for i in range(n)])


def after(first, then):
    return lax.optimization_barrier((first, then))


def along_y(x):
    return [x] + [turn(x, k) for k in range(1, 4)]


def along_sequence(x):
    return along_y(jnp.stack((x, trade(x, "xl"))))


def local(residual, query, key, value, ld, cot, mask, routes, gates, up, down):
    residual, query, key, value, ld = residual[0], query[0], key[0], value[0], ld[0]
    cot, mask, routes, gates, up, down = cot[0, 0], mask[0], routes[0, 0], gates[0, 0], up[0], down[0]
    width = HEADS * HD
    ny, nx, nz, nc = (lax.axis_size(a) for a in ("y", "xl", "z", "c"))
    shard = up.shape[0]
    ids = jnp.stack([lax.axis_index(a) for a in ("y", "xl", "z", "c", "e")]).astype(jnp.int32)

    prepared = call(
        prepare_body,
        [((shard, 384), BF16)] * 4 + [((32, width), BF16)] * 2,
        ids, up, down, cot, mask, routes, gates,
        scalar=True,
        scratch=[pltpu.VMEM((4, shard, 384), BF16)],
    )
    prepared, ld = after(prepared, ld)
    w = [prepared[0]] + [
        lax.ppermute(prepared[k], ("xl", "c"), [(i, i ^ k) for i in range(4)]) for k in range(1, 4)
    ]
    own = prepared[4][None]
    from_e = trade(prepared[5][None], "e")
    states, cum, cum_t = call(
        states_body,
        [((8, 528, HD), BF16), ((HEADS, HD), F32), ((HD, HEADS), F32)],
        ld, key, value, mask,
    )
    parts = exchange(states, SEQ)
    qm, rm, inner, cm = call(
        masked_body,
        [((32, width), BF16), ((32, width), F32), ((32, width), F32), ((32, HEADS), F32)],
        query, key, value, residual, mask, cum, cum_t,
    )
    w = jnp.stack(w)[None]
    (w, from_e, qm), parts = after((w, from_e, qm), parts)
    [carries] = call(carry_body, [((8, 512, HD), BF16)], ids, parts, scalar=True)
    carried = exchange(carries, SEQ)
    two = jnp.concatenate((own, from_e))
    from_x = trade(two, "xl")
    q_two = jnp.stack((qm, trade(qm, "xl")))
    bit = 1
    while bit < nz:
        w = jnp.concatenate((w, trade(w, "z", bit)))
        bit *= 2
    (w, from_x, q_two), carried = after((w, from_x, q_two), carried)
    from_c = trade(jnp.concatenate((two, from_x)), "c")
    routed8, normed, normalized, stats = call(
        rows_body,
        [((8, 32, width), BF16), ((32, width), F32), ((32, width), F32), ((32, HD), F32)],
        qm, rm, inner, cm, cum_t, carried,
    )
    weights = along_y(w)
    rows = exchange(routed8, GRP)
    z_send, *dw = call(
        expert_body,
        [((8, 32, width), BF16)] + [((width // ny, 384), BF16)] * 4,
        ids, rows, own, from_e, from_x, from_c, *weights,
        scalar=True,
        scratch=[pltpu.VMEM((width, 384), BF16), pltpu.VMEM((8, 32, width), BF16)],
        flops=2 * 10**9,
    )
    q_two, dw = after(q_two, dw)
    queries = along_y(q_two)
    z_parts = exchange(z_send, GRP)
    d1 = [dw[0]] + [turn(dw[k], k) for k in range(1, 4)]
    (queries, d1), z_parts = after((queries, d1), z_parts)
    [da] = call(grads_body, [((32, width), BF16)], z_parts, cot, normed, normalized, stats)
    d1, da = after(d1, da)
    decay, scores = call(
        scores_body,
        [((HEADS, HD, 256), F32), ((HEADS, HD, 256), BF16)],
        ids, parts, *queries, key, cum_t,
        scalar=True,
    )
    das = along_sequence(da)
    [d2] = call(sum_y_body, [((nz, nx, nc * shard, 384), BF16)], *d1)
    d3 = exchange(d2, "z")
    [query_grad] = call(query_grad_body, [((HD, width), BF16)], da, key, value, mask, cm, cum, cum_t, carried)
    [d4] = call(sum_z_body, [((nx, nc * shard, 384), F32)], d3)
    d5 = exchange(d4.reshape(4, shard, 384), ("xl", "c"))
    key_grad, value_grad = call(
        key_value_grads_body,
        [((HD, width), BF16), ((HD, width), BF16)],
        *das, *queries, value, decay, scores,
    )
    scale = 1.0 / (ny * nx * nz * nc)

    def finish(g, a, b):
        weight_grads_body(scale, g, a, b)

    up_grad, down_grad = call(finish, [((shard, 768), F32), ((shard, 768), F32)], d5)
    return query_grad[None], key_grad[None], value_grad[None], up_grad[None], down_grad[None]


def solution(mesh):
    shape = mesh.shape
    grid = mesh.devices.reshape(shape["seq"] // 2, 2, shape["rep"] // 2, 2, shape["exp"])
    fine = Mesh(grid, ("y", "xl", "z", "c", "e"))
    sequences, data = ("z", "c", "e"), ("y", "xl", "z", "c")
    in_specs = (
        P(sequences, SEQ, None),
        P(sequences, SEQ, None),
        P(sequences, SEQ, None),
        P(sequences, SEQ, None),
        P(sequences, None, SEQ),
        P(sequences, SEQ, None, None),
        P(sequences, SEQ, None),
        P(sequences, SEQ, None, None),
        P(sequences, SEQ, None, None),
        P("e", data, None),
        P("e", data, None),
    )
    out_specs = (
        P(sequences, SEQ, None),
        P(sequences, SEQ, None),
        P(sequences, SEQ, None),
        P("e", data, None),
        P("e", data, None),
    )
    return jax.shard_map(local, mesh=fine, in_specs=in_specs, out_specs=out_specs, check_vma=False)
```

```python
import jax
import jax.numpy as jnp
from jax import lax
from jax.experimental import pallas as pl
from jax.experimental.pallas import tpu as pltpu
from jax.sharding import Mesh, PartitionSpec as P

HEADS = 16
HD = 128
EPS = 1e-05
SEQ = ("y", "xl")
Y, XL, Z, C, E = range(5)
F32 = jnp.float32
BF16 = jnp.bfloat16
HIGH = lax.Precision.HIGHEST


def call(body, outs, *args, flops=10**8, scalar=False, scratch=(), vmem=56):
    shapes = [jax.ShapeDtypeStruct(s, d) for s, d in outs]
    moved = sum(a.size * a.dtype.itemsize for a in (*args, *shapes))
    in_specs = [pl.BlockSpec()] * len(args)
    if scalar:
        in_specs[0] = pl.BlockSpec(memory_space=pltpu.SMEM)
    result = pl.pallas_call(
        body,
        out_shape=shapes,
        in_specs=in_specs,
        scratch_shapes=list(scratch),
        compiler_params=pltpu.CompilerParams(vmem_limit_bytes=vmem << 20),
        cost_estimate=pl.CostEstimate(flops=flops, bytes_accessed=moved, transcendentals=0),
    )(*args)
    return result


def iota(shape, dim):
    return lax.broadcasted_iota(jnp.int32, shape, dim)


def tn(a, b, **kw):
    return lax.dot_general(a, b, (((0,), (0,)), ((), ())), preferred_element_type=F32, **kw)


def nt(a, b, **kw):
    return lax.dot_general(a, b, (((1,), (1,)), ((), ())), preferred_element_type=F32, **kw)


def nn(a, b, **kw):
    return lax.dot_general(a, b, (((1,), (0,)), ((), ())), preferred_element_type=F32, **kw)


def head(h):
    return slice(h * HD, (h + 1) * HD)


def exchange(x, axes):
    return lax.all_to_all(x, axes, split_axis=0, concat_axis=0, tiled=True)


def prepare_body(ids, up, down, cot, mask, routes, gates, w0, w1, w2, w3, own_out, other_out, slices):
    low = iota((up.shape[0], HD), 1) < 64
    for c in range(12):
        u = up[:, head(c // 2)].astype(F32)
        d = down[:, head(c // 2)].astype(F32)
        if c % 2:
            u = pltpu.roll(u, 64, 1)
        else:
            d = pltpu.roll(d, 64, 1)
        slices[c // 3, :, head(c % 3)] = jnp.where(low, u, d).astype(BF16)
    for k, w in enumerate((w0, w1, w2, w3)):
        w[...] = slices[(ids[XL] * 2 + ids[C]) ^ k]
    lane = iota((HD, HD), 1)
    sub = iota((HD, HD), 0)
    table = jnp.zeros((HD, HD), F32)
    for e in range(2):
        hit = jnp.where(sub == routes[e : e + 1, :], gates[e : e + 1, :], 0.0)
        table = jnp.where(lane == e, jnp.sum(hit, axis=1, keepdims=True), table)
    pick_f = (iota((HD, 32), 0) == mask[...]).astype(F32)
    gm = tn(pick_f, table, precision=HIGH)
    cotf = cot[...].astype(F32)
    first, second = (gm[:, 0:1] * cotf).astype(BF16), (gm[:, 1:2] * cotf).astype(BF16)
    swap = ids[E] == 1
    own_out[...] = jnp.where(swap, second, first)
    other_out[...] = jnp.where(swap, first, second)


def weight_grads_body(scale, g, up, down):
    low = iota((up.shape[0], HD), 1) < 64
    for b in range(6):
        first, second = 2 * b, 2 * b + 1
        x = g[first // 3, :, head(first % 3)] * scale
        y = g[second // 3, :, head(second % 3)] * scale
        up[:, head(b)] = jnp.where(low, x, pltpu.roll(y, 64, 1))
        down[:, head(b)] = jnp.where(low, pltpu.roll(x, 64, 1), y)


def states_body(ld, key, value, mask, out, cum_out, cum_t_out):
    rows, cols = iota((HD, HD), 0), iota((HD, HD), 1)
    ldv = ld[...]
    cum = nn(ldv, (rows <= cols).astype(F32), precision=HIGH)
    cum_t = nt((cols <= rows).astype(F32), ldv, precision=HIGH)
    cum_out[...] = cum
    cum_t_out[...] = cum_t
    falling = jnp.exp(cum_t[HD - 1 : HD, :] - cum_t)
    rising = jnp.exp(cum_t)
    for h in range(HEADS):
        k = key[:, head(h)].astype(F32)
        kf = (k * falling[:, h : h + 1]).astype(BF16)
        kb = (k * rising[:, h : h + 1]).astype(BF16)
        v = value[:, head(h)]
        g, at = h // 2, (h % 2) * HD
        out[g, at : at + HD, :] = tn(kf, v).astype(BF16)
        out[g, 256 + at : 256 + at + HD, :] = tn(kb, v).astype(BF16)
    repeat = (iota((32, HD), 0) == iota((32, HD), 1) % 32).astype(BF16)
    places = nn(mask[...].astype(F32).astype(BF16), repeat).astype(jnp.int32)
    places = jnp.where(iota((1, HD), 1) < 96, places, HD - 1)
    chosen = nn(cum, (rows == places).astype(F32), precision=HIGH)
    hi = chosen.astype(BF16).astype(F32)
    mid = (chosen - hi).astype(BF16).astype(F32)
    low = (chosen - hi - mid).astype(BF16).astype(F32)
    lane = iota((HEADS, HD), 1)
    first = (lane < 32) | (lane == 96)
    second = ((lane >= 32) & (lane < 64)) | (lane == 97)
    third = ((lane >= 64) & (lane < 96)) | (lane == 98)
    packed = jnp.where(first, hi, jnp.where(second, mid, jnp.where(third, low, 0.0))).astype(BF16)
    for g in range(8):
        out[g, 512:528, :] = packed


def masked_body(query, key, value, residual, mask, cum, cum_t, qm_out, rm_out, inner_out, cm_out):
    pick_t = (iota((HD, 32), 0) == mask[...]).astype(BF16)
    qm = tn(pick_t, query[...]).astype(BF16)
    qm_out[...] = qm
    rm_out[...] = tn(pick_t, residual[...])
    cm = tn(pick_t.astype(F32), cum_t[...], precision=HIGH)
    cm_out[...] = cm
    cumv = cum[...]
    for h in range(HEADS):
        s = nt(qm[:, head(h)], key[:, head(h)])
        p = (s * jnp.exp(-jnp.abs(cm[:, h : h + 1] - cumv[h : h + 1, :]))).astype(BF16)
        inner_out[:, head(h)] = nn(p, value[:, head(h)])


def carry_body(ids, parts, out):
    row, lane = iota((HEADS, HD), 0), iota((HEADS, HD), 1)
    ends = (lane >= 96) & (lane < 99)
    n = parts.shape[0]
    for j in range(2):
        at = slice(j * HD, (j + 1) * HD)
        back = slice(256 + j * HD, 256 + (j + 1) * HD)
        wanted = ends & (row == 2 * (2 * ids[Y] + ids[XL]) + j)
        decay = [
            jnp.exp(jnp.sum(jnp.where(wanted, parts[a, 512:528, :].astype(F32), 0.0), keepdims=True))
            for a in range(n)
        ]
        run = jnp.zeros((HD, HD), F32)
        for a in range(n):
            out[a, at, :] = run.astype(BF16)
            run = decay[a] * run + parts[a, at, :].astype(F32)
        run = jnp.zeros((HD, HD), F32)
        for a in reversed(range(n)):
            out[a, back, :] = run.astype(BF16)
            run = decay[a] * run + parts[a, back, :].astype(F32)


def states_of(carried, h):
    at = (h % 2) * HD
    return carried[h // 2, at : at + HD, :], carried[h // 2, 256 + at : 256 + at + HD, :]


def rows_body(qm, rm, inner, cm, cum_t, carried, routed_out, normed_out, normalized_out, stats_out):
    cmv = cm[...]
    rising = jnp.exp(cmv)
    falling = jnp.exp(cum_t[HD - 1 : HD, :] - cmv)
    lane = iota((32, HD), 1)
    stats = jnp.zeros((32, HD), F32)
    total = jnp.zeros((32, HD), F32)
    residuals = []
    for h in range(HEADS):
        fwd, bwd = states_of(carried, h)
        q = qm[:, head(h)]
        attn = inner[:, head(h)] + rising[:, h : h + 1] * nn(q, fwd) + falling[:, h : h + 1] * nn(q, bwd)
        scale = lax.rsqrt(jnp.mean(attn * attn, axis=-1, keepdims=True) + EPS)
        normed = attn * scale
        normed_out[:, head(h)] = normed
        stats = jnp.where(lane == h, scale, stats)
        r = (rm[:, head(h)] + normed).astype(BF16).astype(F32)
        total = total + r * r
        residuals.append(r)
    row_scale = lax.rsqrt(jnp.sum(total, axis=-1, keepdims=True) * (1.0 / (HEADS * HD)) + EPS)
    stats_out[...] = jnp.where(lane == HEADS, row_scale, stats)
    for h in range(HEADS):
        normalized = residuals[h] * row_scale
        normalized_out[:, head(h)] = normalized
        routed_out[:, head(h)] = normalized.astype(BF16)


def expert_body(ids, *refs):
    rows, grads, pieces, (z_own, z_other), sums, (w_ref, r_ref, g_ref) = (
        refs[:8], refs[8:16], refs[16:20], refs[20:22], refs[22:26], refs[26:],
    )
    nz, unit = pieces[0].shape[0], pieces[0].shape[2]
    for k, piece in enumerate(pieces):
        y = (ids[Y] + 4 - k) % 4
        for zs in range(nz):
            z = ids[Z] ^ sum(nz >> (i + 1) for i in range(3) if zs >> i & 1)
            for cs in range(4):
                x = ids[XL] ^ (cs // 2)
                at = (((y * 2 + x) * nz + z) * 2 + (ids[C] ^ (cs % 2))) * unit
                w_ref[pl.ds(pl.multiple_of(at, unit), unit), :] = piece[zs, cs]
    for k in range(8):
        r_ref[k] = rows[k][...]
        g_ref[k] = grads[k][...]
    width = HEADS * HD
    r = r_ref[...].reshape(256, width)
    g = g_ref[...].reshape(256, width)
    w = w_ref[...]
    pre_all = nn(r, w)
    grad_all = nn(g, w)
    low = iota((256, HD), 1) < 64
    pgs, acts = [], []
    for b in range(3):
        pre = pre_all[:, head(b)]
        act_grad = pltpu.roll(grad_all[:, head(b)], 64, 1)
        sig = jax.nn.sigmoid(pre)
        act = pltpu.roll(pre * sig, 64, 1)
        pre_grad = act_grad * sig * (1.0 + pre * (1.0 - sig))
        pgs.append(jnp.where(low, pre_grad, 0.0).astype(BF16))
        acts.append(jnp.where(low, 0.0, act).astype(BF16))
    pg = jnp.concatenate(pgs, axis=1)
    ac = jnp.concatenate(acts, axis=1)
    z_own[...] = nt(pg[:128], w).astype(BF16).reshape(z_own.shape)
    z_other[...] = nt(pg[128:], w).astype(BF16).reshape(z_other.shape)
    both = jnp.concatenate((pg, ac), axis=0)
    for k, out in enumerate(sums):
        y = (ids[Y] + k) % 4
        cols = pl.ds(pl.multiple_of(y * 512, 512), 512)
        sides = jnp.concatenate((r_ref[:, :, cols].reshape(256, 512), g_ref[:, :, cols].reshape(256, 512)), axis=0)
        out[...] = tn(sides, both).astype(BF16)


def fold_body(kept, came, *outs):
    for k, out in enumerate(outs):
        out[...] = (kept[k].astype(F32) + came[k].astype(F32)).astype(BF16)


def sum_y_body(p0, p1, p2, p3, out):
    nz, nx, unit = out.shape[:3]
    for x in range(nx):
        for z in range(nz):
            at = slice((x * nz + z) * unit, (x * nz + z + 1) * unit)
            total = p0[at, :].astype(F32) + p1[at, :].astype(F32) + p2[at, :].astype(F32) + p3[at, :].astype(F32)
            out[z, x] = total.astype(BF16)


def sum_z_body(parts, out):
    total = parts[0].astype(F32)
    for z in range(1, parts.shape[0]):
        total = total + parts[z].astype(F32)
    out[...] = total


def grads_body(z0, z1, z2, z3, cot, normed, normalized, stats, out):
    z = (z0[...].astype(F32) + z1[...].astype(F32)) + (z2[...].astype(F32) + z3[...].astype(F32))
    norm = normalized[...]
    st = stats[...]
    mean = jnp.sum(z * norm, axis=-1, keepdims=True) * (1.0 / (HEADS * HD))
    rg = cot[...].astype(F32) + st[:, HEADS : HEADS + 1] * (z - norm * mean)
    for h in range(HEADS):
        n = normed[:, head(h)]
        g = rg[:, head(h)]
        m = jnp.mean(g * n, axis=-1, keepdims=True)
        out[:, head(h)] = (st[:, h : h + 1] * (g - n * m)).astype(BF16)


def query_grad_body(da_own, key, value, mask, cm, cum, cum_t, carried, out, q_ref):
    da = da_own[...]
    pick_t = (iota((HD, 32), 0) == mask[...]).astype(BF16)
    cmv = cm[...]
    cumv = cum[...]
    rising = jnp.exp(cmv)
    falling = jnp.exp(cum_t[HD - 1 : HD, :] - cmv)
    for h in range(HEADS):
        fwd, bwd = states_of(carried, h)
        a = da[:, head(h)]
        s = nt(a, value[:, head(h)])
        p = (s * jnp.exp(-jnp.abs(cmv[:, h : h + 1] - cumv[h : h + 1, :]))).astype(BF16)
        q = nn(p, key[:, head(h)]) + rising[:, h : h + 1] * nt(a, fwd) + falling[:, h : h + 1] * nt(a, bwd)
        q_ref[:, head(h)] = q.astype(BF16)
    out[...] = nn(pick_t, q_ref[...]).astype(BF16)


def rows_of(pieces, h):
    return jnp.concatenate([p[:, head(h)] for p in pieces], axis=0)


def scores_body(ids, parts, key, cum_t, *refs):
    queries, (decay_out, scores_out) = refs[:8], refs[8:]
    n = parts.shape[0]
    lane, col = iota((HD, n * 32), 0), iota((HD, n * 32), 1)
    me = 2 * ids[Y] + ids[XL]
    block = jnp.zeros((HD, n * 32), jnp.int32)
    for k in range(n):
        there = 2 * ((ids[Y] + 4 - k // 2) % 4) + (ids[XL] ^ (k % 2))
        block = jnp.where(col // 32 == k, there, block)
    at = jnp.zeros((HEADS, n * 32), F32)
    for a in range(n):
        own = (lane < 96) & (lane % 32 == col % 32) & (block == a)
        ends = (lane >= 96) & (lane < 99)
        after = ends & (block > a) & (a >= me)
        before = ends & (block <= a) & (a < me)
        take = jnp.where(own | after, 1.0, jnp.where(before, -1.0, 0.0)).astype(BF16)
        at = at + nn(parts[a, 512:528, :], take)
    ct = cum_t[...]
    for h in range(HEADS):
        decay = jnp.exp(-jnp.abs(ct[:, h : h + 1] - at[h : h + 1, :]))
        decay_out[h] = decay
        scores_out[h] = (nt(key[:, head(h)], rows_of(queries, h)) * decay).astype(BF16)


def key_value_grads_body(value, decay, scores, *refs):
    das, queries, (key_out, value_out) = refs[:8], refs[8:16], refs[16:]
    for h in range(HEADS):
        da = rows_of(das, h)
        value_out[:, head(h)] = nn(scores[h], da).astype(BF16)
        p = (nt(value[:, head(h)], da) * decay[h]).astype(BF16)
        key_out[:, head(h)] = nn(p, rows_of(queries, h)).astype(BF16)


def trade(x, axis, bit=1):
    n = lax.axis_size(axis)
    return lax.ppermute(x, axis, [(i, i ^ bit) for i in range(n)])


def turn(x, k):
    n = lax.axis_size("y")
    return lax.ppermute(x, "y", [(i, (i + k) % n) for i in range(n)])


def after(first, then):
    return lax.optimization_barrier((first, then))


def along_y(x):
    return [x] + [turn(x, k) for k in range(1, 4)]


def along_sequence(x, other):
    return [p for pair in zip(along_y(x), along_y(other)) for p in pair]


def across(pieces):
    return [pieces[0]] + [
        lax.ppermute(pieces[k], ("xl", "e"), [(i, i ^ k) for i in range(4)]) for k in range(1, 4)
    ]


def local(residual, query, key, value, ld, cot, mask, routes, gates, up, down):
    residual, query, key, value, ld = residual[0], query[0], key[0], value[0], ld[0]
    cot, mask, routes, gates, up, down = cot[0, 0], mask[0], routes[0, 0], gates[0, 0], up[0], down[0]
    width = HEADS * HD
    ny, nx, nz, nc = (lax.axis_size(a) for a in ("y", "xl", "z", "c"))
    shard = up.shape[0]
    ids = jnp.stack([lax.axis_index(a) for a in ("y", "xl", "z", "c", "e")]).astype(jnp.int32)

    prepared = call(
        prepare_body,
        [((shard, 384), BF16)] * 4 + [((32, width), BF16)] * 2,
        ids, up, down, cot, mask, routes, gates,
        scalar=True,
        scratch=[pltpu.VMEM((4, shard, 384), BF16)],
    )
    prepared, ld = after(prepared, ld)
    w = [prepared[0]] + [
        lax.ppermute(prepared[k], ("xl", "c"), [(i, i ^ k) for i in range(4)]) for k in range(1, 4)
    ]
    mine, other = prepared[4:]
    grads = across((mine, other, mine, other))
    states, cum, cum_t = call(
        states_body,
        [((8, 528, HD), BF16), ((HEADS, HD), F32), ((HD, HEADS), F32)],
        ld, key, value, mask,
    )
    parts = exchange(states, SEQ)
    qm, rm, inner, cm = call(
        masked_body,
        [((32, width), BF16), ((32, width), F32), ((32, width), F32), ((32, HEADS), F32)],
        query, key, value, residual, mask, cum, cum_t,
    )
    w = jnp.stack(w)[None]
    (w, qm), parts = after((w, qm), parts)
    [carries] = call(carry_body, [((8, 512, HD), BF16)], ids, parts, scalar=True)
    carried = exchange(carries, SEQ)
    bit = nz // 2
    while bit:
        w = jnp.concatenate((w, trade(w, "z", bit)))
        bit //= 2
    (w, grads), carried = after((w, grads), carried)
    routed, normed, normalized, stats = call(
        rows_body,
        [((32, width), BF16), ((32, width), F32), ((32, width), F32), ((32, HD), F32)],
        qm, rm, inner, cm, cum_t, carried,
    )
    weights = along_y(w)
    grads = grads + [trade(g, "c") for g in grads]
    rows = across([routed] * 4)
    rows = rows + [trade(r, "c") for r in rows]
    qx = trade(qm, "xl")
    weights, (qm, qx) = after(weights, (qm, qx))
    z_kept, z_send, *dw = call(
        expert_body,
        [((4, 32, width), BF16)] * 2 + [((width // ny, 384), BF16)] * 4,
        ids, *rows, *grads, *weights,
        scalar=True,
        scratch=[pltpu.VMEM((width, 384), BF16)] + [pltpu.VMEM((8, 32, width), BF16)] * 2,
        flops=2 * 10**9,
    )
    queries = along_sequence(qm, qx)
    folded = call(fold_body, [((32, width), BF16)] * 4, z_kept, trade(z_send, "c"))
    z_parts = across(folded)
    d1 = [dw[0]] + [turn(dw[k], k) for k in range(1, 4)]
    decay, scores = call(
        scores_body,
        [((HEADS, HD, 256), F32), ((HEADS, HD, 256), BF16)],
        ids, parts, key, cum_t, *queries,
        scalar=True,
    )
    scores, z_parts = after(scores, z_parts)
    [da] = call(grads_body, [((32, width), BF16)], *z_parts, cot, normed, normalized, stats)
    d1, da = after(d1, da)
    dx = trade(da, "xl")
    [d2] = call(sum_y_body, [((nz, nx, nc * shard, 384), BF16)], *d1)
    dx, d2 = after(dx, d2)
    das = along_sequence(da, dx)
    d3 = exchange(d2, "z")
    [query_grad] = call(
        query_grad_body, [((HD, width), BF16)], da, key, value, mask, cm, cum, cum_t, carried,
        scratch=[pltpu.VMEM((32, width), BF16)],
    )
    query_grad, d3 = after(query_grad, d3)
    [d4] = call(sum_z_body, [((nx, nc * shard, 384), F32)], d3)
    d5 = exchange(d4.reshape(4, shard, 384), ("xl", "c"))
    key_grad, value_grad = call(
        key_value_grads_body,
        [((HD, width), BF16), ((HD, width), BF16)],
        value, decay, scores, *das, *queries,
    )
    scale = 1.0 / (ny * nx * nz * nc)

    def finish(g, a, b):
        weight_grads_body(scale, g, a, b)

    up_grad, down_grad = call(finish, [((shard, 768), F32), ((shard, 768), F32)], d5)
    return query_grad[None], key_grad[None], value_grad[None], up_grad[None], down_grad[None]


def solution(mesh):
    shape = mesh.shape
    grid = mesh.devices.reshape(shape["seq"] // 2, 2, shape["rep"] // 2, 2, shape["exp"])
    fine = Mesh(grid, ("y", "xl", "z", "c", "e"))
    sequences, data = ("z", "c", "e"), ("y", "xl", "z", "c")
    in_specs = (
        P(sequences, SEQ, None),
        P(sequences, SEQ, None),
        P(sequences, SEQ, None),
        P(sequences, SEQ, None),
        P(sequences, None, SEQ),
        P(sequences, SEQ, None, None),
        P(sequences, SEQ, None),
        P(sequences, SEQ, None, None),
        P(sequences, SEQ, None, None),
        P("e", data, None),
        P("e", data, None),
    )
    out_specs = (
        P(sequences, SEQ, None),
        P(sequences, SEQ, None),
        P(sequences, SEQ, None),
        P("e", data, None),
        P("e", data, None),
    )
    return jax.shard_map(local, mesh=fine, in_specs=in_specs, out_specs=out_specs, check_vma=False)
```

```python
import jax
import jax.numpy as jnp
from jax import lax
from jax.experimental import pallas as pl
from jax.experimental.pallas import tpu as pltpu
from jax.sharding import Mesh, PartitionSpec as P

HEADS = 16
HD = 128
EPS = 1e-05
SEQ = ("y", "xl")
VM = 24
Y, XL, Z, C, E = range(5)
F32 = jnp.float32
BF16 = jnp.bfloat16
HIGH = lax.Precision.HIGHEST


def call(body, outs, *args, flops=10**8, scalar=False, scratch=(), vmem=56):
    shapes = [jax.ShapeDtypeStruct(s, d) for s, d in outs]
    moved = sum(a.size * a.dtype.itemsize for a in (*args, *shapes))
    in_specs = [pl.BlockSpec()] * len(args)
    if scalar:
        in_specs[0] = pl.BlockSpec(memory_space=pltpu.SMEM)
    result = pl.pallas_call(
        body,
        out_shape=shapes,
        in_specs=in_specs,
        scratch_shapes=list(scratch),
        compiler_params=pltpu.CompilerParams(vmem_limit_bytes=vmem << 20),
        cost_estimate=pl.CostEstimate(flops=flops, bytes_accessed=moved, transcendentals=0),
    )(*args)
    return result


def iota(shape, dim):
    return lax.broadcasted_iota(jnp.int32, shape, dim)


def tn(a, b, **kw):
    return lax.dot_general(a, b, (((0,), (0,)), ((), ())), preferred_element_type=F32, **kw)


def nt(a, b, **kw):
    return lax.dot_general(a, b, (((1,), (1,)), ((), ())), preferred_element_type=F32, **kw)


def nn(a, b, **kw):
    return lax.dot_general(a, b, (((1,), (0,)), ((), ())), preferred_element_type=F32, **kw)


def head(h):
    return slice(h * HD, (h + 1) * HD)


def exchange(x, axes):
    return lax.all_to_all(x, axes, split_axis=0, concat_axis=0, tiled=True)


def prepare_body(ids, up, down, cot, mask, routes, gates, w0, w1, w2, w3, own_out, other_out, slices):
    low = iota((up.shape[0], HD), 1) < 64
    for c in range(12):
        u = up[:, head(c // 2)].astype(F32)
        d = down[:, head(c // 2)].astype(F32)
        if c % 2:
            u = pltpu.roll(u, 64, 1)
        else:
            d = pltpu.roll(d, 64, 1)
        slices[c // 3, :, head(c % 3)] = jnp.where(low, u, d).astype(BF16)
    for k, w in enumerate((w0, w1, w2, w3)):
        w[...] = slices[(ids[XL] * 2 + ids[C]) ^ k]
    lane = iota((HD, HD), 1)
    sub = iota((HD, HD), 0)
    table = jnp.zeros((HD, HD), F32)
    for e in range(2):
        hit = jnp.where(sub == routes[e : e + 1, :], gates[e : e + 1, :], 0.0)
        table = jnp.where(lane == e, jnp.sum(hit, axis=1, keepdims=True), table)
    pick_f = (iota((HD, 32), 0) == mask[...]).astype(F32)
    gm = tn(pick_f, table, precision=HIGH)
    cotf = cot[...].astype(F32)
    first, second = (gm[:, 0:1] * cotf).astype(BF16), (gm[:, 1:2] * cotf).astype(BF16)
    swap = ids[E] == 1
    own_out[...] = jnp.where(swap, second, first)
    other_out[...] = jnp.where(swap, first, second)


def weight_grads_body(scale, ids, p0, p1, p2, p3, up, down, g):
    for k, piece in enumerate((p0, p1, p2, p3)):
        g[(ids[XL] * 2 + ids[C]) ^ k] = piece[...]
    low = iota((up.shape[0], HD), 1) < 64
    for b in range(6):
        first, second = 2 * b, 2 * b + 1
        x = g[first // 3, :, head(first % 3)] * scale
        y = g[second // 3, :, head(second % 3)] * scale
        up[:, head(b)] = jnp.where(low, x, pltpu.roll(y, 64, 1))
        down[:, head(b)] = jnp.where(low, pltpu.roll(x, 64, 1), y)


def states_body(ld, key, value, mask, out, cum_out, cum_t_out):
    rows, cols = iota((HD, HD), 0), iota((HD, HD), 1)
    ldv = ld[...]
    cum = nn(ldv, (rows <= cols).astype(F32), precision=HIGH)
    cum_t = nt((cols <= rows).astype(F32), ldv, precision=HIGH)
    cum_out[...] = cum
    cum_t_out[...] = cum_t
    falling = jnp.exp(cum_t[HD - 1 : HD, :] - cum_t)
    rising = jnp.exp(cum_t)
    for h in range(HEADS):
        k = key[:, head(h)].astype(F32)
        kf = (k * falling[:, h : h + 1]).astype(BF16)
        kb = (k * rising[:, h : h + 1]).astype(BF16)
        v = value[:, head(h)]
        g, at = h // 2, (h % 2) * HD
        out[g, at : at + HD, :] = tn(kf, v).astype(BF16)
        out[g, 256 + at : 256 + at + HD, :] = tn(kb, v).astype(BF16)
    repeat = (iota((32, HD), 0) == iota((32, HD), 1) % 32).astype(BF16)
    places = nn(mask[...].astype(F32).astype(BF16), repeat).astype(jnp.int32)
    places = jnp.where(iota((1, HD), 1) < 96, places, HD - 1)
    chosen = nn(cum, (rows == places).astype(F32), precision=HIGH)
    hi = chosen.astype(BF16).astype(F32)
    mid = (chosen - hi).astype(BF16).astype(F32)
    low = (chosen - hi - mid).astype(BF16).astype(F32)
    lane = iota((HEADS, HD), 1)
    first = (lane < 32) | (lane == 96)
    second = ((lane >= 32) & (lane < 64)) | (lane == 97)
    third = ((lane >= 64) & (lane < 96)) | (lane == 98)
    packed = jnp.where(first, hi, jnp.where(second, mid, jnp.where(third, low, 0.0))).astype(BF16)
    for g in range(8):
        out[g, 512:528, :] = packed


def masked_body(query, key, value, residual, mask, cum, cum_t, qm_out, rm_out, inner_out, cm_out):
    pick_t = (iota((HD, 32), 0) == mask[...]).astype(BF16)
    qm = tn(pick_t, query[...]).astype(BF16)
    qm_out[...] = qm
    rm_out[...] = tn(pick_t, residual[...])
    cm = tn(pick_t.astype(F32), cum_t[...], precision=HIGH)
    cm_out[...] = cm
    cumv = cum[...]
    for h in range(HEADS):
        s = nt(qm[:, head(h)], key[:, head(h)])
        p = (s * jnp.exp(-jnp.abs(cm[:, h : h + 1] - cumv[h : h + 1, :]))).astype(BF16)
        inner_out[:, head(h)] = nn(p, value[:, head(h)])


def carry_body(ids, parts, out):
    row, lane = iota((HEADS, HD), 0), iota((HEADS, HD), 1)
    ends = (lane >= 96) & (lane < 99)
    n = parts.shape[0]
    for j in range(2):
        at = slice(j * HD, (j + 1) * HD)
        back = slice(256 + j * HD, 256 + (j + 1) * HD)
        wanted = ends & (row == 2 * (2 * ids[Y] + ids[XL]) + j)
        decay = [
            jnp.exp(jnp.sum(jnp.where(wanted, parts[a, 512:528, :].astype(F32), 0.0), keepdims=True))
            for a in range(n)
        ]
        run = jnp.zeros((HD, HD), F32)
        for a in range(n):
            out[a, at, :] = run.astype(BF16)
            run = decay[a] * run + parts[a, at, :].astype(F32)
        run = jnp.zeros((HD, HD), F32)
        for a in reversed(range(n)):
            out[a, back, :] = run.astype(BF16)
            run = decay[a] * run + parts[a, back, :].astype(F32)


def states_of(carried, h):
    at = (h % 2) * HD
    return carried[h // 2, at : at + HD, :], carried[h // 2, 256 + at : 256 + at + HD, :]


def rows_body(qm, rm, inner, cm, cum_t, carried, routed_out, normed_out, normalized_out, stats_out):
    cmv = cm[...]
    rising = jnp.exp(cmv)
    falling = jnp.exp(cum_t[HD - 1 : HD, :] - cmv)
    lane = iota((32, HD), 1)
    stats = jnp.zeros((32, HD), F32)
    total = jnp.zeros((32, HD), F32)
    residuals = []
    for h in range(HEADS):
        fwd, bwd = states_of(carried, h)
        q = qm[:, head(h)]
        attn = inner[:, head(h)] + rising[:, h : h + 1] * nn(q, fwd) + falling[:, h : h + 1] * nn(q, bwd)
        scale = lax.rsqrt(jnp.mean(attn * attn, axis=-1, keepdims=True) + EPS)
        normed = attn * scale
        normed_out[:, head(h)] = normed
        stats = jnp.where(lane == h, scale, stats)
        r = (rm[:, head(h)] + normed).astype(BF16).astype(F32)
        total = total + r * r
        residuals.append(r)
    row_scale = lax.rsqrt(jnp.sum(total, axis=-1, keepdims=True) * (1.0 / (HEADS * HD)) + EPS)
    stats_out[...] = jnp.where(lane == HEADS, row_scale, stats)
    for h in range(HEADS):
        normalized = residuals[h] * row_scale
        normalized_out[:, head(h)] = normalized
        routed_out[:, head(h)] = normalized.astype(BF16)


def expert_body(ids, *refs):
    rows, grads, pieces, (z_own, z_other), sums, (w_ref, r_ref, g_ref) = (
        refs[:8], refs[8:16], refs[16:20], refs[20:22], refs[22:26], refs[26:],
    )
    nz, unit = pieces[0].shape[0], pieces[0].shape[2]
    for k, piece in enumerate(pieces):
        y = (ids[Y] + 4 - k) % 4
        for zs in range(nz):
            z = ids[Z] ^ sum(nz >> (i + 1) for i in range(3) if zs >> i & 1)
            for cs in range(4):
                x = ids[XL] ^ (cs // 2)
                at = (((y * 2 + x) * nz + z) * 2 + (ids[C] ^ (cs % 2))) * unit
                w_ref[pl.ds(pl.multiple_of(at, unit), unit), :] = piece[zs, cs]
    for k in range(8):
        r_ref[k] = rows[k][...]
        g_ref[k] = grads[k][...]
    width = HEADS * HD
    r = r_ref[...].reshape(256, width)
    g = g_ref[...].reshape(256, width)
    w = w_ref[...]
    pre_all = nn(r, w)
    grad_all = nn(g, w)
    low = iota((256, HD), 1) < 64
    pgs, acts = [], []
    for b in range(3):
        pre = pre_all[:, head(b)]
        act_grad = pltpu.roll(grad_all[:, head(b)], 64, 1)
        sig = jax.nn.sigmoid(pre)
        act = pltpu.roll(pre * sig, 64, 1)
        pre_grad = act_grad * sig * (1.0 + pre * (1.0 - sig))
        pgs.append(jnp.where(low, pre_grad, 0.0).astype(BF16))
        acts.append(jnp.where(low, 0.0, act).astype(BF16))
    pg = jnp.concatenate(pgs, axis=1)
    ac = jnp.concatenate(acts, axis=1)
    z_own[...] = nt(pg[:128], w).astype(BF16).reshape(z_own.shape)
    z_other[...] = nt(pg[128:], w).astype(BF16).reshape(z_other.shape)
    both = jnp.concatenate((pg, ac), axis=0)
    for k, out in enumerate(sums):
        y = (ids[Y] + k) % 4
        cols = pl.ds(pl.multiple_of(y * 512, 512), 512)
        sides = jnp.concatenate((r_ref[:, :, cols].reshape(256, 512), g_ref[:, :, cols].reshape(256, 512)), axis=0)
        out[...] = tn(sides, both).astype(BF16)


def fold_body(kept, came, *outs):
    for k, out in enumerate(outs):
        out[...] = (kept[k].astype(F32) + came[k].astype(F32)).astype(BF16)


def sum_y_body(p0, p1, p2, p3, out):
    nz, nx, unit = out.shape[:3]
    for x in range(nx):
        for z in range(nz):
            at = slice((x * nz + z) * unit, (x * nz + z + 1) * unit)
            total = p0[at, :].astype(F32) + p1[at, :].astype(F32) + p2[at, :].astype(F32) + p3[at, :].astype(F32)
            out[z, x] = total.astype(BF16)


def sum_z_body(ids, parts, o0, o1, o2, o3, total_ref):
    shard = o0.shape[0]
    total = parts[0].astype(F32)
    for z in range(1, parts.shape[0]):
        total = total + parts[z].astype(F32)
    for j in range(4):
        total_ref[j] = total[j // 2, (j % 2) * shard : (j % 2 + 1) * shard]
    for k, out in enumerate((o0, o1, o2, o3)):
        out[...] = total_ref[(ids[XL] * 2 + ids[C]) ^ k]


def grads_body(z0, z1, z2, z3, cot, normed, normalized, stats, out):
    z = (z0[...].astype(F32) + z1[...].astype(F32)) + (z2[...].astype(F32) + z3[...].astype(F32))
    norm = normalized[...]
    st = stats[...]
    mean = jnp.sum(z * norm, axis=-1, keepdims=True) * (1.0 / (HEADS * HD))
    rg = cot[...].astype(F32) + st[:, HEADS : HEADS + 1] * (z - norm * mean)
    for h in range(HEADS):
        n = normed[:, head(h)]
        g = rg[:, head(h)]
        m = jnp.mean(g * n, axis=-1, keepdims=True)
        out[:, head(h)] = (st[:, h : h + 1] * (g - n * m)).astype(BF16)


def query_grad_body(da_own, key, value, mask, cm, cum, cum_t, carried, out, q_ref):
    da = da_own[...]
    pick_t = (iota((HD, 32), 0) == mask[...]).astype(BF16)
    cmv = cm[...]
    cumv = cum[...]
    rising = jnp.exp(cmv)
    falling = jnp.exp(cum_t[HD - 1 : HD, :] - cmv)
    for h in range(HEADS):
        fwd, bwd = states_of(carried, h)
        a = da[:, head(h)]
        s = nt(a, value[:, head(h)])
        p = (s * jnp.exp(-jnp.abs(cmv[:, h : h + 1] - cumv[h : h + 1, :]))).astype(BF16)
        q = nn(p, key[:, head(h)]) + rising[:, h : h + 1] * nt(a, fwd) + falling[:, h : h + 1] * nt(a, bwd)
        q_ref[:, head(h)] = q.astype(BF16)
    out[...] = nn(pick_t, q_ref[...]).astype(BF16)


def rows_of(pieces, h):
    return jnp.concatenate([p[:, head(h)] for p in pieces], axis=0)


def place_of(ids, k):
    return 2 * ((ids[Y] + 4 - k // 2) % 4) + (ids[XL] ^ (k % 2))


def ordered(ids, gathered, h):
    starts = [pl.multiple_of(32 * place_of(ids, k), 32) for k in range(8)]
    return jnp.concatenate([gathered[pl.ds(at, 32), head(h)] for at in starts], axis=0)


def scores_body(ids, parts, key, cum_t, queries, decay_out, scores_out):
    n = parts.shape[0]
    lane, col = iota((HD, n * 32), 0), iota((HD, n * 32), 1)
    me = 2 * ids[Y] + ids[XL]
    block = jnp.zeros((HD, n * 32), jnp.int32)
    for k in range(n):
        block = jnp.where(col // 32 == k, place_of(ids, k), block)
    at = jnp.zeros((HEADS, n * 32), F32)
    for a in range(n):
        own = (lane < 96) & (lane % 32 == col % 32) & (block == a)
        ends = (lane >= 96) & (lane < 99)
        after = ends & (block > a) & (a >= me)
        before = ends & (block <= a) & (a < me)
        take = jnp.where(own | after, 1.0, jnp.where(before, -1.0, 0.0)).astype(BF16)
        at = at + nn(parts[a, 512:528, :], take)
    ct = cum_t[...]
    for h in range(HEADS):
        decay = jnp.exp(-jnp.abs(ct[:, h : h + 1] - at[h : h + 1, :]))
        decay_out[h] = decay
        scores_out[h] = (nt(key[:, head(h)], ordered(ids, queries, h)) * decay).astype(BF16)


def key_value_grads_body(ids, value, decay, scores, queries, *refs):
    das, (key_out, value_out) = refs[:8], refs[8:]
    for h in range(HEADS):
        da = rows_of(das, h)
        value_out[:, head(h)] = nn(scores[h], da).astype(BF16)
        p = (nt(value[:, head(h)], da) * decay[h]).astype(BF16)
        key_out[:, head(h)] = nn(p, ordered(ids, queries, h)).astype(BF16)


def trade(x, axis, bit=1):
    n = lax.axis_size(axis)
    return lax.ppermute(x, axis, [(i, i ^ bit) for i in range(n)])


def turn(x, k):
    n = lax.axis_size("y")
    return lax.ppermute(x, "y", [(i, (i + k) % n) for i in range(n)])


def after(first, then):
    return lax.optimization_barrier((first, then))


def along_y(x):
    return [x] + [turn(x, k) for k in range(1, 4)]


def along_sequence(x, other):
    return [p for pair in zip(along_y(x), along_y(other)) for p in pair]


def among(pieces):
    return [pieces[0]] + [
        lax.ppermute(pieces[k], ("xl", "c"), [(i, i ^ k) for i in range(4)]) for k in range(1, 4)
    ]


def across(pieces):
    return [pieces[0]] + [
        lax.ppermute(pieces[k], ("xl", "e"), [(i, i ^ k) for i in range(4)]) for k in range(1, 4)
    ]


def local(residual, query, key, value, ld, cot, mask, routes, gates, up, down):
    residual, query, key, value, ld = residual[0], query[0], key[0], value[0], ld[0]
    cot, mask, routes, gates, up, down = cot[0, 0], mask[0], routes[0, 0], gates[0, 0], up[0], down[0]
    width = HEADS * HD
    ny, nx, nz, nc = (lax.axis_size(a) for a in ("y", "xl", "z", "c"))
    shard = up.shape[0]
    ids = jnp.stack([lax.axis_index(a) for a in ("y", "xl", "z", "c", "e")]).astype(jnp.int32)

    prepared = call(
        prepare_body,
        [((shard, 384), BF16)] * 4 + [((32, width), BF16)] * 2,
        ids, up, down, cot, mask, routes, gates,
        scalar=True,
        scratch=[pltpu.VMEM((4, shard, 384), BF16)],
    )
    prepared, ld = after(prepared, ld)
    w = among(prepared[:4])
    mine, other = prepared[4:]
    grads = across((mine, other, mine, other))
    states, cum, cum_t = call(
        states_body,
        [((8, 528, HD), BF16), ((HEADS, HD), F32), ((HD, HEADS), F32)],
        ld, key, value, mask,
    )
    parts = exchange(states, SEQ)
    qm, rm, inner, cm = call(
        masked_body,
        [((32, width), BF16), ((32, width), F32), ((32, width), F32), ((32, HEADS), F32)],
        query, key, value, residual, mask, cum, cum_t,
    )
    w = jnp.stack(w)[None]
    queries = lax.all_gather(qm, SEQ, axis=0, tiled=True)
    (w, grads), parts = after((w, grads), parts)
    [carries] = call(carry_body, [((8, 512, HD), BF16)], ids, parts, scalar=True, vmem=VM)
    carried = exchange(carries, SEQ)
    bit = nz // 2
    while bit:
        w = jnp.concatenate((w, trade(w, "z", bit)))
        bit //= 2
    grads = grads + [trade(g, "c") for g in grads]
    (w, grads), carried = after((w, grads), carried)
    routed, normed, normalized, stats = call(
        rows_body,
        [((32, width), BF16), ((32, width), F32), ((32, width), F32), ((32, HD), F32)],
        qm, rm, inner, cm, cum_t, carried,
        vmem=VM,
    )
    weights = along_y(w)
    rows = across([routed] * 4)
    rows = rows + [trade(r, "c") for r in rows]
    z_kept, z_send, *dw = call(
        expert_body,
        [((4, 32, width), BF16)] * 2 + [((width // ny, 384), BF16)] * 4,
        ids, *rows, *grads, *weights,
        scalar=True,
        scratch=[pltpu.VMEM((width, 384), BF16)] + [pltpu.VMEM((8, 32, width), BF16)] * 2,
        flops=2 * 10**9,
        vmem=VM,
    )
    folded = call(fold_body, [((32, width), BF16)] * 4, z_kept, trade(z_send, "c"), vmem=VM)
    z_parts = across(folded)
    z_parts[3], dw[2] = after(z_parts[3], dw[2])
    d1 = [dw[0]] + [turn(dw[k], k) for k in range(1, 4)]
    decay, scores = call(
        scores_body,
        [((HEADS, HD, 256), F32), ((HEADS, HD, 256), BF16)],
        ids, parts, key, cum_t, queries,
        scalar=True,
    )
    scores, z_parts = after(scores, z_parts)
    [da] = call(grads_body, [((32, width), BF16)], *z_parts, cot, normed, normalized, stats, vmem=VM)
    dx = trade(da, "xl")
    d1, dx = after(d1, dx)
    [d2] = call(sum_y_body, [((nz, nx, nc * shard, 384), BF16)], *d1)
    das = along_sequence(da, dx)
    d3 = exchange(d2, "z")
    [query_grad] = call(
        query_grad_body, [((HD, width), BF16)], da, key, value, mask, cm, cum, cum_t, carried,
        scratch=[pltpu.VMEM((32, width), BF16)],
    )
    query_grad, d3 = after(query_grad, d3)
    d4 = call(
        sum_z_body,
        [((shard, 384), F32)] * 4,
        ids, d3,
        scalar=True,
        scratch=[pltpu.VMEM((4, shard, 384), F32)],
    )
    d5 = among(d4)
    key_grad, value_grad = call(
        key_value_grads_body,
        [((HD, width), BF16), ((HD, width), BF16)],
        ids, value, decay, scores, queries, *das,
        scalar=True,
        vmem=VM,
    )
    scale = 1.0 / (ny * nx * nz * nc)

    def finish(*refs):
        weight_grads_body(scale, *refs)

    up_grad, down_grad = call(
        finish,
        [((shard, 768), F32), ((shard, 768), F32)],
        ids, *d5,
        scalar=True,
        scratch=[pltpu.VMEM((4, shard, 384), F32)],
    )
    return query_grad[None], key_grad[None], value_grad[None], up_grad[None], down_grad[None]


def solution(mesh):
    shape = mesh.shape
    grid = mesh.devices.reshape(shape["seq"] // 2, 2, shape["rep"] // 2, 2, shape["exp"])
    fine = Mesh(grid, ("y", "xl", "z", "c", "e"))
    sequences, data = ("z", "c", "e"), ("y", "xl", "z", "c")
    in_specs = (
        P(sequences, SEQ, None),
        P(sequences, SEQ, None),
        P(sequences, SEQ, None),
        P(sequences, SEQ, None),
        P(sequences, None, SEQ),
        P(sequences, SEQ, None, None),
        P(sequences, SEQ, None),
        P(sequences, SEQ, None, None),
        P(sequences, SEQ, None, None),
        P("e", data, None),
        P("e", data, None),
    )
    out_specs = (
        P(sequences, SEQ, None),
        P(sequences, SEQ, None),
        P(sequences, SEQ, None),
        P("e", data, None),
        P("e", data, None),
    )
    return jax.shard_map(local, mesh=fine, in_specs=in_specs, out_specs=out_specs, check_vma=False)
```

```python
import jax
import jax.numpy as jnp
from jax import lax
from jax.experimental import pallas as pl
from jax.experimental.pallas import tpu as pltpu
from jax.sharding import Mesh, PartitionSpec as P

HEADS = 16
HD = 128
EPS = 1e-05
SEQ = ("y", "xl")
VM = 24
Y, XL, Z, C, E = range(5)
F32 = jnp.float32
BF16 = jnp.bfloat16
HIGH = lax.Precision.HIGHEST


def call(body, outs, *args, flops=10**8, scalar=False, scratch=(), vmem=56):
    shapes = [jax.ShapeDtypeStruct(s, d) for s, d in outs]
    moved = sum(a.size * a.dtype.itemsize for a in (*args, *shapes))
    in_specs = [pl.BlockSpec()] * len(args)
    if scalar:
        in_specs[0] = pl.BlockSpec(memory_space=pltpu.SMEM)
    result = pl.pallas_call(
        body,
        out_shape=shapes,
        in_specs=in_specs,
        scratch_shapes=list(scratch),
        compiler_params=pltpu.CompilerParams(vmem_limit_bytes=vmem << 20),
        cost_estimate=pl.CostEstimate(flops=flops, bytes_accessed=moved, transcendentals=0),
    )(*args)
    return result


def iota(shape, dim):
    return lax.broadcasted_iota(jnp.int32, shape, dim)


def tn(a, b, **kw):
    return lax.dot_general(a, b, (((0,), (0,)), ((), ())), preferred_element_type=F32, **kw)


def nt(a, b, **kw):
    return lax.dot_general(a, b, (((1,), (1,)), ((), ())), preferred_element_type=F32, **kw)


def nn(a, b, **kw):
    return lax.dot_general(a, b, (((1,), (0,)), ((), ())), preferred_element_type=F32, **kw)


def head(h):
    return slice(h * HD, (h + 1) * HD)


def exchange(x, axes):
    return lax.all_to_all(x, axes, split_axis=0, concat_axis=0, tiled=True)


def prepare_body(
    ids, up, down, cot, mask, routes, gates, query, w0, w1, w2, w3, own_out, other_out, qm_out, slices
):
    pick_t = (iota((HD, 32), 0) == mask[...]).astype(BF16)
    qm_out[...] = tn(pick_t, query[...]).astype(BF16)
    low = iota((up.shape[0], HD), 1) < 64
    for c in range(12):
        u = up[:, head(c // 2)].astype(F32)
        d = down[:, head(c // 2)].astype(F32)
        if c % 2:
            u = pltpu.roll(u, 64, 1)
        else:
            d = pltpu.roll(d, 64, 1)
        slices[c // 3, :, head(c % 3)] = jnp.where(low, u, d).astype(BF16)
    for k, w in enumerate((w0, w1, w2, w3)):
        w[...] = slices[(ids[XL] * 2 + ids[C]) ^ k]
    lane = iota((HD, HD), 1)
    sub = iota((HD, HD), 0)
    table = jnp.zeros((HD, HD), F32)
    for e in range(2):
        hit = jnp.where(sub == routes[e : e + 1, :], gates[e : e + 1, :], 0.0)
        table = jnp.where(lane == e, jnp.sum(hit, axis=1, keepdims=True), table)
    gm = tn(pick_t.astype(F32), table, precision=HIGH)
    cotf = cot[...].astype(F32)
    first, second = (gm[:, 0:1] * cotf).astype(BF16), (gm[:, 1:2] * cotf).astype(BF16)
    swap = ids[E] == 1
    own_out[...] = jnp.where(swap, second, first)
    other_out[...] = jnp.where(swap, first, second)


def weight_grads_body(scale, ids, p0, p1, p2, p3, up, down, g):
    for k, piece in enumerate((p0, p1, p2, p3)):
        g[(ids[XL] * 2 + ids[C]) ^ k] = piece[...]
    low = iota((up.shape[0], HD), 1) < 64
    for b in range(6):
        first, second = 2 * b, 2 * b + 1
        x = g[first // 3, :, head(first % 3)] * scale
        y = g[second // 3, :, head(second % 3)] * scale
        up[:, head(b)] = jnp.where(low, x, pltpu.roll(y, 64, 1))
        down[:, head(b)] = jnp.where(low, pltpu.roll(x, 64, 1), y)


def states_body(ld, key, value, mask, out, cum_out, cum_t_out):
    rows, cols = iota((HD, HD), 0), iota((HD, HD), 1)
    ldv = ld[...]
    cum = nn(ldv, (rows <= cols).astype(F32), precision=HIGH)
    cum_t = nt((cols <= rows).astype(F32), ldv, precision=HIGH)
    cum_out[...] = cum
    cum_t_out[...] = cum_t
    falling = jnp.exp(cum_t[HD - 1 : HD, :] - cum_t)
    rising = jnp.exp(cum_t)
    for h in range(HEADS):
        k = key[:, head(h)].astype(F32)
        kf = (k * falling[:, h : h + 1]).astype(BF16)
        kb = (k * rising[:, h : h + 1]).astype(BF16)
        v = value[:, head(h)]
        g, at = h // 2, (h % 2) * HD
        out[g, at : at + HD, :] = tn(kf, v).astype(BF16)
        out[g, 256 + at : 256 + at + HD, :] = tn(kb, v).astype(BF16)
    repeat = (iota((32, HD), 0) == iota((32, HD), 1) % 32).astype(BF16)
    places = nn(mask[...].astype(F32).astype(BF16), repeat).astype(jnp.int32)
    places = jnp.where(iota((1, HD), 1) < 96, places, HD - 1)
    chosen = nn(cum, (rows == places).astype(F32), precision=HIGH)
    hi = chosen.astype(BF16).astype(F32)
    mid = (chosen - hi).astype(BF16).astype(F32)
    low = (chosen - hi - mid).astype(BF16).astype(F32)
    lane = iota((HEADS, HD), 1)
    first = (lane < 32) | (lane == 96)
    second = ((lane >= 32) & (lane < 64)) | (lane == 97)
    third = ((lane >= 64) & (lane < 96)) | (lane == 98)
    packed = jnp.where(first, hi, jnp.where(second, mid, jnp.where(third, low, 0.0))).astype(BF16)
    for g in range(8):
        out[g, 512:528, :] = packed


def masked_body(queries, key, value, residual, mask, cum, cum_t, rm_out, inner_out, cm_out):
    pick_t = (iota((HD, 32), 0) == mask[...]).astype(BF16)
    qm = queries[...]
    rm_out[...] = tn(pick_t, residual[...])
    cm = tn(pick_t.astype(F32), cum_t[...], precision=HIGH)
    cm_out[...] = cm
    cumv = cum[...]
    for h in range(HEADS):
        s = nt(qm[:, head(h)], key[:, head(h)])
        p = (s * jnp.exp(-jnp.abs(cm[:, h : h + 1] - cumv[h : h + 1, :]))).astype(BF16)
        inner_out[:, head(h)] = nn(p, value[:, head(h)])


def carry_body(ids, parts, out):
    row, lane = iota((HEADS, HD), 0), iota((HEADS, HD), 1)
    ends = (lane >= 96) & (lane < 99)
    n = parts.shape[0]
    for j in range(2):
        at = slice(j * HD, (j + 1) * HD)
        back = slice(256 + j * HD, 256 + (j + 1) * HD)
        wanted = ends & (row == 2 * (2 * ids[Y] + ids[XL]) + j)
        decay = [
            jnp.exp(jnp.sum(jnp.where(wanted, parts[a, 512:528, :].astype(F32), 0.0), keepdims=True))
            for a in range(n)
        ]
        run = jnp.zeros((HD, HD), F32)
        for a in range(n):
            out[a, at, :] = run.astype(BF16)
            run = decay[a] * run + parts[a, at, :].astype(F32)
        run = jnp.zeros((HD, HD), F32)
        for a in reversed(range(n)):
            out[a, back, :] = run.astype(BF16)
            run = decay[a] * run + parts[a, back, :].astype(F32)


def states_of(carried, h):
    at = (h % 2) * HD
    return carried[h // 2, at : at + HD, :], carried[h // 2, 256 + at : 256 + at + HD, :]


def rows_body(qm, rm, inner, cm, cum_t, carried, routed_out, normed_out, normalized_out, stats_out):
    cmv = cm[...]
    rising = jnp.exp(cmv)
    falling = jnp.exp(cum_t[HD - 1 : HD, :] - cmv)
    lane = iota((32, HD), 1)
    stats = jnp.zeros((32, HD), F32)
    total = jnp.zeros((32, HD), F32)
    residuals = []
    for h in range(HEADS):
        fwd, bwd = states_of(carried, h)
        q = qm[:, head(h)]
        attn = inner[:, head(h)] + rising[:, h : h + 1] * nn(q, fwd) + falling[:, h : h + 1] * nn(q, bwd)
        scale = lax.rsqrt(jnp.mean(attn * attn, axis=-1, keepdims=True) + EPS)
        normed = attn * scale
        normed_out[:, head(h)] = normed
        stats = jnp.where(lane == h, scale, stats)
        r = (rm[:, head(h)] + normed).astype(BF16).astype(F32)
        total = total + r * r
        residuals.append(r)
    row_scale = lax.rsqrt(jnp.sum(total, axis=-1, keepdims=True) * (1.0 / (HEADS * HD)) + EPS)
    stats_out[...] = jnp.where(lane == HEADS, row_scale, stats)
    for h in range(HEADS):
        normalized = residuals[h] * row_scale
        normalized_out[:, head(h)] = normalized
        routed_out[:, head(h)] = normalized.astype(BF16)


def expert_body(ids, *refs):
    rows, grads, pieces, (z_own, z_other), sums, (w_ref, r_ref, g_ref) = (
        refs[:8], refs[8:16], refs[16:20], refs[20:22], refs[22:26], refs[26:],
    )
    nz, unit = pieces[0].shape[0], pieces[0].shape[2]
    for k, piece in enumerate(pieces):
        y = (ids[Y] + 4 - k) % 4
        for zs in range(nz):
            z = ids[Z] ^ sum(nz >> (i + 1) for i in range(3) if zs >> i & 1)
            for cs in range(4):
                x = ids[XL] ^ (cs // 2)
                at = (((y * 2 + x) * nz + z) * 2 + (ids[C] ^ (cs % 2))) * unit
                w_ref[pl.ds(pl.multiple_of(at, unit), unit), :] = piece[zs, cs]
    for k in range(8):
        r_ref[k] = rows[k][...]
        g_ref[k] = grads[k][...]
    width = HEADS * HD
    r = r_ref[...].reshape(256, width)
    g = g_ref[...].reshape(256, width)
    w = w_ref[...]
    pre_all = nn(r, w)
    grad_all = nn(g, w)
    low = iota((256, HD), 1) < 64
    pgs, acts = [], []
    for b in range(3):
        pre = pre_all[:, head(b)]
        act_grad = pltpu.roll(grad_all[:, head(b)], 64, 1)
        sig = jax.nn.sigmoid(pre)
        act = pltpu.roll(pre * sig, 64, 1)
        pre_grad = act_grad * sig * (1.0 + pre * (1.0 - sig))
        pgs.append(jnp.where(low, pre_grad, 0.0).astype(BF16))
        acts.append(jnp.where(low, 0.0, act).astype(BF16))
    pg = jnp.concatenate(pgs, axis=1)
    ac = jnp.concatenate(acts, axis=1)
    z_own[...] = nt(pg[:128], w).astype(BF16).reshape(z_own.shape)
    z_other[...] = nt(pg[128:], w).astype(BF16).reshape(z_other.shape)
    both = jnp.concatenate((pg, ac), axis=0)
    for k, out in enumerate(sums):
        y = (ids[Y] + k) % 4
        cols = pl.ds(pl.multiple_of(y * 512, 512), 512)
        sides = jnp.concatenate((r_ref[:, :, cols].reshape(256, 512), g_ref[:, :, cols].reshape(256, 512)), axis=0)
        out[...] = tn(sides, both).astype(BF16)


def fold_body(kept, came, *outs):
    for k, out in enumerate(outs):
        out[...] = (kept[k].astype(F32) + came[k].astype(F32)).astype(BF16)


def sum_y_body(p0, p1, p2, p3, out):
    nz, nx, unit = out.shape[:3]
    for x in range(nx):
        for z in range(nz):
            at = slice((x * nz + z) * unit, (x * nz + z + 1) * unit)
            total = p0[at, :].astype(F32) + p1[at, :].astype(F32) + p2[at, :].astype(F32) + p3[at, :].astype(F32)
            out[z, x] = total.astype(BF16)


def sum_z_body(ids, parts, o0, o1, o2, o3, total_ref):
    shard = o0.shape[0]
    total = parts[0].astype(F32)
    for z in range(1, parts.shape[0]):
        total = total + parts[z].astype(F32)
    for j in range(4):
        total_ref[j] = total[j // 2, (j % 2) * shard : (j % 2 + 1) * shard]
    for k, out in enumerate((o0, o1, o2, o3)):
        out[...] = total_ref[(ids[XL] * 2 + ids[C]) ^ k]


def grads_body(z0, z1, z2, z3, cot, normed, normalized, stats, out):
    z = (z0[...].astype(F32) + z1[...].astype(F32)) + (z2[...].astype(F32) + z3[...].astype(F32))
    norm = normalized[...]
    st = stats[...]
    mean = jnp.sum(z * norm, axis=-1, keepdims=True) * (1.0 / (HEADS * HD))
    rg = cot[...].astype(F32) + st[:, HEADS : HEADS + 1] * (z - norm * mean)
    for h in range(HEADS):
        n = normed[:, head(h)]
        g = rg[:, head(h)]
        m = jnp.mean(g * n, axis=-1, keepdims=True)
        out[:, head(h)] = (st[:, h : h + 1] * (g - n * m)).astype(BF16)


def query_grad_body(da_own, key, value, mask, cm, cum, cum_t, carried, out, q_ref):
    da = da_own[...]
    pick_t = (iota((HD, 32), 0) == mask[...]).astype(BF16)
    cmv = cm[...]
    cumv = cum[...]
    rising = jnp.exp(cmv)
    falling = jnp.exp(cum_t[HD - 1 : HD, :] - cmv)
    for h in range(HEADS):
        fwd, bwd = states_of(carried, h)
        a = da[:, head(h)]
        s = nt(a, value[:, head(h)])
        p = (s * jnp.exp(-jnp.abs(cmv[:, h : h + 1] - cumv[h : h + 1, :]))).astype(BF16)
        q = nn(p, key[:, head(h)]) + rising[:, h : h + 1] * nt(a, fwd) + falling[:, h : h + 1] * nt(a, bwd)
        q_ref[:, head(h)] = q.astype(BF16)
    out[...] = nn(pick_t, q_ref[...]).astype(BF16)


def rows_of(pieces, h):
    return jnp.concatenate([p[:, head(h)] for p in pieces], axis=0)


def place_of(ids, k):
    return 2 * ((ids[Y] + 4 - k // 2) % 4) + (ids[XL] ^ (k % 2))


def pairs_of(pieces, h):
    return jnp.concatenate([p[:, :, head(h)].reshape(64, HD) for p in pieces], axis=0)


def scores_body(ids, parts, key, cum_t, q0, q1, q2, q3, decay_out, scores_out):
    n = parts.shape[0]
    lane, col = iota((HD, n * 32), 0), iota((HD, n * 32), 1)
    me = 2 * ids[Y] + ids[XL]
    block = jnp.zeros((HD, n * 32), jnp.int32)
    for k in range(n):
        block = jnp.where(col // 32 == k, place_of(ids, k), block)
    at = jnp.zeros((HEADS, n * 32), F32)
    for a in range(n):
        own = (lane < 96) & (lane % 32 == col % 32) & (block == a)
        ends = (lane >= 96) & (lane < 99)
        after = ends & (block > a) & (a >= me)
        before = ends & (block <= a) & (a < me)
        take = jnp.where(own | after, 1.0, jnp.where(before, -1.0, 0.0)).astype(BF16)
        at = at + nn(parts[a, 512:528, :], take)
    ct = cum_t[...]
    for h in range(HEADS):
        decay = jnp.exp(-jnp.abs(ct[:, h : h + 1] - at[h : h + 1, :]))
        decay_out[h] = decay
        scores_out[h] = (nt(key[:, head(h)], pairs_of((q0, q1, q2, q3), h)) * decay).astype(BF16)


def key_value_grads_body(value, decay, scores, q0, q1, q2, q3, *refs):
    das, (key_out, value_out) = refs[:8], refs[8:]
    for h in range(HEADS):
        da = rows_of(das, h)
        value_out[:, head(h)] = nn(scores[h], da).astype(BF16)
        p = (nt(value[:, head(h)], da) * decay[h]).astype(BF16)
        key_out[:, head(h)] = nn(p, pairs_of((q0, q1, q2, q3), h)).astype(BF16)


def trade(x, axis, bit=1):
    n = lax.axis_size(axis)
    return lax.ppermute(x, axis, [(i, i ^ bit) for i in range(n)])


def turn(x, k):
    n = lax.axis_size("y")
    return lax.ppermute(x, "y", [(i, (i + k) % n) for i in range(n)])


def after(first, then):
    return lax.optimization_barrier((first, then))


def along_y(x):
    return [x] + [turn(x, k) for k in range(1, 4)]


def along_sequence(x, other):
    return [p for pair in zip(along_y(x), along_y(other)) for p in pair]


def among(pieces):
    return [pieces[0]] + [
        lax.ppermute(pieces[k], ("xl", "c"), [(i, i ^ k) for i in range(4)]) for k in range(1, 4)
    ]


def across(pieces):
    return [pieces[0]] + [
        lax.ppermute(pieces[k], ("xl", "e"), [(i, i ^ k) for i in range(4)]) for k in range(1, 4)
    ]


def local(residual, query, key, value, ld, cot, mask, routes, gates, up, down):
    residual, query, key, value, ld = residual[0], query[0], key[0], value[0], ld[0]
    cot, mask, routes, gates, up, down = cot[0, 0], mask[0], routes[0, 0], gates[0, 0], up[0], down[0]
    width = HEADS * HD
    ny, nx, nz, nc = (lax.axis_size(a) for a in ("y", "xl", "z", "c"))
    shard = up.shape[0]
    ids = jnp.stack([lax.axis_index(a) for a in ("y", "xl", "z", "c", "e")]).astype(jnp.int32)

    prepared = call(
        prepare_body,
        [((shard, 384), BF16)] * 4 + [((32, width), BF16)] * 3,
        ids, up, down, cot, mask, routes, gates, query,
        scalar=True,
        scratch=[pltpu.VMEM((4, shard, 384), BF16)],
    )
    prepared, ld = after(prepared, ld)
    w = among(prepared[:4])
    mine, other, qm = prepared[4:]
    qx = trade(qm, "xl")
    grads = across((mine, other, mine, other))
    states, cum, cum_t = call(
        states_body,
        [((8, 528, HD), BF16), ((HEADS, HD), F32), ((HD, HEADS), F32)],
        ld, key, value, mask,
    )
    parts = exchange(states, SEQ)
    rm, inner, cm = call(
        masked_body,
        [((32, width), F32), ((32, width), F32), ((32, HEADS), F32)],
        qm, key, value, residual, mask, cum, cum_t,
    )
    w = jnp.stack(w)[None]
    (w, grads, qx, inner), parts = after((w, grads, qx, inner), parts)
    queries = along_y(jnp.stack((qm, qx)))
    [carries] = call(carry_body, [((8, 512, HD), BF16)], ids, parts, scalar=True, vmem=VM)
    carried = exchange(carries, SEQ)
    bit = nz // 2
    while bit:
        w = jnp.concatenate((w, trade(w, "z", bit)))
        bit //= 2
    (w, queries), carried = after((w, queries), carried)
    grads = grads + [trade(g, "c") for g in grads]
    routed, normed, normalized, stats = call(
        rows_body,
        [((32, width), BF16), ((32, width), F32), ((32, width), F32), ((32, HD), F32)],
        qm, rm, inner, cm, cum_t, carried,
        vmem=VM,
    )
    weights = along_y(w)
    rows = across([routed] * 4)
    rows = rows + [trade(r, "c") for r in rows]
    z_kept, z_send, *dw = call(
        expert_body,
        [((4, 32, width), BF16)] * 2 + [((width // ny, 384), BF16)] * 4,
        ids, *rows, *grads, *weights,
        scalar=True,
        scratch=[pltpu.VMEM((width, 384), BF16)] + [pltpu.VMEM((8, 32, width), BF16)] * 2,
        flops=2 * 10**9,
        vmem=VM,
    )
    folded = call(fold_body, [((32, width), BF16)] * 4, z_kept, trade(z_send, "c"), vmem=VM)
    z_parts = across(folded)
    d1 = [dw[0]] + [turn(dw[k], k) for k in range(1, 4)]
    decay, scores = call(
        scores_body,
        [((HEADS, HD, 256), F32), ((HEADS, HD, 256), BF16)],
        ids, parts, key, cum_t, *queries,
        scalar=True,
    )
    scores, z_parts = after(scores, z_parts)
    [da] = call(grads_body, [((32, width), BF16)], *z_parts, cot, normed, normalized, stats, vmem=VM)
    dx = trade(da, "xl")
    d1, dx = after(d1, dx)
    [d2] = call(sum_y_body, [((nz, nx, nc * shard, 384), BF16)], *d1)
    das = along_sequence(da, dx)
    (das[2], das[4], das[6]), d2 = after((das[2], das[4], das[6]), d2)
    d3 = exchange(d2, "z")
    [query_grad] = call(
        query_grad_body, [((HD, width), BF16)], da, key, value, mask, cm, cum, cum_t, carried,
        scratch=[pltpu.VMEM((32, width), BF16)],
    )
    query_grad, d3 = after(query_grad, d3)
    d4 = call(
        sum_z_body,
        [((shard, 384), F32)] * 4,
        ids, d3,
        scalar=True,
        scratch=[pltpu.VMEM((4, shard, 384), F32)],
    )
    d5 = among(d4)
    key_grad, value_grad = call(
        key_value_grads_body,
        [((HD, width), BF16), ((HD, width), BF16)],
        value, decay, scores, *queries, *das,
        vmem=VM,
    )
    scale = 1.0 / (ny * nx * nz * nc)

    def finish(*refs):
        weight_grads_body(scale, *refs)

    up_grad, down_grad = call(
        finish,
        [((shard, 768), F32), ((shard, 768), F32)],
        ids, *d5,
        scalar=True,
        scratch=[pltpu.VMEM((4, shard, 384), F32)],
    )
    return query_grad[None], key_grad[None], value_grad[None], up_grad[None], down_grad[None]


def solution(mesh):
    shape = mesh.shape
    grid = mesh.devices.reshape(shape["seq"] // 2, 2, shape["rep"] // 2, 2, shape["exp"])
    fine = Mesh(grid, ("y", "xl", "z", "c", "e"))
    sequences, data = ("z", "c", "e"), ("y", "xl", "z", "c")
    in_specs = (
        P(sequences, SEQ, None),
        P(sequences, SEQ, None),
        P(sequences, SEQ, None),
        P(sequences, SEQ, None),
        P(sequences, None, SEQ),
        P(sequences, SEQ, None, None),
        P(sequences, SEQ, None),
        P(sequences, SEQ, None, None),
        P(sequences, SEQ, None, None),
        P("e", data, None),
        P("e", data, None),
    )
    out_specs = (
        P(sequences, SEQ, None),
        P(sequences, SEQ, None),
        P(sequences, SEQ, None),
        P("e", data, None),
        P("e", data, None),
    )
    return jax.shard_map(local, mesh=fine, in_specs=in_specs, out_specs=out_specs, check_vma=False)
```

```python
import jax
import jax.numpy as jnp
from jax import lax
from jax.experimental import pallas as pl
from jax.experimental.pallas import tpu as pltpu
from jax.sharding import Mesh, PartitionSpec as P

HEADS = 16
HD = 128
EPS = 1e-05
SEQ = ("y", "xl")
VM = 24
Y, XL, Z, C, E = range(5)
F32 = jnp.float32
BF16 = jnp.bfloat16
HIGH = lax.Precision.HIGHEST


def call(body, outs, *args, flops=10**8, scalar=False, scratch=(), vmem=24):
    shapes = [jax.ShapeDtypeStruct(s, d) for s, d in outs]
    moved = sum(a.size * a.dtype.itemsize for a in (*args, *shapes))
    in_specs = [pl.BlockSpec()] * len(args)
    if scalar:
        in_specs[0] = pl.BlockSpec(memory_space=pltpu.SMEM)
    result = pl.pallas_call(
        body,
        out_shape=shapes,
        in_specs=in_specs,
        scratch_shapes=list(scratch),
        compiler_params=pltpu.CompilerParams(vmem_limit_bytes=vmem << 20),
        cost_estimate=pl.CostEstimate(flops=flops, bytes_accessed=moved, transcendentals=0),
    )(*args)
    return result


def iota(shape, dim):
    return lax.broadcasted_iota(jnp.int32, shape, dim)


def tn(a, b, **kw):
    return lax.dot_general(a, b, (((0,), (0,)), ((), ())), preferred_element_type=F32, **kw)


def nt(a, b, **kw):
    return lax.dot_general(a, b, (((1,), (1,)), ((), ())), preferred_element_type=F32, **kw)


def nn(a, b, **kw):
    return lax.dot_general(a, b, (((1,), (0,)), ((), ())), preferred_element_type=F32, **kw)


def head(h):
    return slice(h * HD, (h + 1) * HD)


def exchange(x, axes):
    return lax.all_to_all(x, axes, split_axis=0, concat_axis=0, tiled=True)


def prepare_body(
    ids, up, down, cot, mask, routes, gates, query, w0, w1, w2, w3, own_out, other_out, qm_out, slices
):
    pick_t = (iota((HD, 32), 0) == mask[...]).astype(BF16)
    qm_out[...] = tn(pick_t, query[...]).astype(BF16)
    low = iota((up.shape[0], HD), 1) < 64
    for c in range(12):
        u = up[:, head(c // 2)].astype(F32)
        d = down[:, head(c // 2)].astype(F32)
        if c % 2:
            u = pltpu.roll(u, 64, 1)
        else:
            d = pltpu.roll(d, 64, 1)
        slices[c // 3, :, head(c % 3)] = jnp.where(low, u, d).astype(BF16)
    for k, w in enumerate((w0, w1, w2, w3)):
        w[...] = slices[(ids[XL] * 2 + ids[C]) ^ k]
    lane = iota((HD, HD), 1)
    sub = iota((HD, HD), 0)
    table = jnp.zeros((HD, HD), F32)
    for e in range(2):
        hit = jnp.where(sub == routes[e : e + 1, :], gates[e : e + 1, :], 0.0)
        table = jnp.where(lane == e, jnp.sum(hit, axis=1, keepdims=True), table)
    gm = tn(pick_t.astype(F32), table, precision=HIGH)
    cotf = cot[...].astype(F32)
    first, second = (gm[:, 0:1] * cotf).astype(BF16), (gm[:, 1:2] * cotf).astype(BF16)
    swap = ids[E] == 1
    own_out[...] = jnp.where(swap, second, first)
    other_out[...] = jnp.where(swap, first, second)


def weight_grads_body(scale, ids, p0, p1, p2, p3, up, down, g):
    for k, piece in enumerate((p0, p1, p2, p3)):
        g[(ids[XL] * 2 + ids[C]) ^ k] = piece[...]
    low = iota((up.shape[0], HD), 1) < 64
    for b in range(6):
        first, second = 2 * b, 2 * b + 1
        x = g[first // 3, :, head(first % 3)] * scale
        y = g[second // 3, :, head(second % 3)] * scale
        up[:, head(b)] = jnp.where(low, x, pltpu.roll(y, 64, 1))
        down[:, head(b)] = jnp.where(low, pltpu.roll(x, 64, 1), y)


def states_body(ld, key, value, mask, out, cum_out, cum_t_out):
    rows, cols = iota((HD, HD), 0), iota((HD, HD), 1)
    ldv = ld[...]
    cum = nn(ldv, (rows <= cols).astype(F32), precision=HIGH)
    cum_t = nt((cols <= rows).astype(F32), ldv, precision=HIGH)
    cum_out[...] = cum
    cum_t_out[...] = cum_t
    falling = jnp.exp(cum_t[HD - 1 : HD, :] - cum_t)
    rising = jnp.exp(cum_t)
    for h in range(HEADS):
        k = key[:, head(h)].astype(F32)
        kf = (k * falling[:, h : h + 1]).astype(BF16)
        kb = (k * rising[:, h : h + 1]).astype(BF16)
        v = value[:, head(h)]
        g, at = h // 2, (h % 2) * HD
        out[g, at : at + HD, :] = tn(kf, v).astype(BF16)
        out[g, 256 + at : 256 + at + HD, :] = tn(kb, v).astype(BF16)
    repeat = (iota((32, HD), 0) == iota((32, HD), 1) % 32).astype(BF16)
    places = nn(mask[...].astype(F32).astype(BF16), repeat).astype(jnp.int32)
    places = jnp.where(iota((1, HD), 1) < 96, places, HD - 1)
    chosen = nn(cum, (rows == places).astype(F32), precision=HIGH)
    hi = chosen.astype(BF16).astype(F32)
    mid = (chosen - hi).astype(BF16).astype(F32)
    low = (chosen - hi - mid).astype(BF16).astype(F32)
    lane = iota((HEADS, HD), 1)
    first = (lane < 32) | (lane == 96)
    second = ((lane >= 32) & (lane < 64)) | (lane == 97)
    third = ((lane >= 64) & (lane < 96)) | (lane == 98)
    packed = jnp.where(first, hi, jnp.where(second, mid, jnp.where(third, low, 0.0))).astype(BF16)
    for g in range(8):
        out[g, 512:528, :] = packed


def masked_body(queries, key, value, residual, mask, cum, cum_t, rm_out, inner_out, cm_out):
    pick_t = (iota((HD, 32), 0) == mask[...]).astype(BF16)
    qm = queries[...]
    rm_out[...] = tn(pick_t, residual[...])
    cm = tn(pick_t.astype(F32), cum_t[...], precision=HIGH)
    cm_out[...] = cm
    cumv = cum[...]
    for h in range(HEADS):
        s = nt(qm[:, head(h)], key[:, head(h)])
        p = (s * jnp.exp(-jnp.abs(cm[:, h : h + 1] - cumv[h : h + 1, :]))).astype(BF16)
        inner_out[:, head(h)] = nn(p, value[:, head(h)])


def carry_body(ids, parts, out):
    row, lane = iota((HEADS, HD), 0), iota((HEADS, HD), 1)
    ends = (lane >= 96) & (lane < 99)
    n = parts.shape[0]
    for j in range(2):
        at = slice(j * HD, (j + 1) * HD)
        back = slice(256 + j * HD, 256 + (j + 1) * HD)
        wanted = ends & (row == 2 * (2 * ids[Y] + ids[XL]) + j)
        decay = [
            jnp.exp(jnp.sum(jnp.where(wanted, parts[a, 512:528, :].astype(F32), 0.0), keepdims=True))
            for a in range(n)
        ]
        run = jnp.zeros((HD, HD), F32)
        for a in range(n):
            out[a, at, :] = run.astype(BF16)
            run = decay[a] * run + parts[a, at, :].astype(F32)
        run = jnp.zeros((HD, HD), F32)
        for a in reversed(range(n)):
            out[a, back, :] = run.astype(BF16)
            run = decay[a] * run + parts[a, back, :].astype(F32)


def states_of(carried, h):
    at = (h % 2) * HD
    return carried[h // 2, at : at + HD, :], carried[h // 2, 256 + at : 256 + at + HD, :]


def rows_body(qm, rm, inner, cm, cum_t, carried, routed_out, normed_out, normalized_out, stats_out):
    cmv = cm[...]
    rising = jnp.exp(cmv)
    falling = jnp.exp(cum_t[HD - 1 : HD, :] - cmv)
    lane = iota((32, HD), 1)
    stats = jnp.zeros((32, HD), F32)
    total = jnp.zeros((32, HD), F32)
    residuals = []
    for h in range(HEADS):
        fwd, bwd = states_of(carried, h)
        q = qm[:, head(h)]
        attn = inner[:, head(h)] + rising[:, h : h + 1] * nn(q, fwd) + falling[:, h : h + 1] * nn(q, bwd)
        scale = lax.rsqrt(jnp.mean(attn * attn, axis=-1, keepdims=True) + EPS)
        normed = attn * scale
        normed_out[:, head(h)] = normed
        stats = jnp.where(lane == h, scale, stats)
        r = (rm[:, head(h)] + normed).astype(BF16).astype(F32)
        total = total + r * r
        residuals.append(r)
    row_scale = lax.rsqrt(jnp.sum(total, axis=-1, keepdims=True) * (1.0 / (HEADS * HD)) + EPS)
    stats_out[...] = jnp.where(lane == HEADS, row_scale, stats)
    for h in range(HEADS):
        normalized = residuals[h] * row_scale
        normalized_out[:, head(h)] = normalized
        routed_out[:, head(h)] = normalized.astype(BF16)


def expert_body(ids, *refs):
    rows, grads, pieces, (z_own, z_other), sums, (w_ref, r_ref, g_ref) = (
        refs[:8], refs[8:10], refs[10:14], refs[14:16], refs[16:20], refs[20:],
    )
    nz, unit = pieces[0].shape[0], pieces[0].shape[2]
    for k, piece in enumerate(pieces):
        y = (ids[Y] + 4 - k) % 4
        for zs in range(nz):
            z = ids[Z] ^ sum(nz >> (i + 1) for i in range(3) if zs >> i & 1)
            for cs in range(4):
                x = ids[XL] ^ (cs // 2)
                at = (((y * 2 + x) * nz + z) * 2 + (ids[C] ^ (cs % 2))) * unit
                w_ref[pl.ds(pl.multiple_of(at, unit), unit), :] = piece[zs, cs]
    for k in range(8):
        r_ref[k] = rows[k][...]
        g_ref[k] = grads[k // 4][k % 4]
    width = HEADS * HD
    r = r_ref[...].reshape(256, width)
    g = g_ref[...].reshape(256, width)
    w = w_ref[...]
    pre_all = nn(r, w)
    grad_all = nn(g, w)
    low = iota((256, HD), 1) < 64
    pgs, acts = [], []
    for b in range(3):
        pre = pre_all[:, head(b)]
        act_grad = pltpu.roll(grad_all[:, head(b)], 64, 1)
        sig = jax.nn.sigmoid(pre)
        act = pltpu.roll(pre * sig, 64, 1)
        pre_grad = act_grad * sig * (1.0 + pre * (1.0 - sig))
        pgs.append(jnp.where(low, pre_grad, 0.0).astype(BF16))
        acts.append(jnp.where(low, 0.0, act).astype(BF16))
    pg = jnp.concatenate(pgs, axis=1)
    ac = jnp.concatenate(acts, axis=1)
    z_own[...] = nt(pg[:128], w).astype(BF16).reshape(z_own.shape)
    z_other[...] = nt(pg[128:], w).astype(BF16).reshape(z_other.shape)
    both = jnp.concatenate((pg, ac), axis=0)
    for k, out in enumerate(sums):
        y = (ids[Y] + k) % 4
        cols = pl.ds(pl.multiple_of(y * 512, 512), 512)
        sides = jnp.concatenate((r_ref[:, :, cols].reshape(256, 512), g_ref[:, :, cols].reshape(256, 512)), axis=0)
        out[...] = tn(sides, both).astype(BF16)


def fold_body(kept, came, *outs):
    for k, out in enumerate(outs):
        out[...] = (kept[k].astype(F32) + came[k].astype(F32)).astype(BF16)


def sum_y_body(p0, p1, p2, p3, out):
    nz, nx, unit = out.shape[:3]
    for x in range(nx):
        for z in range(nz):
            at = slice((x * nz + z) * unit, (x * nz + z + 1) * unit)
            total = p0[at, :].astype(F32) + p1[at, :].astype(F32) + p2[at, :].astype(F32) + p3[at, :].astype(F32)
            out[z, x] = total.astype(BF16)


def sum_z_body(ids, parts, o0, o1, o2, o3, total_ref):
    shard = o0.shape[0]
    total = parts[0].astype(F32)
    for z in range(1, parts.shape[0]):
        total = total + parts[z].astype(F32)
    for j in range(4):
        total_ref[j] = total[j // 2, (j % 2) * shard : (j % 2 + 1) * shard]
    for k, out in enumerate((o0, o1, o2, o3)):
        out[...] = total_ref[(ids[XL] * 2 + ids[C]) ^ k]


def grads_body(z0, z1, z2, z3, cot, normed, normalized, stats, out):
    z = (z0[...].astype(F32) + z1[...].astype(F32)) + (z2[...].astype(F32) + z3[...].astype(F32))
    norm = normalized[...]
    st = stats[...]
    mean = jnp.sum(z * norm, axis=-1, keepdims=True) * (1.0 / (HEADS * HD))
    rg = cot[...].astype(F32) + st[:, HEADS : HEADS + 1] * (z - norm * mean)
    for h in range(HEADS):
        n = normed[:, head(h)]
        g = rg[:, head(h)]
        m = jnp.mean(g * n, axis=-1, keepdims=True)
        out[:, head(h)] = (st[:, h : h + 1] * (g - n * m)).astype(BF16)


def query_grad_body(da_own, key, value, mask, cm, cum, cum_t, carried, out, q_ref):
    da = da_own[...]
    pick_t = (iota((HD, 32), 0) == mask[...]).astype(BF16)
    cmv = cm[...]
    cumv = cum[...]
    rising = jnp.exp(cmv)
    falling = jnp.exp(cum_t[HD - 1 : HD, :] - cmv)
    for h in range(HEADS):
        fwd, bwd = states_of(carried, h)
        a = da[:, head(h)]
        s = nt(a, value[:, head(h)])
        p = (s * jnp.exp(-jnp.abs(cmv[:, h : h + 1] - cumv[h : h + 1, :]))).astype(BF16)
        q = nn(p, key[:, head(h)]) + rising[:, h : h + 1] * nt(a, fwd) + falling[:, h : h + 1] * nt(a, bwd)
        q_ref[:, head(h)] = q.astype(BF16)
    out[...] = nn(pick_t, q_ref[...]).astype(BF16)


def rows_of(pieces, h):
    return jnp.concatenate([p[:, head(h)] for p in pieces], axis=0)


def place_of(ids, k):
    return 2 * ((ids[Y] + 4 - k // 2) % 4) + (ids[XL] ^ (k % 2))


def pairs_of(pieces, h):
    return jnp.concatenate([p[:, :, head(h)].reshape(64, HD) for p in pieces], axis=0)


def scores_body(ids, parts, key, cum_t, q0, q1, q2, q3, decay_out, scores_out):
    n = parts.shape[0]
    lane, col = iota((HD, n * 32), 0), iota((HD, n * 32), 1)
    me = 2 * ids[Y] + ids[XL]
    block = jnp.zeros((HD, n * 32), jnp.int32)
    for k in range(n):
        block = jnp.where(col // 32 == k, place_of(ids, k), block)
    at = jnp.zeros((HEADS, n * 32), F32)
    for a in range(n):
        own = (lane < 96) & (lane % 32 == col % 32) & (block == a)
        ends = (lane >= 96) & (lane < 99)
        after = ends & (block > a) & (a >= me)
        before = ends & (block <= a) & (a < me)
        take = jnp.where(own | after, 1.0, jnp.where(before, -1.0, 0.0)).astype(BF16)
        at = at + nn(parts[a, 512:528, :], take)
    ct = cum_t[...]
    for h in range(HEADS):
        decay = jnp.exp(-jnp.abs(ct[:, h : h + 1] - at[h : h + 1, :]))
        decay_out[h] = decay
        scores_out[h] = (nt(key[:, head(h)], pairs_of((q0, q1, q2, q3), h)) * decay).astype(BF16)


def key_value_grads_body(value, decay, scores, q0, q1, q2, q3, *refs):
    das, (key_out, value_out) = refs[:8], refs[8:]
    for h in range(HEADS):
        da = rows_of(das, h)
        value_out[:, head(h)] = nn(scores[h], da).astype(BF16)
        p = (nt(value[:, head(h)], da) * decay[h]).astype(BF16)
        key_out[:, head(h)] = nn(p, pairs_of((q0, q1, q2, q3), h)).astype(BF16)


def trade(x, axis, bit=1):
    n = lax.axis_size(axis)
    return lax.ppermute(x, axis, [(i, i ^ bit) for i in range(n)])


def turn(x, k):
    n = lax.axis_size("y")
    return lax.ppermute(x, "y", [(i, (i + k) % n) for i in range(n)])


def after(first, then):
    return lax.optimization_barrier((first, then))


def along_y(x):
    return [x] + [turn(x, k) for k in range(1, 4)]


def along_sequence(x, other):
    return [p for pair in zip(along_y(x), along_y(other)) for p in pair]


def among(pieces):
    return [pieces[0]] + [
        lax.ppermute(pieces[k], ("xl", "c"), [(i, i ^ k) for i in range(4)]) for k in range(1, 4)
    ]


def across(pieces):
    return [pieces[0]] + [
        lax.ppermute(pieces[k], ("xl", "e"), [(i, i ^ k) for i in range(4)]) for k in range(1, 4)
    ]


def local(residual, query, key, value, ld, cot, mask, routes, gates, up, down):
    residual, query, key, value, ld = residual[0], query[0], key[0], value[0], ld[0]
    cot, mask, routes, gates, up, down = cot[0, 0], mask[0], routes[0, 0], gates[0, 0], up[0], down[0]
    width = HEADS * HD
    ny, nx, nz, nc = (lax.axis_size(a) for a in ("y", "xl", "z", "c"))
    shard = up.shape[0]
    ids = jnp.stack([lax.axis_index(a) for a in ("y", "xl", "z", "c", "e")]).astype(jnp.int32)

    prepared = call(
        prepare_body,
        [((shard, 384), BF16)] * 4 + [((32, width), BF16)] * 3,
        ids, up, down, cot, mask, routes, gates, query,
        scalar=True,
        scratch=[pltpu.VMEM((4, shard, 384), BF16)],
        vmem=56,
    )
    prepared, ld = after(prepared, ld)
    w = among(prepared[:4])
    mine, other, qm = prepared[4:]
    qx = trade(qm, "xl")
    grads = across((mine, other, mine, other))
    states, cum, cum_t = call(
        states_body,
        [((8, 528, HD), BF16), ((HEADS, HD), F32), ((HD, HEADS), F32)],
        ld, key, value, mask,
        vmem=56,
    )
    w, states = after(jnp.stack(w)[None], states)
    parts = exchange(states, SEQ)
    bit = nz // 2
    while bit:
        w = jnp.concatenate((w, trade(w, "z", bit)))
        bit //= 2
    rm, inner, cm = call(
        masked_body,
        [((32, width), F32), ((32, width), F32), ((32, HEADS), F32)],
        qm, key, value, residual, mask, cum, cum_t,
        vmem=56,
    )
    (w, grads, qx, inner), parts = after((w, grads, qx, inner), parts)
    q_two = jnp.stack((qm, qx))
    [carries] = call(carry_body, [((8, 512, HD), BF16)], ids, parts, scalar=True, vmem=VM)
    carried = exchange(carries, SEQ)
    weights = along_y(w)
    grads = jnp.stack(grads)
    grads = (grads, trade(grads, "c"))
    (weights[1], weights[3], grads), carried = after((weights[1], weights[3], grads), carried)
    routed, normed, normalized, stats = call(
        rows_body,
        [((32, width), BF16), ((32, width), F32), ((32, width), F32), ((32, HD), F32)],
        qm, rm, inner, cm, cum_t, carried,
        vmem=VM,
    )
    q_two, routed = after(q_two, routed)
    queries = along_y(q_two)
    rows = across([routed] * 4)
    rows = rows + [trade(r, "c") for r in rows]
    queries, rows = after(queries, rows)
    z_kept, z_send, *dw = call(
        expert_body,
        [((4, 32, width), BF16)] * 2 + [((width // ny, 384), BF16)] * 4,
        ids, *rows, *grads, *weights,
        scalar=True,
        scratch=[pltpu.VMEM((width, 384), BF16)] + [pltpu.VMEM((8, 32, width), BF16)] * 2,
        flops=2 * 10**9,
        vmem=VM,
    )
    folded = call(fold_body, [((32, width), BF16)] * 4, z_kept, trade(z_send, "c"), vmem=VM)
    z_parts = across(folded)
    d1 = [dw[0]] + [turn(dw[k], k) for k in range(1, 4)]
    decay, scores = call(
        scores_body,
        [((HEADS, HD, 256), F32), ((HEADS, HD, 256), BF16)],
        ids, parts, key, cum_t, *queries,
        scalar=True,
    )
    scores, z_parts = after(scores, z_parts)
    [da] = call(grads_body, [((32, width), BF16)], *z_parts, cot, normed, normalized, stats, vmem=VM)
    dx = trade(da, "xl")
    d1, dx = after(d1, dx)
    [d2] = call(sum_y_body, [((nz, nx, nc * shard, 384), BF16)], *d1)
    das = along_sequence(da, dx)
    das[2], d2 = after(das[2], d2)
    d3 = exchange(d2, "z")
    [query_grad] = call(
        query_grad_body, [((HD, width), BF16)], da, key, value, mask, cm, cum, cum_t, carried,
        scratch=[pltpu.VMEM((32, width), BF16)],
    )
    query_grad, d3 = after(query_grad, d3)
    d4 = call(
        sum_z_body,
        [((shard, 384), F32)] * 4,
        ids, d3,
        scalar=True,
        scratch=[pltpu.VMEM((4, shard, 384), F32)],
    )
    d5 = among(d4)
    key_grad, value_grad = call(
        key_value_grads_body,
        [((HD, width), BF16), ((HD, width), BF16)],
        value, decay, scores, *queries, *das,
        vmem=VM,
    )
    scale = 1.0 / (ny * nx * nz * nc)

    def finish(*refs):
        weight_grads_body(scale, *refs)

    up_grad, down_grad = call(
        finish,
        [((shard, 768), F32), ((shard, 768), F32)],
        ids, *d5,
        scalar=True,
        scratch=[pltpu.VMEM((4, shard, 384), F32)],
    )
    return query_grad[None], key_grad[None], value_grad[None], up_grad[None], down_grad[None]


def solution(mesh):
    shape = mesh.shape
    grid = mesh.devices.reshape(shape["seq"] // 2, 2, shape["rep"] // 2, 2, shape["exp"])
    fine = Mesh(grid, ("y", "xl", "z", "c", "e"))
    sequences, data = ("z", "c", "e"), ("y", "xl", "z", "c")
    in_specs = (
        P(sequences, SEQ, None),
        P(sequences, SEQ, None),
        P(sequences, SEQ, None),
        P(sequences, SEQ, None),
        P(sequences, None, SEQ),
        P(sequences, SEQ, None, None),
        P(sequences, SEQ, None),
        P(sequences, SEQ, None, None),
        P(sequences, SEQ, None, None),
        P("e", data, None),
        P("e", data, None),
    )
    out_specs = (
        P(sequences, SEQ, None),
        P(sequences, SEQ, None),
        P(sequences, SEQ, None),
        P("e", data, None),
        P("e", data, None),
    )
    return jax.shard_map(local, mesh=fine, in_specs=in_specs, out_specs=out_specs, check_vma=False)
```

```python
import jax
import jax.numpy as jnp
from jax import lax
from jax.experimental import pallas as pl
from jax.experimental.pallas import tpu as pltpu
from jax.sharding import Mesh, PartitionSpec as P

HEADS = 16
HD = 128
EPS = 1e-05
SEQ = ("y", "xl")
VM = 24
Y, XL, Z, C, E = range(5)
F32 = jnp.float32
BF16 = jnp.bfloat16
HIGH = lax.Precision.HIGHEST


def call(body, outs, *args, flops=10**8, scalar=False, scratch=(), vmem=56):
    shapes = [jax.ShapeDtypeStruct(s, d) for s, d in outs]
    moved = sum(a.size * a.dtype.itemsize for a in (*args, *shapes))
    in_specs = [pl.BlockSpec()] * len(args)
    if scalar:
        in_specs[0] = pl.BlockSpec(memory_space=pltpu.SMEM)
    result = pl.pallas_call(
        body,
        out_shape=shapes,
        in_specs=in_specs,
        scratch_shapes=list(scratch),
        compiler_params=pltpu.CompilerParams(vmem_limit_bytes=vmem << 20),
        cost_estimate=pl.CostEstimate(flops=flops, bytes_accessed=moved, transcendentals=0),
    )(*args)
    return result


def iota(shape, dim):
    return lax.broadcasted_iota(jnp.int32, shape, dim)


def tn(a, b, **kw):
    return lax.dot_general(a, b, (((0,), (0,)), ((), ())), preferred_element_type=F32, **kw)


def nt(a, b, **kw):
    return lax.dot_general(a, b, (((1,), (1,)), ((), ())), preferred_element_type=F32, **kw)


def nn(a, b, **kw):
    return lax.dot_general(a, b, (((1,), (0,)), ((), ())), preferred_element_type=F32, **kw)


def head(h):
    return slice(h * HD, (h + 1) * HD)


def exchange(x, axes):
    return lax.all_to_all(x, axes, split_axis=0, concat_axis=0, tiled=True)


def prepare_body(
    ids, up, down, cot, mask, routes, gates, query, w0, w1, w2, w3, own_out, other_out, qm_out, slices
):
    pick_t = (iota((HD, 32), 0) == mask[...]).astype(BF16)
    qm_out[...] = tn(pick_t, query[...]).astype(BF16)
    low = iota((up.shape[0], HD), 1) < 64
    for c in range(12):
        u = up[:, head(c // 2)].astype(F32)
        d = down[:, head(c // 2)].astype(F32)
        if c % 2:
            u = pltpu.roll(u, 64, 1)
        else:
            d = pltpu.roll(d, 64, 1)
        slices[c // 3, :, head(c % 3)] = jnp.where(low, u, d).astype(BF16)
    for k, w in enumerate((w0, w1, w2, w3)):
        w[...] = slices[(ids[XL] * 2 + ids[C]) ^ k]
    lane = iota((HD, HD), 1)
    sub = iota((HD, HD), 0)
    table = jnp.zeros((HD, HD), F32)
    for e in range(2):
        hit = jnp.where(sub == routes[e : e + 1, :], gates[e : e + 1, :], 0.0)
        table = jnp.where(lane == e, jnp.sum(hit, axis=1, keepdims=True), table)
    gm = tn(pick_t.astype(F32), table, precision=HIGH)
    cotf = cot[...].astype(F32)
    first, second = (gm[:, 0:1] * cotf).astype(BF16), (gm[:, 1:2] * cotf).astype(BF16)
    swap = ids[E] == 1
    own_out[...] = jnp.where(swap, second, first)
    other_out[...] = jnp.where(swap, first, second)


def weight_grads_body(scale, ids, p0, p1, p2, p3, up, down, g):
    for k, piece in enumerate((p0, p1, p2, p3)):
        g[(ids[XL] * 2 + ids[C]) ^ k] = piece[...]
    low = iota((up.shape[0], HD), 1) < 64
    for b in range(6):
        first, second = 2 * b, 2 * b + 1
        x = g[first // 3, :, head(first % 3)] * scale
        y = g[second // 3, :, head(second % 3)] * scale
        up[:, head(b)] = jnp.where(low, x, pltpu.roll(y, 64, 1))
        down[:, head(b)] = jnp.where(low, pltpu.roll(x, 64, 1), y)


def states_body(ld, key, value, mask, out, cum_out, cum_t_out):
    rows, cols = iota((HD, HD), 0), iota((HD, HD), 1)
    ldv = ld[...]
    cum = nn(ldv, (rows <= cols).astype(F32), precision=HIGH)
    cum_t = nt((cols <= rows).astype(F32), ldv, precision=HIGH)
    cum_out[...] = cum
    cum_t_out[...] = cum_t
    falling = jnp.exp(cum_t[HD - 1 : HD, :] - cum_t)
    rising = jnp.exp(cum_t)
    for h in range(HEADS):
        k = key[:, head(h)].astype(F32)
        kf = (k * falling[:, h : h + 1]).astype(BF16)
        kb = (k * rising[:, h : h + 1]).astype(BF16)
        v = value[:, head(h)]
        g, at = h // 2, (h % 2) * HD
        out[g, at : at + HD, :] = tn(kf, v).astype(BF16)
        out[g, 256 + at : 256 + at + HD, :] = tn(kb, v).astype(BF16)
    repeat = (iota((32, HD), 0) == iota((32, HD), 1) % 32).astype(BF16)
    places = nn(mask[...].astype(F32).astype(BF16), repeat).astype(jnp.int32)
    places = jnp.where(iota((1, HD), 1) < 96, places, HD - 1)
    chosen = nn(cum, (rows == places).astype(F32), precision=HIGH)
    hi = chosen.astype(BF16).astype(F32)
    mid = (chosen - hi).astype(BF16).astype(F32)
    low = (chosen - hi - mid).astype(BF16).astype(F32)
    lane = iota((HEADS, HD), 1)
    first = (lane < 32) | (lane == 96)
    second = ((lane >= 32) & (lane < 64)) | (lane == 97)
    third = ((lane >= 64) & (lane < 96)) | (lane == 98)
    packed = jnp.where(first, hi, jnp.where(second, mid, jnp.where(third, low, 0.0))).astype(BF16)
    for g in range(8):
        out[g, 512:528, :] = packed


def masked_body(queries, key, value, residual, mask, cum, cum_t, rm_out, inner_out, cm_out):
    pick_t = (iota((HD, 32), 0) == mask[...]).astype(BF16)
    qm = queries[...]
    rm_out[...] = tn(pick_t, residual[...])
    cm = tn(pick_t.astype(F32), cum_t[...], precision=HIGH)
    cm_out[...] = cm
    cumv = cum[...]
    for h in range(HEADS):
        s = nt(qm[:, head(h)], key[:, head(h)])
        p = (s * jnp.exp(-jnp.abs(cm[:, h : h + 1] - cumv[h : h + 1, :]))).astype(BF16)
        inner_out[:, head(h)] = nn(p, value[:, head(h)])


def carry_body(ids, parts, out):
    row, lane = iota((HEADS, HD), 0), iota((HEADS, HD), 1)
    ends = (lane >= 96) & (lane < 99)
    n = parts.shape[0]
    for j in range(2):
        at = slice(j * HD, (j + 1) * HD)
        back = slice(256 + j * HD, 256 + (j + 1) * HD)
        wanted = ends & (row == 2 * (2 * ids[Y] + ids[XL]) + j)
        decay = [
            jnp.exp(jnp.sum(jnp.where(wanted, parts[a, 512:528, :].astype(F32), 0.0), keepdims=True))
            for a in range(n)
        ]
        run = jnp.zeros((HD, HD), F32)
        for a in range(n):
            out[a, at, :] = run.astype(BF16)
            run = decay[a] * run + parts[a, at, :].astype(F32)
        run = jnp.zeros((HD, HD), F32)
        for a in reversed(range(n)):
            out[a, back, :] = run.astype(BF16)
            run = decay[a] * run + parts[a, back, :].astype(F32)


def states_of(carried, h):
    at = (h % 2) * HD
    return carried[h // 2, at : at + HD, :], carried[h // 2, 256 + at : 256 + at + HD, :]


def rows_body(qm, rm, inner, cm, cum_t, carried, routed_out, normed_out, normalized_out, stats_out):
    cmv = cm[...]
    rising = jnp.exp(cmv)
    falling = jnp.exp(cum_t[HD - 1 : HD, :] - cmv)
    lane = iota((32, HD), 1)
    stats = jnp.zeros((32, HD), F32)
    total = jnp.zeros((32, HD), F32)
    residuals = []
    for h in range(HEADS):
        fwd, bwd = states_of(carried, h)
        q = qm[:, head(h)]
        attn = inner[:, head(h)] + rising[:, h : h + 1] * nn(q, fwd) + falling[:, h : h + 1] * nn(q, bwd)
        scale = lax.rsqrt(jnp.mean(attn * attn, axis=-1, keepdims=True) + EPS)
        normed = attn * scale
        normed_out[:, head(h)] = normed
        stats = jnp.where(lane == h, scale, stats)
        r = (rm[:, head(h)] + normed).astype(BF16).astype(F32)
        total = total + r * r
        residuals.append(r)
    row_scale = lax.rsqrt(jnp.sum(total, axis=-1, keepdims=True) * (1.0 / (HEADS * HD)) + EPS)
    stats_out[...] = jnp.where(lane == HEADS, row_scale, stats)
    for h in range(HEADS):
        normalized = residuals[h] * row_scale
        normalized_out[:, head(h)] = normalized
        routed_out[:, head(h)] = normalized.astype(BF16)


def expert_body(ids, *refs):
    rows, grads, pieces, (z_own, z_other, sums), (w_ref, r_ref, g_ref) = (
        refs[:8], refs[8:16], refs[16:20], refs[20:23], refs[23:],
    )
    nz, unit = pieces[0].shape[0], pieces[0].shape[2]
    for k, piece in enumerate(pieces):
        y = (ids[Y] + 4 - k) % 4
        for zs in range(nz):
            z = ids[Z] ^ sum(nz >> (i + 1) for i in range(3) if zs >> i & 1)
            for cs in range(4):
                x = ids[XL] ^ (cs // 2)
                at = (((y * 2 + x) * nz + z) * 2 + (ids[C] ^ (cs % 2))) * unit
                w_ref[pl.ds(pl.multiple_of(at, unit), unit), :] = piece[zs, cs]
    for k in range(8):
        r_ref[k] = rows[k][...]
        g_ref[k] = grads[k][...]
    width = HEADS * HD
    r = r_ref[...].reshape(256, width)
    g = g_ref[...].reshape(256, width)
    w = w_ref[...]
    pre_all = nn(r, w)
    grad_all = nn(g, w)
    low = iota((256, HD), 1) < 64
    pgs, acts = [], []
    for b in range(3):
        pre = pre_all[:, head(b)]
        act_grad = pltpu.roll(grad_all[:, head(b)], 64, 1)
        sig = jax.nn.sigmoid(pre)
        act = pltpu.roll(pre * sig, 64, 1)
        pre_grad = act_grad * sig * (1.0 + pre * (1.0 - sig))
        pgs.append(jnp.where(low, pre_grad, 0.0).astype(BF16))
        acts.append(jnp.where(low, 0.0, act).astype(BF16))
    pg = jnp.concatenate(pgs, axis=1)
    ac = jnp.concatenate(acts, axis=1)
    z_own[...] = nt(pg[:128], w).astype(BF16).reshape(z_own.shape)
    z_other[...] = nt(pg[128:], w).astype(BF16).reshape(z_other.shape)
    both = jnp.concatenate((pg, ac), axis=0)
    for y in range(4):
        cols = slice(y * 512, (y + 1) * 512)
        sides = jnp.concatenate((r[:, cols], g[:, cols]), axis=0)
        block = tn(sides, both).astype(BF16).reshape(2, nz, 2 * unit, 384)
        for x in range(2):
            for z in range(nz):
                sums[z, y, x] = block[x, z]


def fold_body(kept, came, *outs):
    for k, out in enumerate(outs):
        out[...] = (kept[k].astype(F32) + came[k].astype(F32)).astype(BF16)


def sum_z_body(ids, parts, o0, o1, o2, o3, total_ref):
    total = parts[0].astype(F32)
    for z in range(1, parts.shape[0]):
        total = total + parts[z].astype(F32)
    total_ref[...] = total
    for k, out in enumerate((o0, o1, o2, o3)):
        out[...] = total_ref[(ids[Y] + k) % 4].astype(BF16)


def sum_y_body(ids, p0, p1, p2, p3, o0, o1, o2, o3, total_ref):
    shard = o0.shape[0]
    total = (p0[...].astype(F32) + p1[...].astype(F32)) + (p2[...].astype(F32) + p3[...].astype(F32))
    for j in range(4):
        total_ref[j] = total[j // 2, (j % 2) * shard : (j % 2 + 1) * shard]
    for k, out in enumerate((o0, o1, o2, o3)):
        out[...] = total_ref[(ids[XL] * 2 + ids[C]) ^ k]


def grads_body(z0, z1, z2, z3, cot, normed, normalized, stats, out):
    z = (z0[...].astype(F32) + z1[...].astype(F32)) + (z2[...].astype(F32) + z3[...].astype(F32))
    norm = normalized[...]
    st = stats[...]
    mean = jnp.sum(z * norm, axis=-1, keepdims=True) * (1.0 / (HEADS * HD))
    rg = cot[...].astype(F32) + st[:, HEADS : HEADS + 1] * (z - norm * mean)
    for h in range(HEADS):
        n = normed[:, head(h)]
        g = rg[:, head(h)]
        m = jnp.mean(g * n, axis=-1, keepdims=True)
        out[:, head(h)] = (st[:, h : h + 1] * (g - n * m)).astype(BF16)


def query_grad_body(da_own, key, value, mask, cm, cum, cum_t, carried, out, q_ref):
    da = da_own[...]
    pick_t = (iota((HD, 32), 0) == mask[...]).astype(BF16)
    cmv = cm[...]
    cumv = cum[...]
    rising = jnp.exp(cmv)
    falling = jnp.exp(cum_t[HD - 1 : HD, :] - cmv)
    for h in range(HEADS):
        fwd, bwd = states_of(carried, h)
        a = da[:, head(h)]
        s = nt(a, value[:, head(h)])
        p = (s * jnp.exp(-jnp.abs(cmv[:, h : h + 1] - cumv[h : h + 1, :]))).astype(BF16)
        q = nn(p, key[:, head(h)]) + rising[:, h : h + 1] * nt(a, fwd) + falling[:, h : h + 1] * nt(a, bwd)
        q_ref[:, head(h)] = q.astype(BF16)
    out[...] = nn(pick_t, q_ref[...]).astype(BF16)


def rows_of(pieces, h):
    return jnp.concatenate([p[:, head(h)] for p in pieces], axis=0)


def place_of(ids, k):
    return 2 * ((ids[Y] + 4 - k // 2) % 4) + (ids[XL] ^ (k % 2))


def pairs_of(pieces, h):
    return jnp.concatenate([p[:, :, head(h)].reshape(64, HD) for p in pieces], axis=0)


def scores_body(ids, parts, key, cum_t, q0, q1, q2, q3, decay_out, scores_out):
    n = parts.shape[0]
    lane, col = iota((HD, n * 32), 0), iota((HD, n * 32), 1)
    me = 2 * ids[Y] + ids[XL]
    block = jnp.zeros((HD, n * 32), jnp.int32)
    for k in range(n):
        block = jnp.where(col // 32 == k, place_of(ids, k), block)
    at = jnp.zeros((HEADS, n * 32), F32)
    for a in range(n):
        own = (lane < 96) & (lane % 32 == col % 32) & (block == a)
        ends = (lane >= 96) & (lane < 99)
        after = ends & (block > a) & (a >= me)
        before = ends & (block <= a) & (a < me)
        take = jnp.where(own | after, 1.0, jnp.where(before, -1.0, 0.0)).astype(BF16)
        at = at + nn(parts[a, 512:528, :], take)
    ct = cum_t[...]
    for h in range(HEADS):
        decay = jnp.exp(-jnp.abs(ct[:, h : h + 1] - at[h : h + 1, :]))
        decay_out[h] = decay
        scores_out[h] = (nt(key[:, head(h)], pairs_of((q0, q1, q2, q3), h)) * decay).astype(BF16)


def key_value_grads_body(value, decay, scores, q0, q1, q2, q3, *refs):
    das, (key_out, value_out) = refs[:8], refs[8:]
    for h in range(HEADS):
        da = rows_of(das, h)
        value_out[:, head(h)] = nn(scores[h], da).astype(BF16)
        p = (nt(value[:, head(h)], da) * decay[h]).astype(BF16)
        key_out[:, head(h)] = nn(p, pairs_of((q0, q1, q2, q3), h)).astype(BF16)


def trade(x, axis, bit=1):
    n = lax.axis_size(axis)
    return lax.ppermute(x, axis, [(i, i ^ bit) for i in range(n)])


def turn(x, k):
    n = lax.axis_size("y")
    return lax.ppermute(x, "y", [(i, (i + k) % n) for i in range(n)])


def after(first, then):
    return lax.optimization_barrier((first, then))


def along_y(x):
    return [x] + [turn(x, k) for k in range(1, 4)]


def along_sequence(x, other):
    return [p for pair in zip(along_y(x), along_y(other)) for p in pair]


def among(pieces):
    return [pieces[0]] + [
        lax.ppermute(pieces[k], ("xl", "c"), [(i, i ^ k) for i in range(4)]) for k in range(1, 4)
    ]


def across(pieces):
    return [pieces[0]] + [
        lax.ppermute(pieces[k], ("xl", "e"), [(i, i ^ k) for i in range(4)]) for k in range(1, 4)
    ]


def local(residual, query, key, value, ld, cot, mask, routes, gates, up, down):
    residual, query, key, value, ld = residual[0], query[0], key[0], value[0], ld[0]
    cot, mask, routes, gates, up, down = cot[0, 0], mask[0], routes[0, 0], gates[0, 0], up[0], down[0]
    width = HEADS * HD
    ny, nx, nz, nc = (lax.axis_size(a) for a in ("y", "xl", "z", "c"))
    shard = up.shape[0]
    ids = jnp.stack([lax.axis_index(a) for a in ("y", "xl", "z", "c", "e")]).astype(jnp.int32)

    prepared = call(
        prepare_body,
        [((shard, 384), BF16)] * 4 + [((32, width), BF16)] * 3,
        ids, up, down, cot, mask, routes, gates, query,
        scalar=True,
        scratch=[pltpu.VMEM((4, shard, 384), BF16)],
    )
    prepared, ld = after(prepared, ld)
    w = among(prepared[:4])
    mine, other, qm = prepared[4:]
    qx = trade(qm, "xl")
    grads = across((mine, other, mine, other))
    states, cum, cum_t = call(
        states_body,
        [((8, 528, HD), BF16), ((HEADS, HD), F32), ((HD, HEADS), F32)],
        ld, key, value, mask,
    )
    parts = exchange(states, SEQ)
    rm, inner, cm = call(
        masked_body,
        [((32, width), F32), ((32, width), F32), ((32, HEADS), F32)],
        qm, key, value, residual, mask, cum, cum_t,
    )
    w = jnp.stack(w)[None]
    (w, grads, inner), parts = after((w, grads, inner), parts)
    [carries] = call(carry_body, [((8, 512, HD), BF16)], ids, parts, scalar=True, vmem=VM)
    carried = exchange(carries, SEQ)
    bit = nz // 2
    while bit:
        w = jnp.concatenate((w, trade(w, "z", bit)))
        bit //= 2
    q_two = jnp.stack((qm, qx))
    (w, q_two), carried = after((w, q_two), carried)
    grads = grads + [trade(g, "c") for g in grads]
    routed, normed, normalized, stats = call(
        rows_body,
        [((32, width), BF16), ((32, width), F32), ((32, width), F32), ((32, HD), F32)],
        qm, rm, inner, cm, cum_t, carried,
        vmem=VM,
    )
    weights = along_y(w)
    rows = across([routed] * 4)
    rows = rows + [trade(r, "c") for r in rows]
    z_kept, z_send, dw = call(
        expert_body,
        [((4, 32, width), BF16)] * 2 + [((nz, ny, nx, nc * shard, 384), BF16)],
        ids, *rows, *grads, *weights,
        scalar=True,
        scratch=[pltpu.VMEM((width, 384), BF16)] + [pltpu.VMEM((8, 32, width), BF16)] * 2,
        flops=2 * 10**9,
        vmem=VM,
    )
    folded = call(fold_body, [((32, width), BF16)] * 4, z_kept, trade(z_send, "c"), vmem=VM)
    folded, dw = after(folded, dw)
    z_parts = across(folded)
    d1 = exchange(dw, "z")
    q_two, folded = after(q_two, folded)
    queries = along_y(q_two)
    decay, scores = call(
        scores_body,
        [((HEADS, HD, 256), F32), ((HEADS, HD, 256), BF16)],
        ids, parts, key, cum_t, *queries,
        scalar=True,
        vmem=VM,
    )
    [da] = call(grads_body, [((32, width), BF16)], *z_parts, cot, normed, normalized, stats, vmem=VM)
    dx = trade(da, "xl")
    scores, dx = after(scores, dx)
    das = along_sequence(da, dx)
    [query_grad] = call(
        query_grad_body, [((HD, width), BF16)], da, key, value, mask, cm, cum, cum_t, carried,
        scratch=[pltpu.VMEM((32, width), BF16)],
        vmem=VM,
    )
    key_grad, value_grad = call(
        key_value_grads_body,
        [((HD, width), BF16), ((HD, width), BF16)],
        value, decay, scores, *queries, *das,
        vmem=VM,
    )
    (query_grad, key_grad), d1 = after((query_grad, key_grad), d1)
    d2 = call(
        sum_z_body,
        [((nx, nc * shard, 384), BF16)] * 4,
        ids, d1,
        scalar=True,
        scratch=[pltpu.VMEM((ny, nx, nc * shard, 384), F32)],
        vmem=VM,
    )
    d3 = [d2[0]] + [turn(d2[k], k) for k in range(1, 4)]
    d4 = call(
        sum_y_body,
        [((shard, 384), F32)] * 4,
        ids, *d3,
        scalar=True,
        scratch=[pltpu.VMEM((4, shard, 384), F32)],
        vmem=VM,
    )
    d5 = among(d4)
    scale = 1.0 / (ny * nx * nz * nc)

    def finish(*refs):
        weight_grads_body(scale, *refs)

    up_grad, down_grad = call(
        finish,
        [((shard, 768), F32), ((shard, 768), F32)],
        ids, *d5,
        scalar=True,
        scratch=[pltpu.VMEM((4, shard, 384), F32)],
    )
    return query_grad[None], key_grad[None], value_grad[None], up_grad[None], down_grad[None]


def solution(mesh):
    shape = mesh.shape
    grid = mesh.devices.reshape(shape["seq"] // 2, 2, shape["rep"] // 2, 2, shape["exp"])
    fine = Mesh(grid, ("y", "xl", "z", "c", "e"))
    sequences, data = ("z", "c", "e"), ("y", "xl", "z", "c")
    in_specs = (
        P(sequences, SEQ, None),
        P(sequences, SEQ, None),
        P(sequences, SEQ, None),
        P(sequences, SEQ, None),
        P(sequences, None, SEQ),
        P(sequences, SEQ, None, None),
        P(sequences, SEQ, None),
        P(sequences, SEQ, None, None),
        P(sequences, SEQ, None, None),
        P("e", data, None),
        P("e", data, None),
    )
    out_specs = (
        P(sequences, SEQ, None),
        P(sequences, SEQ, None),
        P(sequences, SEQ, None),
        P("e", data, None),
        P("e", data, None),
    )
    return jax.shard_map(local, mesh=fine, in_specs=in_specs, out_specs=out_specs, check_vma=False)
```

```python
import jax
import jax.numpy as jnp
from jax import lax
from jax.experimental import pallas as pl
from jax.experimental.pallas import tpu as pltpu
from jax.sharding import Mesh, PartitionSpec as P

HEADS = 16
HD = 128
EPS = 1e-05
SEQ = ("y", "xl")
VM = 24
Y, XL, Z, C, E = range(5)
F32 = jnp.float32
BF16 = jnp.bfloat16
HIGH = lax.Precision.HIGHEST


def call(body, outs, *args, flops=10**8, scalar=False, scratch=(), vmem=56):
    shapes = [jax.ShapeDtypeStruct(s, d) for s, d in outs]
    moved = sum(a.size * a.dtype.itemsize for a in (*args, *shapes))
    in_specs = [pl.BlockSpec()] * len(args)
    if scalar:
        in_specs[0] = pl.BlockSpec(memory_space=pltpu.SMEM)
    result = pl.pallas_call(
        body,
        out_shape=shapes,
        in_specs=in_specs,
        scratch_shapes=list(scratch),
        compiler_params=pltpu.CompilerParams(vmem_limit_bytes=vmem << 20),
        cost_estimate=pl.CostEstimate(flops=flops, bytes_accessed=moved, transcendentals=0),
    )(*args)
    return result


def iota(shape, dim):
    return lax.broadcasted_iota(jnp.int32, shape, dim)


def tn(a, b, **kw):
    return lax.dot_general(a, b, (((0,), (0,)), ((), ())), preferred_element_type=F32, **kw)


def nt(a, b, **kw):
    return lax.dot_general(a, b, (((1,), (1,)), ((), ())), preferred_element_type=F32, **kw)


def nn(a, b, **kw):
    return lax.dot_general(a, b, (((1,), (0,)), ((), ())), preferred_element_type=F32, **kw)


def head(h):
    return slice(h * HD, (h + 1) * HD)


def exchange(x, axes):
    return lax.all_to_all(x, axes, split_axis=0, concat_axis=0, tiled=True)


def prepare_body(
    ids, up, down, cot, mask, routes, gates, query, w_out, own_out, other_out, qm_out, slices
):
    pick_t = (iota((HD, 32), 0) == mask[...]).astype(BF16)
    qm_out[...] = tn(pick_t, query[...]).astype(BF16)
    low = iota((up.shape[0], HD), 1) < 64
    for c in range(12):
        u = up[:, head(c // 2)].astype(F32)
        d = down[:, head(c // 2)].astype(F32)
        if c % 2:
            u = pltpu.roll(u, 64, 1)
        else:
            d = pltpu.roll(d, 64, 1)
        slices[c // 3, :, head(c % 3)] = jnp.where(low, u, d).astype(BF16)
    for k in range(4):
        w_out[k] = slices[(ids[XL] * 2 + ids[C]) ^ k]
    lane = iota((HD, HD), 1)
    sub = iota((HD, HD), 0)
    table = jnp.zeros((HD, HD), F32)
    for e in range(2):
        hit = jnp.where(sub == routes[e : e + 1, :], gates[e : e + 1, :], 0.0)
        table = jnp.where(lane == e, jnp.sum(hit, axis=1, keepdims=True), table)
    gm = tn(pick_t.astype(F32), table, precision=HIGH)
    cotf = cot[...].astype(F32)
    first, second = (gm[:, 0:1] * cotf).astype(BF16), (gm[:, 1:2] * cotf).astype(BF16)
    swap = ids[E] == 1
    own_out[...] = jnp.where(swap, second, first)
    other_out[...] = jnp.where(swap, first, second)


def weight_grads_body(scale, ids, p0, p1, p2, p3, up, down, g):
    for k, piece in enumerate((p0, p1, p2, p3)):
        g[(ids[XL] * 2 + ids[C]) ^ k] = piece[...]
    low = iota((up.shape[0], HD), 1) < 64
    for b in range(6):
        first, second = 2 * b, 2 * b + 1
        x = g[first // 3, :, head(first % 3)] * scale
        y = g[second // 3, :, head(second % 3)] * scale
        up[:, head(b)] = jnp.where(low, x, pltpu.roll(y, 64, 1))
        down[:, head(b)] = jnp.where(low, pltpu.roll(x, 64, 1), y)


def states_body(ld, key, value, mask, out, cum_out, cum_t_out):
    rows, cols = iota((HD, HD), 0), iota((HD, HD), 1)
    ldv = ld[...]
    cum = nn(ldv, (rows <= cols).astype(F32), precision=HIGH)
    cum_t = nt((cols <= rows).astype(F32), ldv, precision=HIGH)
    cum_out[...] = cum
    cum_t_out[...] = cum_t
    falling = jnp.exp(cum_t[HD - 1 : HD, :] - cum_t)
    rising = jnp.exp(cum_t)
    for h in range(HEADS):
        k = key[:, head(h)].astype(F32)
        kf = (k * falling[:, h : h + 1]).astype(BF16)
        kb = (k * rising[:, h : h + 1]).astype(BF16)
        v = value[:, head(h)]
        g, at = h // 2, (h % 2) * HD
        out[g, at : at + HD, :] = tn(kf, v).astype(BF16)
        out[g, 256 + at : 256 + at + HD, :] = tn(kb, v).astype(BF16)
    repeat = (iota((32, HD), 0) == iota((32, HD), 1) % 32).astype(BF16)
    places = nn(mask[...].astype(F32).astype(BF16), repeat).astype(jnp.int32)
    places = jnp.where(iota((1, HD), 1) < 96, places, HD - 1)
    chosen = nn(cum, (rows == places).astype(F32), precision=HIGH)
    hi = chosen.astype(BF16).astype(F32)
    mid = (chosen - hi).astype(BF16).astype(F32)
    low = (chosen - hi - mid).astype(BF16).astype(F32)
    lane = iota((HEADS, HD), 1)
    first = (lane < 32) | (lane == 96)
    second = ((lane >= 32) & (lane < 64)) | (lane == 97)
    third = ((lane >= 64) & (lane < 96)) | (lane == 98)
    packed = jnp.where(first, hi, jnp.where(second, mid, jnp.where(third, low, 0.0))).astype(BF16)
    for g in range(8):
        out[g, 512:528, :] = packed


def masked_body(queries, key, value, residual, mask, cum, cum_t, rm_out, inner_out, cm_out):
    pick_t = (iota((HD, 32), 0) == mask[...]).astype(BF16)
    qm = queries[...]
    rm_out[...] = tn(pick_t, residual[...])
    cm = tn(pick_t.astype(F32), cum_t[...], precision=HIGH)
    cm_out[...] = cm
    cumv = cum[...]
    for h in range(HEADS):
        s = nt(qm[:, head(h)], key[:, head(h)])
        p = (s * jnp.exp(-jnp.abs(cm[:, h : h + 1] - cumv[h : h + 1, :]))).astype(BF16)
        inner_out[:, head(h)] = nn(p, value[:, head(h)])


def carry_body(ids, parts, out):
    row, lane = iota((HEADS, HD), 0), iota((HEADS, HD), 1)
    ends = (lane >= 96) & (lane < 99)
    n = parts.shape[0]
    for j in range(2):
        at = slice(j * HD, (j + 1) * HD)
        back = slice(256 + j * HD, 256 + (j + 1) * HD)
        wanted = ends & (row == 2 * (2 * ids[Y] + ids[XL]) + j)
        decay = [
            jnp.exp(jnp.sum(jnp.where(wanted, parts[a, 512:528, :].astype(F32), 0.0), keepdims=True))
            for a in range(n)
        ]
        run = jnp.zeros((HD, HD), F32)
        for a in range(n):
            out[a, at, :] = run.astype(BF16)
            run = decay[a] * run + parts[a, at, :].astype(F32)
        run = jnp.zeros((HD, HD), F32)
        for a in reversed(range(n)):
            out[a, back, :] = run.astype(BF16)
            run = decay[a] * run + parts[a, back, :].astype(F32)


def states_of(carried, h):
    at = (h % 2) * HD
    return carried[h // 2, at : at + HD, :], carried[h // 2, 256 + at : 256 + at + HD, :]


def rows_body(qm, rm, inner, cm, cum_t, carried, routed_out, normed_out, normalized_out, stats_out):
    cmv = cm[...]
    rising = jnp.exp(cmv)
    falling = jnp.exp(cum_t[HD - 1 : HD, :] - cmv)
    lane = iota((32, HD), 1)
    stats = jnp.zeros((32, HD), F32)
    total = jnp.zeros((32, HD), F32)
    residuals = []
    for h in range(HEADS):
        fwd, bwd = states_of(carried, h)
        q = qm[:, head(h)]
        attn = inner[:, head(h)] + rising[:, h : h + 1] * nn(q, fwd) + falling[:, h : h + 1] * nn(q, bwd)
        scale = lax.rsqrt(jnp.mean(attn * attn, axis=-1, keepdims=True) + EPS)
        normed = attn * scale
        normed_out[:, head(h)] = normed
        stats = jnp.where(lane == h, scale, stats)
        r = (rm[:, head(h)] + normed).astype(BF16).astype(F32)
        total = total + r * r
        residuals.append(r)
    row_scale = lax.rsqrt(jnp.sum(total, axis=-1, keepdims=True) * (1.0 / (HEADS * HD)) + EPS)
    stats_out[...] = jnp.where(lane == HEADS, row_scale, stats)
    for h in range(HEADS):
        normalized = residuals[h] * row_scale
        normalized_out[:, head(h)] = normalized
        routed_out[:, head(h)] = normalized.astype(BF16)


def expert_body(ids, *refs):
    rows, grads, pieces, (z_own, z_other, sums), (w_ref, r_ref, g_ref) = (
        refs[:8], refs[8:16], refs[16:20], refs[20:23], refs[23:],
    )
    nz, unit = pieces[0].shape[0], pieces[0].shape[2]
    for k, piece in enumerate(pieces):
        y = (ids[Y] + 4 - k) % 4
        for zs in range(nz):
            z = ids[Z] ^ sum(nz >> (i + 1) for i in range(3) if zs >> i & 1)
            for cs in range(4):
                x = ids[XL] ^ (cs // 2)
                at = (((y * 2 + x) * nz + z) * 2 + (ids[C] ^ (cs % 2))) * unit
                w_ref[pl.ds(pl.multiple_of(at, unit), unit), :] = piece[zs, cs]
    for k in range(8):
        r_ref[k] = rows[k][...]
        g_ref[k] = grads[k][...]
    width = HEADS * HD
    r = r_ref[...].reshape(256, width)
    g = g_ref[...].reshape(256, width)
    w = w_ref[...]
    pre_all = nn(r, w)
    grad_all = nn(g, w)
    low = iota((256, HD), 1) < 64
    pgs, acts = [], []
    for b in range(3):
        pre = pre_all[:, head(b)]
        act_grad = pltpu.roll(grad_all[:, head(b)], 64, 1)
        sig = jax.nn.sigmoid(pre)
        act = pltpu.roll(pre * sig, 64, 1)
        pre_grad = act_grad * sig * (1.0 + pre * (1.0 - sig))
        pgs.append(jnp.where(low, pre_grad, 0.0).astype(BF16))
        acts.append(jnp.where(low, 0.0, act).astype(BF16))
    pg = jnp.concatenate(pgs, axis=1)
    ac = jnp.concatenate(acts, axis=1)
    z_own[...] = nt(pg[:128], w).astype(BF16).reshape(z_own.shape)
    z_other[...] = nt(pg[128:], w).astype(BF16).reshape(z_other.shape)
    both = jnp.concatenate((pg, ac), axis=0)
    for y in range(4):
        cols = slice(y * 512, (y + 1) * 512)
        sides = jnp.concatenate((r[:, cols], g[:, cols]), axis=0)
        block = tn(sides, both).astype(BF16).reshape(2, nz, 2 * unit, 384)
        for x in range(2):
            for z in range(nz):
                sums[z, y, x] = block[x, z]


def fold_body(kept, came, *outs):
    for k, out in enumerate(outs):
        out[...] = (kept[k].astype(F32) + came[k].astype(F32)).astype(BF16)


def sum_z_body(ids, parts, o0, o1, o2, o3, total_ref):
    total = parts[0].astype(F32)
    for z in range(1, parts.shape[0]):
        total = total + parts[z].astype(F32)
    total_ref[...] = total
    for k, out in enumerate((o0, o1, o2, o3)):
        out[...] = total_ref[(ids[Y] + k) % 4].astype(BF16)


def sum_y_body(ids, p0, p1, p2, p3, o0, o1, o2, o3, total_ref):
    shard = o0.shape[0]
    total = (p0[...].astype(F32) + p1[...].astype(F32)) + (p2[...].astype(F32) + p3[...].astype(F32))
    for j in range(4):
        total_ref[j] = total[j // 2, (j % 2) * shard : (j % 2 + 1) * shard]
    for k, out in enumerate((o0, o1, o2, o3)):
        out[...] = total_ref[(ids[XL] * 2 + ids[C]) ^ k]


def grads_body(z0, z1, z2, z3, cot, normed, normalized, stats, out):
    z = (z0[...].astype(F32) + z1[...].astype(F32)) + (z2[...].astype(F32) + z3[...].astype(F32))
    norm = normalized[...]
    st = stats[...]
    mean = jnp.sum(z * norm, axis=-1, keepdims=True) * (1.0 / (HEADS * HD))
    rg = cot[...].astype(F32) + st[:, HEADS : HEADS + 1] * (z - norm * mean)
    for h in range(HEADS):
        n = normed[:, head(h)]
        g = rg[:, head(h)]
        m = jnp.mean(g * n, axis=-1, keepdims=True)
        out[:, head(h)] = (st[:, h : h + 1] * (g - n * m)).astype(BF16)


def query_grad_body(da_own, key, value, mask, cm, cum, cum_t, carried, out, q_ref):
    da = da_own[...]
    pick_t = (iota((HD, 32), 0) == mask[...]).astype(BF16)
    cmv = cm[...]
    cumv = cum[...]
    rising = jnp.exp(cmv)
    falling = jnp.exp(cum_t[HD - 1 : HD, :] - cmv)
    for h in range(HEADS):
        fwd, bwd = states_of(carried, h)
        a = da[:, head(h)]
        s = nt(a, value[:, head(h)])
        p = (s * jnp.exp(-jnp.abs(cmv[:, h : h + 1] - cumv[h : h + 1, :]))).astype(BF16)
        q = nn(p, key[:, head(h)]) + rising[:, h : h + 1] * nt(a, fwd) + falling[:, h : h + 1] * nt(a, bwd)
        q_ref[:, head(h)] = q.astype(BF16)
    out[...] = nn(pick_t, q_ref[...]).astype(BF16)


def rows_of(pieces, h):
    return jnp.concatenate([p[:, head(h)] for p in pieces], axis=0)


def place_of(ids, k):
    return 2 * ((ids[Y] + 4 - k // 2) % 4) + (ids[XL] ^ (k % 2))


def pairs_of(pieces, h):
    return jnp.concatenate([p[:, :, head(h)].reshape(64, HD) for p in pieces], axis=0)


def scores_body(ids, parts, key, cum_t, q0, q1, q2, q3, decay_out, scores_out):
    n = parts.shape[0]
    lane, col = iota((HD, n * 32), 0), iota((HD, n * 32), 1)
    me = 2 * ids[Y] + ids[XL]
    block = jnp.zeros((HD, n * 32), jnp.int32)
    for k in range(n):
        block = jnp.where(col // 32 == k, place_of(ids, k), block)
    at = jnp.zeros((HEADS, n * 32), F32)
    for a in range(n):
        own = (lane < 96) & (lane % 32 == col % 32) & (block == a)
        ends = (lane >= 96) & (lane < 99)
        after = ends & (block > a) & (a >= me)
        before = ends & (block <= a) & (a < me)
        take = jnp.where(own | after, 1.0, jnp.where(before, -1.0, 0.0)).astype(BF16)
        at = at + nn(parts[a, 512:528, :], take)
    ct = cum_t[...]
    for h in range(HEADS):
        decay = jnp.exp(-jnp.abs(ct[:, h : h + 1] - at[h : h + 1, :]))
        decay_out[h] = decay
        scores_out[h] = (nt(key[:, head(h)], pairs_of((q0, q1, q2, q3), h)) * decay).astype(BF16)


def key_value_grads_body(value, decay, scores, q0, q1, q2, q3, *refs):
    das, (key_out, value_out) = refs[:8], refs[8:]
    for h in range(HEADS):
        da = rows_of(das, h)
        value_out[:, head(h)] = nn(scores[h], da).astype(BF16)
        p = (nt(value[:, head(h)], da) * decay[h]).astype(BF16)
        key_out[:, head(h)] = nn(p, pairs_of((q0, q1, q2, q3), h)).astype(BF16)


def trade(x, axis, bit=1):
    n = lax.axis_size(axis)
    return lax.ppermute(x, axis, [(i, i ^ bit) for i in range(n)])


def turn(x, k):
    n = lax.axis_size("y")
    return lax.ppermute(x, "y", [(i, (i + k) % n) for i in range(n)])


def after(first, then):
    return lax.optimization_barrier((first, then))


def along_y(x):
    return [x] + [turn(x, k) for k in range(1, 4)]


def along_sequence(x, other):
    return [p for pair in zip(along_y(x), along_y(other)) for p in pair]


def among(pieces):
    return [pieces[0]] + [
        lax.ppermute(pieces[k], ("xl", "c"), [(i, i ^ k) for i in range(4)]) for k in range(1, 4)
    ]


def across(pieces):
    return [pieces[0]] + [
        lax.ppermute(pieces[k], ("xl", "e"), [(i, i ^ k) for i in range(4)]) for k in range(1, 4)
    ]


def local(residual, query, key, value, ld, cot, mask, routes, gates, up, down):
    residual, query, key, value, ld = residual[0], query[0], key[0], value[0], ld[0]
    cot, mask, routes, gates, up, down = cot[0, 0], mask[0], routes[0, 0], gates[0, 0], up[0], down[0]
    width = HEADS * HD
    ny, nx, nz, nc = (lax.axis_size(a) for a in ("y", "xl", "z", "c"))
    shard = up.shape[0]
    ids = jnp.stack([lax.axis_index(a) for a in ("y", "xl", "z", "c", "e")]).astype(jnp.int32)

    prepared = call(
        prepare_body,
        [((4, shard, 384), BF16)] + [((32, width), BF16)] * 3,
        ids, up, down, cot, mask, routes, gates, query,
        scalar=True,
        scratch=[pltpu.VMEM((4, shard, 384), BF16)],
    )
    prepared, ld = after(prepared, ld)
    bit = nz // 2
    w = jnp.stack((prepared[0], trade(prepared[0], "z", bit)), axis=1)
    w = jnp.stack(among([w[k] for k in range(4)]), axis=1)
    mine, other, qm = prepared[1:]
    qx = trade(qm, "xl")
    grads = across((mine, other, mine, other))
    states, cum, cum_t = call(
        states_body,
        [((8, 528, HD), BF16), ((HEADS, HD), F32), ((HD, HEADS), F32)],
        ld, key, value, mask,
    )
    parts = exchange(states, SEQ)
    rm, inner, cm = call(
        masked_body,
        [((32, width), F32), ((32, width), F32), ((32, HEADS), F32)],
        qm, key, value, residual, mask, cum, cum_t,
    )
    (w, grads, inner), parts = after((w, grads, inner), parts)
    [carries] = call(carry_body, [((8, 512, HD), BF16)], ids, parts, scalar=True, vmem=VM)
    carried = exchange(carries, SEQ)
    bit //= 2
    while bit:
        w = jnp.concatenate((w, trade(w, "z", bit)))
        bit //= 2
    q_two = jnp.stack((qm, qx))
    (w, q_two), carried = after((w, q_two), carried)
    grads = grads + [trade(g, "c") for g in grads]
    routed, normed, normalized, stats = call(
        rows_body,
        [((32, width), BF16), ((32, width), F32), ((32, width), F32), ((32, HD), F32)],
        qm, rm, inner, cm, cum_t, carried,
        vmem=VM,
    )
    weights = along_y(w)
    rows = across([routed] * 4)
    rows = rows + [trade(r, "c") for r in rows]
    z_kept, z_send, dw = call(
        expert_body,
        [((4, 32, width), BF16)] * 2 + [((nz, ny, nx, nc * shard, 384), BF16)],
        ids, *rows, *grads, *weights,
        scalar=True,
        scratch=[pltpu.VMEM((width, 384), BF16)] + [pltpu.VMEM((8, 32, width), BF16)] * 2,
        flops=2 * 10**9,
        vmem=VM,
    )
    folded = call(fold_body, [((32, width), BF16)] * 4, z_kept, trade(z_send, "c"), vmem=VM)
    folded, dw = after(folded, dw)
    z_parts = across(folded)
    d1 = exchange(dw, "z")
    q_two, folded = after(q_two, folded)
    queries = along_y(q_two)
    decay, scores = call(
        scores_body,
        [((HEADS, HD, 256), F32), ((HEADS, HD, 256), BF16)],
        ids, parts, key, cum_t, *queries,
        scalar=True,
        vmem=VM,
    )
    [da] = call(grads_body, [((32, width), BF16)], *z_parts, cot, normed, normalized, stats, vmem=VM)
    dx = trade(da, "xl")
    scores, dx = after(scores, dx)
    das = along_sequence(da, dx)
    [query_grad] = call(
        query_grad_body, [((HD, width), BF16)], da, key, value, mask, cm, cum, cum_t, carried,
        scratch=[pltpu.VMEM((32, width), BF16)],
        vmem=VM,
    )
    key_grad, value_grad = call(
        key_value_grads_body,
        [((HD, width), BF16), ((HD, width), BF16)],
        value, decay, scores, *queries, *das,
        vmem=VM,
    )
    (query_grad, key_grad), d1 = after((query_grad, key_grad), d1)
    d2 = call(
        sum_z_body,
        [((nx, nc * shard, 384), BF16)] * 4,
        ids, d1,
        scalar=True,
        scratch=[pltpu.VMEM((ny, nx, nc * shard, 384), F32)],
        vmem=VM,
    )
    d3 = [d2[0]] + [turn(d2[k], k) for k in range(1, 4)]
    d4 = call(
        sum_y_body,
        [((shard, 384), F32)] * 4,
        ids, *d3,
        scalar=True,
        scratch=[pltpu.VMEM((4, shard, 384), F32)],
        vmem=VM,
    )
    d5 = among(d4)
    scale = 1.0 / (ny * nx * nz * nc)

    def finish(*refs):
        weight_grads_body(scale, *refs)

    up_grad, down_grad = call(
        finish,
        [((shard, 768), F32), ((shard, 768), F32)],
        ids, *d5,
        scalar=True,
        scratch=[pltpu.VMEM((4, shard, 384), F32)],
    )
    return query_grad[None], key_grad[None], value_grad[None], up_grad[None], down_grad[None]


def solution(mesh):
    shape = mesh.shape
    grid = mesh.devices.reshape(shape["seq"] // 2, 2, shape["rep"] // 2, 2, shape["exp"])
    fine = Mesh(grid, ("y", "xl", "z", "c", "e"))
    sequences, data = ("z", "c", "e"), ("y", "xl", "z", "c")
    in_specs = (
        P(sequences, SEQ, None),
        P(sequences, SEQ, None),
        P(sequences, SEQ, None),
        P(sequences, SEQ, None),
        P(sequences, None, SEQ),
        P(sequences, SEQ, None, None),
        P(sequences, SEQ, None),
        P(sequences, SEQ, None, None),
        P(sequences, SEQ, None, None),
        P("e", data, None),
        P("e", data, None),
    )
    out_specs = (
        P(sequences, SEQ, None),
        P(sequences, SEQ, None),
        P(sequences, SEQ, None),
        P("e", data, None),
        P("e", data, None),
    )
    return jax.shard_map(local, mesh=fine, in_specs=in_specs, out_specs=out_specs, check_vma=False)
```

```python
import jax
import jax.numpy as jnp
from jax import lax
from jax.experimental import pallas as pl
from jax.experimental.pallas import tpu as pltpu
from jax.sharding import Mesh, PartitionSpec as P

HEADS = 16
HD = 128
EPS = 1e-05
SEQ = ("y", "xl")
VM = 24
Y, XL, Z, C, E = range(5)
F32 = jnp.float32
BF16 = jnp.bfloat16
HIGH = lax.Precision.HIGHEST


def call(body, outs, *args, flops=10**8, scalar=False, scratch=(), vmem=56):
    shapes = [jax.ShapeDtypeStruct(s, d) for s, d in outs]
    moved = sum(a.size * a.dtype.itemsize for a in (*args, *shapes))
    in_specs = [pl.BlockSpec()] * len(args)
    if scalar:
        in_specs[0] = pl.BlockSpec(memory_space=pltpu.SMEM)
    result = pl.pallas_call(
        body,
        out_shape=shapes,
        in_specs=in_specs,
        scratch_shapes=list(scratch),
        compiler_params=pltpu.CompilerParams(vmem_limit_bytes=vmem << 20),
        cost_estimate=pl.CostEstimate(flops=flops, bytes_accessed=moved, transcendentals=0),
    )(*args)
    return result


def iota(shape, dim):
    return lax.broadcasted_iota(jnp.int32, shape, dim)


def tn(a, b, **kw):
    return lax.dot_general(a, b, (((0,), (0,)), ((), ())), preferred_element_type=F32, **kw)


def nt(a, b, **kw):
    return lax.dot_general(a, b, (((1,), (1,)), ((), ())), preferred_element_type=F32, **kw)


def nn(a, b, **kw):
    return lax.dot_general(a, b, (((1,), (0,)), ((), ())), preferred_element_type=F32, **kw)


def head(h):
    return slice(h * HD, (h + 1) * HD)


def exchange(x, axes):
    return lax.all_to_all(x, axes, split_axis=0, concat_axis=0, tiled=True)


def prepare_body(
    ids, up, down, cot, mask, routes, gates, query, w_out, own_out, other_out, qm_out, slices
):
    pick_t = (iota((HD, 32), 0) == mask[...]).astype(BF16)
    qm_out[...] = tn(pick_t, query[...]).astype(BF16)
    low = iota((up.shape[0], HD), 1) < 64
    for c in range(12):
        u = up[:, head(c // 2)].astype(F32)
        d = down[:, head(c // 2)].astype(F32)
        if c % 2:
            u = pltpu.roll(u, 64, 1)
        else:
            d = pltpu.roll(d, 64, 1)
        slices[c // 3, :, head(c % 3)] = jnp.where(low, u, d).astype(BF16)
    for k in range(4):
        w_out[k] = slices[(ids[XL] * 2 + ids[C]) ^ k]
    lane = iota((HD, HD), 1)
    sub = iota((HD, HD), 0)
    table = jnp.zeros((HD, HD), F32)
    for e in range(2):
        hit = jnp.where(sub == routes[e : e + 1, :], gates[e : e + 1, :], 0.0)
        table = jnp.where(lane == e, jnp.sum(hit, axis=1, keepdims=True), table)
    gm = tn(pick_t.astype(F32), table, precision=HIGH)
    cotf = cot[...].astype(F32)
    first, second = (gm[:, 0:1] * cotf).astype(BF16), (gm[:, 1:2] * cotf).astype(BF16)
    swap = ids[E] == 1
    own_out[...] = jnp.where(swap, second, first)
    other_out[...] = jnp.where(swap, first, second)


def weight_grads_body(scale, ids, p0, p1, p2, p3, up, down, g):
    for k, piece in enumerate((p0, p1, p2, p3)):
        g[(ids[XL] * 2 + ids[C]) ^ k] = piece[...]
    low = iota((up.shape[0], HD), 1) < 64
    for b in range(6):
        first, second = 2 * b, 2 * b + 1
        x = g[first // 3, :, head(first % 3)] * scale
        y = g[second // 3, :, head(second % 3)] * scale
        up[:, head(b)] = jnp.where(low, x, pltpu.roll(y, 64, 1))
        down[:, head(b)] = jnp.where(low, pltpu.roll(x, 64, 1), y)


def states_body(ld, key, value, mask, out, cum_out, cum_t_out):
    rows, cols = iota((HD, HD), 0), iota((HD, HD), 1)
    ldv = ld[...]
    cum = nn(ldv, (rows <= cols).astype(F32), precision=HIGH)
    cum_t = nt((cols <= rows).astype(F32), ldv, precision=HIGH)
    cum_out[...] = cum
    cum_t_out[...] = cum_t
    falling = jnp.exp(cum_t[HD - 1 : HD, :] - cum_t)
    rising = jnp.exp(cum_t)
    for h in range(HEADS):
        k = key[:, head(h)].astype(F32)
        kf = (k * falling[:, h : h + 1]).astype(BF16)
        kb = (k * rising[:, h : h + 1]).astype(BF16)
        v = value[:, head(h)]
        g, at = h // 2, (h % 2) * HD
        out[g, at : at + HD, :] = tn(kf, v).astype(BF16)
        out[g, 256 + at : 256 + at + HD, :] = tn(kb, v).astype(BF16)
    repeat = (iota((32, HD), 0) == iota((32, HD), 1) % 32).astype(BF16)
    places = nn(mask[...].astype(F32).astype(BF16), repeat).astype(jnp.int32)
    places = jnp.where(iota((1, HD), 1) < 96, places, HD - 1)
    chosen = nn(cum, (rows == places).astype(F32), precision=HIGH)
    hi = chosen.astype(BF16).astype(F32)
    mid = (chosen - hi).astype(BF16).astype(F32)
    low = (chosen - hi - mid).astype(BF16).astype(F32)
    lane = iota((HEADS, HD), 1)
    first = (lane < 32) | (lane == 96)
    second = ((lane >= 32) & (lane < 64)) | (lane == 97)
    third = ((lane >= 64) & (lane < 96)) | (lane == 98)
    packed = jnp.where(first, hi, jnp.where(second, mid, jnp.where(third, low, 0.0))).astype(BF16)
    for g in range(8):
        out[g, 512:528, :] = packed


def masked_body(queries, key, value, residual, mask, cum, cum_t, rm_out, inner_out, cm_out):
    pick_t = (iota((HD, 32), 0) == mask[...]).astype(BF16)
    qm = queries[...]
    rm_out[...] = tn(pick_t, residual[...])
    cm = tn(pick_t.astype(F32), cum_t[...], precision=HIGH)
    cm_out[...] = cm
    cumv = cum[...]
    for h in range(HEADS):
        s = nt(qm[:, head(h)], key[:, head(h)])
        p = (s * jnp.exp(-jnp.abs(cm[:, h : h + 1] - cumv[h : h + 1, :]))).astype(BF16)
        inner_out[:, head(h)] = nn(p, value[:, head(h)])


def carry_body(ids, parts, out):
    row, lane = iota((HEADS, HD), 0), iota((HEADS, HD), 1)
    ends = (lane >= 96) & (lane < 99)
    n = parts.shape[0]
    for j in range(2):
        at = slice(j * HD, (j + 1) * HD)
        back = slice(256 + j * HD, 256 + (j + 1) * HD)
        wanted = ends & (row == 2 * (2 * ids[Y] + ids[XL]) + j)
        decay = [
            jnp.exp(jnp.sum(jnp.where(wanted, parts[a, 512:528, :].astype(F32), 0.0), keepdims=True))
            for a in range(n)
        ]
        run = jnp.zeros((HD, HD), F32)
        for a in range(n):
            out[a, at, :] = run.astype(BF16)
            run = decay[a] * run + parts[a, at, :].astype(F32)
        run = jnp.zeros((HD, HD), F32)
        for a in reversed(range(n)):
            out[a, back, :] = run.astype(BF16)
            run = decay[a] * run + parts[a, back, :].astype(F32)


def states_of(carried, h):
    at = (h % 2) * HD
    return carried[h // 2, at : at + HD, :], carried[h // 2, 256 + at : 256 + at + HD, :]


def rows_body(qm, rm, inner, cm, cum_t, carried, routed_out, normed_out, normalized_out, stats_out):
    cmv = cm[...]
    rising = jnp.exp(cmv)
    falling = jnp.exp(cum_t[HD - 1 : HD, :] - cmv)
    lane = iota((32, HD), 1)
    stats = jnp.zeros((32, HD), F32)
    total = jnp.zeros((32, HD), F32)
    residuals = []
    for h in range(HEADS):
        fwd, bwd = states_of(carried, h)
        q = qm[:, head(h)]
        attn = inner[:, head(h)] + rising[:, h : h + 1] * nn(q, fwd) + falling[:, h : h + 1] * nn(q, bwd)
        scale = lax.rsqrt(jnp.mean(attn * attn, axis=-1, keepdims=True) + EPS)
        normed = attn * scale
        normed_out[:, head(h)] = normed
        stats = jnp.where(lane == h, scale, stats)
        r = (rm[:, head(h)] + normed).astype(BF16).astype(F32)
        total = total + r * r
        residuals.append(r)
    row_scale = lax.rsqrt(jnp.sum(total, axis=-1, keepdims=True) * (1.0 / (HEADS * HD)) + EPS)
    stats_out[...] = jnp.where(lane == HEADS, row_scale, stats)
    for h in range(HEADS):
        normalized = residuals[h] * row_scale
        normalized_out[:, head(h)] = normalized
        routed_out[:, head(h)] = normalized.astype(BF16)


def expert_body(ids, *refs):
    rows, grads, pieces, (z_own, z_other, sums), (w_ref, r_ref, g_ref) = (
        refs[:8], refs[8:16], refs[16:20], refs[20:23], refs[23:],
    )
    nz, unit = pieces[0].shape[0], pieces[0].shape[2]
    for k, piece in enumerate(pieces):
        y = (ids[Y] + 4 - k) % 4
        for zs in range(nz):
            z = ids[Z] ^ sum(nz >> (i + 1) for i in range(3) if zs >> i & 1)
            for cs in range(4):
                x = ids[XL] ^ (cs // 2)
                at = (((y * 2 + x) * nz + z) * 2 + (ids[C] ^ (cs % 2))) * unit
                w_ref[pl.ds(pl.multiple_of(at, unit), unit), :] = piece[zs, cs]
    for k in range(8):
        r_ref[k] = rows[k][...]
        g_ref[k] = grads[k][...]
    width = HEADS * HD
    r = r_ref[...].reshape(256, width)
    g = g_ref[...].reshape(256, width)
    w = w_ref[...]
    pre_all = nn(r, w)
    grad_all = nn(g, w)
    low = iota((256, HD), 1) < 64
    pgs, acts = [], []
    for b in range(3):
        pre = pre_all[:, head(b)]
        act_grad = pltpu.roll(grad_all[:, head(b)], 64, 1)
        sig = jax.nn.sigmoid(pre)
        act = pltpu.roll(pre * sig, 64, 1)
        pre_grad = act_grad * sig * (1.0 + pre * (1.0 - sig))
        pgs.append(jnp.where(low, pre_grad, 0.0).astype(BF16))
        acts.append(jnp.where(low, 0.0, act).astype(BF16))
    pg = jnp.concatenate(pgs, axis=1)
    ac = jnp.concatenate(acts, axis=1)
    z_own[...] = nt(pg[:128], w).astype(BF16).reshape(z_own.shape)
    z_other[...] = nt(pg[128:], w).astype(BF16).reshape(z_other.shape)
    both = jnp.concatenate((pg, ac), axis=0)
    for y in range(4):
        cols = slice(y * 512, (y + 1) * 512)
        sides = jnp.concatenate((r[:, cols], g[:, cols]), axis=0)
        block = tn(sides, both).astype(BF16).reshape(2, nz, 2 * unit, 384)
        for x in range(2):
            for z in range(nz):
                sums[z, y, x] = block[x, z]


def fold_body(kept, came, *outs):
    for k, out in enumerate(outs):
        out[...] = (kept[k].astype(F32) + came[k].astype(F32)).astype(BF16)


def sum_z_body(ids, parts, o0, o1, o2, o3, total_ref):
    total = parts[0].astype(F32)
    for z in range(1, parts.shape[0]):
        total = total + parts[z].astype(F32)
    total_ref[...] = total
    for k, out in enumerate((o0, o1, o2, o3)):
        out[...] = total_ref[(ids[Y] + k) % 4].astype(BF16)


def sum_y_body(ids, p0, p1, p2, p3, o0, o1, o2, o3, total_ref):
    shard = o0.shape[0]
    total = (p0[...].astype(F32) + p1[...].astype(F32)) + (p2[...].astype(F32) + p3[...].astype(F32))
    for j in range(4):
        total_ref[j] = total[j // 2, (j % 2) * shard : (j % 2 + 1) * shard]
    for k, out in enumerate((o0, o1, o2, o3)):
        out[...] = total_ref[(ids[XL] * 2 + ids[C]) ^ k]


def grads_body(z0, z1, z2, z3, cot, normed, normalized, stats, out):
    z = (z0[...].astype(F32) + z1[...].astype(F32)) + (z2[...].astype(F32) + z3[...].astype(F32))
    norm = normalized[...]
    st = stats[...]
    mean = jnp.sum(z * norm, axis=-1, keepdims=True) * (1.0 / (HEADS * HD))
    rg = cot[...].astype(F32) + st[:, HEADS : HEADS + 1] * (z - norm * mean)
    for h in range(HEADS):
        n = normed[:, head(h)]
        g = rg[:, head(h)]
        m = jnp.mean(g * n, axis=-1, keepdims=True)
        out[:, head(h)] = (st[:, h : h + 1] * (g - n * m)).astype(BF16)


def query_grad_body(da_own, key, value, mask, cm, cum, cum_t, carried, out, q_ref):
    da = da_own[...]
    pick_t = (iota((HD, 32), 0) == mask[...]).astype(BF16)
    cmv = cm[...]
    cumv = cum[...]
    rising = jnp.exp(cmv)
    falling = jnp.exp(cum_t[HD - 1 : HD, :] - cmv)
    for h in range(HEADS):
        fwd, bwd = states_of(carried, h)
        a = da[:, head(h)]
        s = nt(a, value[:, head(h)])
        p = (s * jnp.exp(-jnp.abs(cmv[:, h : h + 1] - cumv[h : h + 1, :]))).astype(BF16)
        q = nn(p, key[:, head(h)]) + rising[:, h : h + 1] * nt(a, fwd) + falling[:, h : h + 1] * nt(a, bwd)
        q_ref[:, head(h)] = q.astype(BF16)
    out[...] = nn(pick_t, q_ref[...]).astype(BF16)


def rows_of(pieces, h):
    return jnp.concatenate([p[:, head(h)] for p in pieces], axis=0)


def place_of(ids, k):
    return 2 * ((ids[Y] + 4 - k // 2) % 4) + (ids[XL] ^ (k % 2))


def pairs_of(pieces, h):
    return jnp.concatenate([p[:, :, head(h)].reshape(64, HD) for p in pieces], axis=0)


def scores_body(ids, parts, key, cum_t, q0, q1, q2, q3, decay_out, scores_out):
    n = parts.shape[0]
    lane, col = iota((HD, n * 32), 0), iota((HD, n * 32), 1)
    me = 2 * ids[Y] + ids[XL]
    block = jnp.zeros((HD, n * 32), jnp.int32)
    for k in range(n):
        block = jnp.where(col // 32 == k, place_of(ids, k), block)
    at = jnp.zeros((HEADS, n * 32), F32)
    for a in range(n):
        own = (lane < 96) & (lane % 32 == col % 32) & (block == a)
        ends = (lane >= 96) & (lane < 99)
        after = ends & (block > a) & (a >= me)
        before = ends & (block <= a) & (a < me)
        take = jnp.where(own | after, 1.0, jnp.where(before, -1.0, 0.0)).astype(BF16)
        at = at + nn(parts[a, 512:528, :], take)
    ct = cum_t[...]
    for h in range(HEADS):
        decay = jnp.exp(-jnp.abs(ct[:, h : h + 1] - at[h : h + 1, :]))
        decay_out[h] = decay
        scores_out[h] = (nt(key[:, head(h)], pairs_of((q0, q1, q2, q3), h)) * decay).astype(BF16)


def key_value_grads_body(value, decay, scores, q0, q1, q2, q3, *refs):
    das, (key_out, value_out) = refs[:8], refs[8:]
    for h in range(HEADS):
        da = rows_of(das, h)
        value_out[:, head(h)] = nn(scores[h], da).astype(BF16)
        p = (nt(value[:, head(h)], da) * decay[h]).astype(BF16)
        key_out[:, head(h)] = nn(p, pairs_of((q0, q1, q2, q3), h)).astype(BF16)


def trade(x, axis, bit=1):
    n = lax.axis_size(axis)
    return lax.ppermute(x, axis, [(i, i ^ bit) for i in range(n)])


def turn(x, k):
    n = lax.axis_size("y")
    return lax.ppermute(x, "y", [(i, (i + k) % n) for i in range(n)])


def after(first, then):
    return lax.optimization_barrier((first, then))


def along_y(x):
    return [x] + [turn(x, k) for k in range(1, 4)]


def along_sequence(x, other):
    return [p for pair in zip(along_y(x), along_y(other)) for p in pair]


def among(pieces):
    return [pieces[0]] + [
        lax.ppermute(pieces[k], ("xl", "c"), [(i, i ^ k) for i in range(4)]) for k in range(1, 4)
    ]


def across(pieces):
    return [pieces[0]] + [
        lax.ppermute(pieces[k], ("xl", "e"), [(i, i ^ k) for i in range(4)]) for k in range(1, 4)
    ]


def local(residual, query, key, value, ld, cot, mask, routes, gates, up, down):
    residual, query, key, value, ld = residual[0], query[0], key[0], value[0], ld[0]
    cot, mask, routes, gates, up, down = cot[0, 0], mask[0], routes[0, 0], gates[0, 0], up[0], down[0]
    width = HEADS * HD
    ny, nx, nz, nc = (lax.axis_size(a) for a in ("y", "xl", "z", "c"))
    shard = up.shape[0]
    ids = jnp.stack([lax.axis_index(a) for a in ("y", "xl", "z", "c", "e")]).astype(jnp.int32)

    prepared = call(
        prepare_body,
        [((4, shard, 384), BF16)] + [((32, width), BF16)] * 3,
        ids, up, down, cot, mask, routes, gates, query,
        scalar=True,
        scratch=[pltpu.VMEM((4, shard, 384), BF16)],
    )
    prepared, ld = after(prepared, ld)
    bit = nz // 2
    w = jnp.stack((prepared[0], trade(prepared[0], "z", bit)), axis=1)
    w = jnp.stack(among([w[k] for k in range(4)]), axis=1)
    mine, other, qm = prepared[1:]
    qx = trade(qm, "xl")
    grads = across((mine, other, mine, other))
    states, cum, cum_t = call(
        states_body,
        [((8, 528, HD), BF16), ((HEADS, HD), F32), ((HD, HEADS), F32)],
        ld, key, value, mask,
    )
    parts = exchange(states, SEQ)
    rm, inner, cm = call(
        masked_body,
        [((32, width), F32), ((32, width), F32), ((32, HEADS), F32)],
        qm, key, value, residual, mask, cum, cum_t,
    )
    (w, grads, inner), parts = after((w, grads, inner), parts)
    [carries] = call(carry_body, [((8, 512, HD), BF16)], ids, parts, scalar=True, vmem=VM)
    carried = exchange(carries, SEQ)
    bit //= 2
    while bit:
        w = jnp.concatenate((w, trade(w, "z", bit)))
        bit //= 2
    q_two = jnp.stack((qm, qx))
    weights = along_y(w)
    (weights[1], q_two), carried = after((weights[1], q_two), carried)
    grads = grads + [trade(g, "c") for g in grads]
    routed, normed, normalized, stats = call(
        rows_body,
        [((32, width), BF16), ((32, width), F32), ((32, width), F32), ((32, HD), F32)],
        qm, rm, inner, cm, cum_t, carried,
        vmem=VM,
    )
    rows = across([routed] * 4)
    rows = rows + [trade(r, "c") for r in rows]
    z_kept, z_send, dw = call(
        expert_body,
        [((4, 32, width), BF16)] * 2 + [((nz, ny, nx, nc * shard, 384), BF16)],
        ids, *rows, *grads, *weights,
        scalar=True,
        scratch=[pltpu.VMEM((width, 384), BF16)] + [pltpu.VMEM((8, 32, width), BF16)] * 2,
        flops=2 * 10**9,
        vmem=VM,
    )
    folded = call(fold_body, [((32, width), BF16)] * 4, z_kept, trade(z_send, "c"), vmem=VM)
    z_parts = across(folded)
    d1 = exchange(dw, "z")
    q_two, folded = after(q_two, folded)
    queries = along_y(q_two)
    decay, scores = call(
        scores_body,
        [((HEADS, HD, 256), F32), ((HEADS, HD, 256), BF16)],
        ids, parts, key, cum_t, *queries,
        scalar=True,
        vmem=VM,
    )
    [da] = call(grads_body, [((32, width), BF16)], *z_parts, cot, normed, normalized, stats, vmem=VM)
    dx = trade(da, "xl")
    scores, dx = after(scores, dx)
    das = along_sequence(da, dx)
    [query_grad] = call(
        query_grad_body, [((HD, width), BF16)], da, key, value, mask, cm, cum, cum_t, carried,
        scratch=[pltpu.VMEM((32, width), BF16)],
        vmem=VM,
    )
    key_grad, value_grad = call(
        key_value_grads_body,
        [((HD, width), BF16), ((HD, width), BF16)],
        value, decay, scores, *queries, *das,
        vmem=VM,
    )
    (query_grad, key_grad), d1 = after((query_grad, key_grad), d1)
    d2 = call(
        sum_z_body,
        [((nx, nc * shard, 384), BF16)] * 4,
        ids, d1,
        scalar=True,
        scratch=[pltpu.VMEM((ny, nx, nc * shard, 384), F32)],
        vmem=VM,
    )
    d3 = [d2[0]] + [turn(d2[k], k) for k in range(1, 4)]
    d4 = call(
        sum_y_body,
        [((shard, 384), F32)] * 4,
        ids, *d3,
        scalar=True,
        scratch=[pltpu.VMEM((4, shard, 384), F32)],
        vmem=VM,
    )
    d5 = among(d4)
    scale = 1.0 / (ny * nx * nz * nc)

    def finish(*refs):
        weight_grads_body(scale, *refs)

    up_grad, down_grad = call(
        finish,
        [((shard, 768), F32), ((shard, 768), F32)],
        ids, *d5,
        scalar=True,
        scratch=[pltpu.VMEM((4, shard, 384), F32)],
    )
    return query_grad[None], key_grad[None], value_grad[None], up_grad[None], down_grad[None]


def solution(mesh):
    shape = mesh.shape
    grid = mesh.devices.reshape(shape["seq"] // 2, 2, shape["rep"] // 2, 2, shape["exp"])
    fine = Mesh(grid, ("y", "xl", "z", "c", "e"))
    sequences, data = ("z", "c", "e"), ("y", "xl", "z", "c")
    in_specs = (
        P(sequences, SEQ, None),
        P(sequences, SEQ, None),
        P(sequences, SEQ, None),
        P(sequences, SEQ, None),
        P(sequences, None, SEQ),
        P(sequences, SEQ, None, None),
        P(sequences, SEQ, None),
        P(sequences, SEQ, None, None),
        P(sequences, SEQ, None, None),
        P("e", data, None),
        P("e", data, None),
    )
    out_specs = (
        P(sequences, SEQ, None),
        P(sequences, SEQ, None),
        P(sequences, SEQ, None),
        P("e", data, None),
        P("e", data, None),
    )
    return jax.shard_map(local, mesh=fine, in_specs=in_specs, out_specs=out_specs, check_vma=False)
```

```python
import jax
import jax.numpy as jnp
from jax import lax
from jax.experimental import pallas as pl
from jax.experimental.pallas import tpu as pltpu
from jax.sharding import Mesh, PartitionSpec as P

HEADS = 16
HD = 128
EPS = 1e-05
SEQ = ("y", "xl")
VM = 24
Y, XL, Z, C, E = range(5)
F32 = jnp.float32
BF16 = jnp.bfloat16
HIGH = lax.Precision.HIGHEST


def call(body, outs, *args, flops=10**8, scalar=False, scratch=(), vmem=56):
    shapes = [jax.ShapeDtypeStruct(s, d) for s, d in outs]
    moved = sum(a.size * a.dtype.itemsize for a in (*args, *shapes))
    in_specs = [pl.BlockSpec()] * len(args)
    if scalar:
        in_specs[0] = pl.BlockSpec(memory_space=pltpu.SMEM)
    result = pl.pallas_call(
        body,
        out_shape=shapes,
        in_specs=in_specs,
        scratch_shapes=list(scratch),
        compiler_params=pltpu.CompilerParams(vmem_limit_bytes=vmem << 20),
        cost_estimate=pl.CostEstimate(flops=flops, bytes_accessed=moved, transcendentals=0),
    )(*args)
    return result


def iota(shape, dim):
    return lax.broadcasted_iota(jnp.int32, shape, dim)


def tn(a, b, **kw):
    return lax.dot_general(a, b, (((0,), (0,)), ((), ())), preferred_element_type=F32, **kw)


def nt(a, b, **kw):
    return lax.dot_general(a, b, (((1,), (1,)), ((), ())), preferred_element_type=F32, **kw)


def nn(a, b, **kw):
    return lax.dot_general(a, b, (((1,), (0,)), ((), ())), preferred_element_type=F32, **kw)


def head(h):
    return slice(h * HD, (h + 1) * HD)


def exchange(x, axes):
    return lax.all_to_all(x, axes, split_axis=0, concat_axis=0, tiled=True)


def prepare_body(
    ids, up, down, cot, mask, routes, gates, query, w_out, own_out, other_out, qm_out, slices
):
    pick_t = (iota((HD, 32), 0) == mask[...]).astype(BF16)
    qm_out[...] = tn(pick_t, query[...]).astype(BF16)
    low = iota((up.shape[0], HD), 1) < 64
    for c in range(12):
        u = up[:, head(c // 2)].astype(F32)
        d = down[:, head(c // 2)].astype(F32)
        if c % 2:
            u = pltpu.roll(u, 64, 1)
        else:
            d = pltpu.roll(d, 64, 1)
        slices[c // 3, :, head(c % 3)] = jnp.where(low, u, d).astype(BF16)
    for k in range(4):
        w_out[k] = slices[(ids[XL] * 2 + ids[C]) ^ k]
    lane = iota((HD, HD), 1)
    sub = iota((HD, HD), 0)
    table = jnp.zeros((HD, HD), F32)
    for e in range(2):
        hit = jnp.where(sub == routes[e : e + 1, :], gates[e : e + 1, :], 0.0)
        table = jnp.where(lane == e, jnp.sum(hit, axis=1, keepdims=True), table)
    gm = tn(pick_t.astype(F32), table, precision=HIGH)
    cotf = cot[...].astype(F32)
    first, second = (gm[:, 0:1] * cotf).astype(BF16), (gm[:, 1:2] * cotf).astype(BF16)
    swap = ids[E] == 1
    own_out[...] = jnp.where(swap, second, first)
    other_out[...] = jnp.where(swap, first, second)


def weight_grads_body(scale, ids, p0, p1, p2, p3, up, down, g):
    for k, piece in enumerate((p0, p1, p2, p3)):
        g[(ids[XL] * 2 + ids[C]) ^ k] = piece[...]
    low = iota((up.shape[0], HD), 1) < 64
    for b in range(6):
        first, second = 2 * b, 2 * b + 1
        x = g[first // 3, :, head(first % 3)] * scale
        y = g[second // 3, :, head(second % 3)] * scale
        up[:, head(b)] = jnp.where(low, x, pltpu.roll(y, 64, 1))
        down[:, head(b)] = jnp.where(low, pltpu.roll(x, 64, 1), y)


def states_body(ld, key, value, mask, out, cum_out, cum_t_out):
    rows, cols = iota((HD, HD), 0), iota((HD, HD), 1)
    ldv = ld[...]
    cum = nn(ldv, (rows <= cols).astype(F32), precision=HIGH)
    cum_t = nt((cols <= rows).astype(F32), ldv, precision=HIGH)
    cum_out[...] = cum
    cum_t_out[...] = cum_t
    falling = jnp.exp(cum_t[HD - 1 : HD, :] - cum_t)
    rising = jnp.exp(cum_t)
    for h in range(HEADS):
        k = key[:, head(h)].astype(F32)
        kf = (k * falling[:, h : h + 1]).astype(BF16)
        kb = (k * rising[:, h : h + 1]).astype(BF16)
        v = value[:, head(h)]
        g, at = h // 2, (h % 2) * HD
        out[g, at : at + HD, :] = tn(kf, v).astype(BF16)
        out[g, 256 + at : 256 + at + HD, :] = tn(kb, v).astype(BF16)
    repeat = (iota((32, HD), 0) == iota((32, HD), 1) % 32).astype(BF16)
    places = nn(mask[...].astype(F32).astype(BF16), repeat).astype(jnp.int32)
    places = jnp.where(iota((1, HD), 1) < 96, places, HD - 1)
    chosen = nn(cum, (rows == places).astype(F32), precision=HIGH)
    hi = chosen.astype(BF16).astype(F32)
    mid = (chosen - hi).astype(BF16).astype(F32)
    low = (chosen - hi - mid).astype(BF16).astype(F32)
    lane = iota((HEADS, HD), 1)
    first = (lane < 32) | (lane == 96)
    second = ((lane >= 32) & (lane < 64)) | (lane == 97)
    third = ((lane >= 64) & (lane < 96)) | (lane == 98)
    packed = jnp.where(first, hi, jnp.where(second, mid, jnp.where(third, low, 0.0))).astype(BF16)
    for g in range(8):
        out[g, 512:528, :] = packed


def masked_body(queries, key, value, residual, mask, cum, cum_t, rm_out, inner_out, cm_out):
    pick_t = (iota((HD, 32), 0) == mask[...]).astype(BF16)
    qm = queries[...]
    rm_out[...] = tn(pick_t, residual[...])
    cm = tn(pick_t.astype(F32), cum_t[...], precision=HIGH)
    cm_out[...] = cm
    cumv = cum[...]
    for h in range(HEADS):
        s = nt(qm[:, head(h)], key[:, head(h)])
        p = (s * jnp.exp(-jnp.abs(cm[:, h : h + 1] - cumv[h : h + 1, :]))).astype(BF16)
        inner_out[:, head(h)] = nn(p, value[:, head(h)])


def carry_body(ids, parts, out):
    row, lane = iota((HEADS, HD), 0), iota((HEADS, HD), 1)
    ends = (lane >= 96) & (lane < 99)
    n = parts.shape[0]
    for j in range(2):
        at = slice(j * HD, (j + 1) * HD)
        back = slice(256 + j * HD, 256 + (j + 1) * HD)
        wanted = ends & (row == 2 * (2 * ids[Y] + ids[XL]) + j)
        decay = [
            jnp.exp(jnp.sum(jnp.where(wanted, parts[a, 512:528, :].astype(F32), 0.0), keepdims=True))
            for a in range(n)
        ]
        run = jnp.zeros((HD, HD), F32)
        for a in range(n):
            out[a, at, :] = run.astype(BF16)
            run = decay[a] * run + parts[a, at, :].astype(F32)
        run = jnp.zeros((HD, HD), F32)
        for a in reversed(range(n)):
            out[a, back, :] = run.astype(BF16)
            run = decay[a] * run + parts[a, back, :].astype(F32)


def states_of(carried, h):
    at = (h % 2) * HD
    return carried[h // 2, at : at + HD, :], carried[h // 2, 256 + at : 256 + at + HD, :]


def rows_body(qm, rm, inner, cm, cum_t, carried, routed_out, normed_out, normalized_out, stats_out):
    cmv = cm[...]
    rising = jnp.exp(cmv)
    falling = jnp.exp(cum_t[HD - 1 : HD, :] - cmv)
    lane = iota((32, HD), 1)
    stats = jnp.zeros((32, HD), F32)
    total = jnp.zeros((32, HD), F32)
    residuals = []
    for h in range(HEADS):
        fwd, bwd = states_of(carried, h)
        q = qm[:, head(h)]
        attn = inner[:, head(h)] + rising[:, h : h + 1] * nn(q, fwd) + falling[:, h : h + 1] * nn(q, bwd)
        scale = lax.rsqrt(jnp.mean(attn * attn, axis=-1, keepdims=True) + EPS)
        normed = attn * scale
        normed_out[:, head(h)] = normed
        stats = jnp.where(lane == h, scale, stats)
        r = (rm[:, head(h)] + normed).astype(BF16).astype(F32)
        total = total + r * r
        residuals.append(r)
    row_scale = lax.rsqrt(jnp.sum(total, axis=-1, keepdims=True) * (1.0 / (HEADS * HD)) + EPS)
    stats_out[...] = jnp.where(lane == HEADS, row_scale, stats)
    for h in range(HEADS):
        normalized = residuals[h] * row_scale
        normalized_out[:, head(h)] = normalized
        routed_out[:, head(h)] = normalized.astype(BF16)


def expert_body(ids, *refs):
    rows, grads, pieces, (z_own, z_other, sums), (w_ref, r_ref, g_ref) = (
        refs[:8], refs[8:10], refs[10:14], refs[14:17], refs[17:],
    )
    nz, unit = pieces[0].shape[0], pieces[0].shape[2]
    for k, piece in enumerate(pieces):
        y = (ids[Y] + 4 - k) % 4
        for zs in range(nz):
            z = ids[Z] ^ sum(nz >> (i + 1) for i in range(3) if zs >> i & 1)
            for cs in range(4):
                x = ids[XL] ^ (cs // 2)
                at = (((y * 2 + x) * nz + z) * 2 + (ids[C] ^ (cs % 2))) * unit
                w_ref[pl.ds(pl.multiple_of(at, unit), unit), :] = piece[zs, cs]
    for k in range(8):
        r_ref[k] = rows[k][...]
        g_ref[k] = grads[k // 4][k % 4]
    width = HEADS * HD
    r = r_ref[...].reshape(256, width)
    g = g_ref[...].reshape(256, width)
    w = w_ref[...]
    pre_all = nn(r, w)
    grad_all = nn(g, w)
    low = iota((256, HD), 1) < 64
    pgs, acts = [], []
    for b in range(3):
        pre = pre_all[:, head(b)]
        act_grad = pltpu.roll(grad_all[:, head(b)], 64, 1)
        sig = jax.nn.sigmoid(pre)
        act = pltpu.roll(pre * sig, 64, 1)
        pre_grad = act_grad * sig * (1.0 + pre * (1.0 - sig))
        pgs.append(jnp.where(low, pre_grad, 0.0).astype(BF16))
        acts.append(jnp.where(low, 0.0, act).astype(BF16))
    pg = jnp.concatenate(pgs, axis=1)
    ac = jnp.concatenate(acts, axis=1)
    z_own[...] = nt(pg[:128], w).astype(BF16).reshape(z_own.shape)
    z_other[...] = nt(pg[128:], w).astype(BF16).reshape(z_other.shape)
    both = jnp.concatenate((pg, ac), axis=0)
    for y in range(4):
        cols = slice(y * 512, (y + 1) * 512)
        sides = jnp.concatenate((r[:, cols], g[:, cols]), axis=0)
        block = tn(sides, both).astype(BF16).reshape(2, nz, 2 * unit, 384)
        for x in range(2):
            for z in range(nz):
                sums[z, y, x] = block[x, z]


def fold_body(kept, came, *outs):
    for k, out in enumerate(outs):
        out[...] = (kept[k].astype(F32) + came[k].astype(F32)).astype(BF16)


def sum_z_body(ids, parts, o0, o1, o2, o3, total_ref):
    total = parts[0].astype(F32)
    for z in range(1, parts.shape[0]):
        total = total + parts[z].astype(F32)
    total_ref[...] = total
    for k, out in enumerate((o0, o1, o2, o3)):
        out[...] = total_ref[(ids[Y] + k) % 4].astype(BF16)


def sum_y_body(ids, p0, p1, p2, p3, o0, o1, o2, o3, total_ref):
    shard = o0.shape[0]
    total = (p0[...].astype(F32) + p1[...].astype(F32)) + (p2[...].astype(F32) + p3[...].astype(F32))
    for j in range(4):
        total_ref[j] = total[j // 2, (j % 2) * shard : (j % 2 + 1) * shard]
    for k, out in enumerate((o0, o1, o2, o3)):
        out[...] = total_ref[(ids[XL] * 2 + ids[C]) ^ k]


def grads_body(z0, z1, z2, z3, cot, normed, normalized, stats, out):
    z = (z0[...].astype(F32) + z1[...].astype(F32)) + (z2[...].astype(F32) + z3[...].astype(F32))
    norm = normalized[...]
    st = stats[...]
    mean = jnp.sum(z * norm, axis=-1, keepdims=True) * (1.0 / (HEADS * HD))
    rg = cot[...].astype(F32) + st[:, HEADS : HEADS + 1] * (z - norm * mean)
    for h in range(HEADS):
        n = normed[:, head(h)]
        g = rg[:, head(h)]
        m = jnp.mean(g * n, axis=-1, keepdims=True)
        out[:, head(h)] = (st[:, h : h + 1] * (g - n * m)).astype(BF16)


def query_grad_body(da_own, key, value, mask, cm, cum, cum_t, carried, out, q_ref):
    da = da_own[...]
    pick_t = (iota((HD, 32), 0) == mask[...]).astype(BF16)
    cmv = cm[...]
    cumv = cum[...]
    rising = jnp.exp(cmv)
    falling = jnp.exp(cum_t[HD - 1 : HD, :] - cmv)
    for h in range(HEADS):
        fwd, bwd = states_of(carried, h)
        a = da[:, head(h)]
        s = nt(a, value[:, head(h)])
        p = (s * jnp.exp(-jnp.abs(cmv[:, h : h + 1] - cumv[h : h + 1, :]))).astype(BF16)
        q = nn(p, key[:, head(h)]) + rising[:, h : h + 1] * nt(a, fwd) + falling[:, h : h + 1] * nt(a, bwd)
        q_ref[:, head(h)] = q.astype(BF16)
    out[...] = nn(pick_t, q_ref[...]).astype(BF16)


def rows_of(pieces, h):
    return jnp.concatenate([p[:, head(h)] for p in pieces], axis=0)


def place_of(ids, k):
    return 2 * ((ids[Y] + 4 - k // 2) % 4) + (ids[XL] ^ (k % 2))


def pairs_of(pieces, h):
    return jnp.concatenate([p[:, :, head(h)].reshape(64, HD) for p in pieces], axis=0)


def scores_body(ids, parts, key, cum_t, q0, q1, q2, q3, decay_out, scores_out):
    n = parts.shape[0]
    lane, col = iota((HD, n * 32), 0), iota((HD, n * 32), 1)
    me = 2 * ids[Y] + ids[XL]
    block = jnp.zeros((HD, n * 32), jnp.int32)
    for k in range(n):
        block = jnp.where(col // 32 == k, place_of(ids, k), block)
    at = jnp.zeros((HEADS, n * 32), F32)
    for a in range(n):
        own = (lane < 96) & (lane % 32 == col % 32) & (block == a)
        ends = (lane >= 96) & (lane < 99)
        after = ends & (block > a) & (a >= me)
        before = ends & (block <= a) & (a < me)
        take = jnp.where(own | after, 1.0, jnp.where(before, -1.0, 0.0)).astype(BF16)
        at = at + nn(parts[a, 512:528, :], take)
    ct = cum_t[...]
    for h in range(HEADS):
        decay = jnp.exp(-jnp.abs(ct[:, h : h + 1] - at[h : h + 1, :]))
        decay_out[h] = decay
        scores_out[h] = (nt(key[:, head(h)], pairs_of((q0, q1, q2, q3), h)) * decay).astype(BF16)


def key_value_grads_body(value, decay, scores, q0, q1, q2, q3, *refs):
    das, (key_out, value_out) = refs[:8], refs[8:]
    for h in range(HEADS):
        da = rows_of(das, h)
        value_out[:, head(h)] = nn(scores[h], da).astype(BF16)
        p = (nt(value[:, head(h)], da) * decay[h]).astype(BF16)
        key_out[:, head(h)] = nn(p, pairs_of((q0, q1, q2, q3), h)).astype(BF16)


def trade(x, axis, bit=1):
    n = lax.axis_size(axis)
    return lax.ppermute(x, axis, [(i, i ^ bit) for i in range(n)])


def turn(x, k):
    n = lax.axis_size("y")
    return lax.ppermute(x, "y", [(i, (i + k) % n) for i in range(n)])


def after(first, then):
    return lax.optimization_barrier((first, then))


def along_y(x):
    return [x] + [turn(x, k) for k in range(1, 4)]


def along_sequence(x, other):
    return [p for pair in zip(along_y(x), along_y(other)) for p in pair]


def among(pieces):
    return [pieces[0]] + [
        lax.ppermute(pieces[k], ("xl", "c"), [(i, i ^ k) for i in range(4)]) for k in range(1, 4)
    ]


def across(pieces):
    return [pieces[0]] + [
        lax.ppermute(pieces[k], ("xl", "e"), [(i, i ^ k) for i in range(4)]) for k in range(1, 4)
    ]


def local(residual, query, key, value, ld, cot, mask, routes, gates, up, down):
    residual, query, key, value, ld = residual[0], query[0], key[0], value[0], ld[0]
    cot, mask, routes, gates, up, down = cot[0, 0], mask[0], routes[0, 0], gates[0, 0], up[0], down[0]
    width = HEADS * HD
    ny, nx, nz, nc = (lax.axis_size(a) for a in ("y", "xl", "z", "c"))
    shard = up.shape[0]
    ids = jnp.stack([lax.axis_index(a) for a in ("y", "xl", "z", "c", "e")]).astype(jnp.int32)

    prepared = call(
        prepare_body,
        [((4, shard, 384), BF16)] + [((32, width), BF16)] * 3,
        ids, up, down, cot, mask, routes, gates, query,
        scalar=True,
        scratch=[pltpu.VMEM((4, shard, 384), BF16)],
    )
    prepared, ld = after(prepared, ld)
    bit = nz // 2
    w = jnp.stack((prepared[0], trade(prepared[0], "z", bit)), axis=1)
    w = jnp.stack(among([w[k] for k in range(4)]), axis=1)
    mine, other, qm = prepared[1:]
    qx = trade(qm, "xl")
    grads = across((mine, other, mine, other))
    states, cum, cum_t = call(
        states_body,
        [((8, 528, HD), BF16), ((HEADS, HD), F32), ((HD, HEADS), F32)],
        ld, key, value, mask,
    )
    parts = exchange(states, SEQ)
    rm, inner, cm = call(
        masked_body,
        [((32, width), F32), ((32, width), F32), ((32, HEADS), F32)],
        qm, key, value, residual, mask, cum, cum_t,
    )
    (w, grads, inner), parts = after((w, grads, inner), parts)
    [carries] = call(carry_body, [((8, 512, HD), BF16)], ids, parts, scalar=True, vmem=VM)
    carried = exchange(carries, SEQ)
    bit //= 2
    while bit:
        w = jnp.concatenate((w, trade(w, "z", bit)))
        bit //= 2
    q_two = jnp.stack((qm, qx))
    weights = along_y(w)
    (w, q_two), carried = after((w, q_two), carried)
    weights[0] = w
    grads = jnp.stack(grads)
    grads = (grads, trade(grads, "c"))
    routed, normed, normalized, stats = call(
        rows_body,
        [((32, width), BF16), ((32, width), F32), ((32, width), F32), ((32, HD), F32)],
        qm, rm, inner, cm, cum_t, carried,
        vmem=VM,
    )
    weights[1], routed = after(weights[1], routed)
    rows = across([routed] * 4)
    rows = rows + [trade(r, "c") for r in rows]
    z_kept, z_send, dw = call(
        expert_body,
        [((4, 32, width), BF16)] * 2 + [((nz, ny, nx, nc * shard, 384), BF16)],
        ids, *rows, *grads, *weights,
        scalar=True,
        scratch=[pltpu.VMEM((width, 384), BF16)] + [pltpu.VMEM((8, 32, width), BF16)] * 2,
        flops=2 * 10**9,
        vmem=VM,
    )
    folded = call(fold_body, [((32, width), BF16)] * 4, z_kept, trade(z_send, "c"), vmem=VM)
    z_parts = across(folded)
    d1 = exchange(dw, "z")
    q_two, folded = after(q_two, folded)
    queries = along_y(q_two)
    decay, scores = call(
        scores_body,
        [((HEADS, HD, 256), F32), ((HEADS, HD, 256), BF16)],
        ids, parts, key, cum_t, *queries,
        scalar=True,
        vmem=VM,
    )
    [da] = call(grads_body, [((32, width), BF16)], *z_parts, cot, normed, normalized, stats, vmem=VM)
    dx = trade(da, "xl")
    scores, dx = after(scores, dx)
    das = along_sequence(da, dx)
    [query_grad] = call(
        query_grad_body, [((HD, width), BF16)], da, key, value, mask, cm, cum, cum_t, carried,
        scratch=[pltpu.VMEM((32, width), BF16)],
        vmem=VM,
    )
    key_grad, value_grad = call(
        key_value_grads_body,
        [((HD, width), BF16), ((HD, width), BF16)],
        value, decay, scores, *queries, *das,
        vmem=VM,
    )
    (query_grad, key_grad), d1 = after((query_grad, key_grad), d1)
    d2 = call(
        sum_z_body,
        [((nx, nc * shard, 384), BF16)] * 4,
        ids, d1,
        scalar=True,
        scratch=[pltpu.VMEM((ny, nx, nc * shard, 384), F32)],
        vmem=VM,
    )
    d3 = [d2[0]] + [turn(d2[k], k) for k in range(1, 4)]
    d4 = call(
        sum_y_body,
        [((shard, 384), F32)] * 4,
        ids, *d3,
        scalar=True,
        scratch=[pltpu.VMEM((4, shard, 384), F32)],
        vmem=VM,
    )
    d5 = among(d4)
    scale = 1.0 / (ny * nx * nz * nc)

    def finish(*refs):
        weight_grads_body(scale, *refs)

    up_grad, down_grad = call(
        finish,
        [((shard, 768), F32), ((shard, 768), F32)],
        ids, *d5,
        scalar=True,
        scratch=[pltpu.VMEM((4, shard, 384), F32)],
    )
    return query_grad[None], key_grad[None], value_grad[None], up_grad[None], down_grad[None]


def solution(mesh):
    shape = mesh.shape
    grid = mesh.devices.reshape(shape["seq"] // 2, 2, shape["rep"] // 2, 2, shape["exp"])
    fine = Mesh(grid, ("y", "xl", "z", "c", "e"))
    sequences, data = ("z", "c", "e"), ("y", "xl", "z", "c")
    in_specs = (
        P(sequences, SEQ, None),
        P(sequences, SEQ, None),
        P(sequences, SEQ, None),
        P(sequences, SEQ, None),
        P(sequences, None, SEQ),
        P(sequences, SEQ, None, None),
        P(sequences, SEQ, None),
        P(sequences, SEQ, None, None),
        P(sequences, SEQ, None, None),
        P("e", data, None),
        P("e", data, None),
    )
    out_specs = (
        P(sequences, SEQ, None),
        P(sequences, SEQ, None),
        P(sequences, SEQ, None),
        P("e", data, None),
        P("e", data, None),
    )
    return jax.shard_map(local, mesh=fine, in_specs=in_specs, out_specs=out_specs, check_vma=False)
```
